32 devices in a mesh: dp: 8 (over y, x, core), blk: 4 (over z).
Axes of the slice: x: 2, y: 2, z: 4, core: 2. Of those that a mesh axis runs over, the one named last changes fastest.
Arguments:
- tokens: bfloat16 [16, 2048, 768], P('dp', 'blk'), may hold values from -6 to 6
- cotangent: bfloat16 [16, 2048, 768], P('dp', 'blk'), may hold values from -6 to 6
- lengths: int32 [16], P('dp'), may hold values from 512 to 2048, as said below
- query_weight: bfloat16 [768, 768], P(('dp', 'blk')), may hold values from -0.21875 to 0.21875
- key_weight: bfloat16 [768, 768], P(('dp', 'blk')), may hold values from -0.21875 to 0.21875
- value_weight: bfloat16 [768, 768], P(('dp', 'blk')), may hold values from -0.21875 to 0.21875
- output_weight: bfloat16 [768, 768], P(('dp', 'blk')), may hold values from -1.75 to 1.75
- up_weight: bfloat16 [768, 3072], P(('dp', 'blk')), may hold values from -0.21875 to 0.21875
- down_weight: bfloat16 [3072, 768], P(('dp', 'blk')), may hold values from -0.109375 to 0.109375
- query_bias: bfloat16 [768], P(('dp', 'blk')), may hold values from -2 to 2
- value_bias: bfloat16 [768], P(('dp', 'blk')), may hold values from -2 to 2
- output_bias: bfloat16 [768], P(('dp', 'blk')), may hold values from -2 to 2
- up_bias: bfloat16 [3072], P(('dp', 'blk')), may hold values from -2 to 2
- down_bias: bfloat16 [768], P(('dp', 'blk')), may hold values from -2 to 2
- attn_gain: bfloat16 [768], P(('dp', 'blk')), may hold values from 0.5 to 1.5
- attn_shift: bfloat16 [768], P(('dp', 'blk')), may hold values from -2 to 2
- ffn_gain: bfloat16 [768], P(('dp', 'blk')), may hold values from 0.5 to 1.5
- ffn_shift: bfloat16 [768], P(('dp', 'blk')), may hold values from -2 to 2
Outputs:
- layer_out: bfloat16 [16, 2048, 768], P('dp', 'blk')
- tokens_grad: float32 [16, 2048, 768], P('dp', 'blk')
- grad_query_weight: float32 [768, 768], P(('dp', 'blk'))
- grad_key_weight: float32 [768, 768], P(('dp', 'blk'))
- grad_value_weight: float32 [768, 768], P(('dp', 'blk'))
- grad_output_weight: float32 [768, 768], P(('dp', 'blk'))
- grad_up_weight: float32 [768, 3072], P(('dp', 'blk'))
- grad_down_weight: float32 [3072, 768], P(('dp', 'blk'))
- grad_query_bias: float32 [768], P(('dp', 'blk'))
- grad_value_bias: float32 [768], P(('dp', 'blk'))
- grad_output_bias: float32 [768], P(('dp', 'blk'))
- grad_up_bias: float32 [3072], P(('dp', 'blk'))
- grad_down_bias: float32 [768], P(('dp', 'blk'))
- grad_attn_gain: float32 [768], P(('dp', 'blk'))
- grad_attn_shift: float32 [768], P(('dp', 'blk'))
- grad_ffn_gain: float32 [768], P(('dp', 'blk'))
- grad_ffn_shift: float32 [768], P(('dp', 'blk'))
The draws below stay inside these ranges and needn't reach their ends.
Inputs may be any that keep to these rules, and one draw needn't show every extreme that they name: `lengths`: each sequence is valid up to its length; the first sequence of every data group of 2 has length exactly 2048; the others fall in buckets of at most 2048, 1536 or 1024 positions and hold at least half of their bucket.
All inputs are finite; a program needn't handle non-finite values.
Results may differ from the reference program's by a relative error of at most 0.018.
Values may be sent and summed in bfloat16 or wider, within the bound.
No kernel may reach another device: no remote copies, remote signals or barrier semaphores. Data moves between devices by JAX's collectives and lax.ppermute only.
A program may use at most 384 MiB of HBM per device.

```python
import jax
import jax.numpy as jnp
from jax import lax

D = 768
HEADS = 12
HEAD = 64
FF = 3072
SEQ = 2048
SEQS = 2
NSEQ = 16


def draw_lengths(key, part):
    bucket_key, offset_key = jax.random.split(jax.random.fold_in(key, 11))
    bucket = jax.random.randint(bucket_key, (NSEQ,), 0, 3)
    ceiling = SEQ * (4 - bucket) // 4
    least_len = ceiling // 2
    offset = jax.random.randint(offset_key, (NSEQ,), 0, 1 << 20)
    drawn = least_len + offset % (ceiling - least_len + 1)
    leading = jnp.arange(NSEQ, dtype=jnp.int32) % SEQS == 0
    return jnp.where(leading, SEQ, drawn).astype(jnp.int32)


def level_of(rng, shape, cuts, low, high):
    level, own = 1.0, jax.random.fold_in(rng, 6)
    for axis_at, blocks in cuts:
        draws = jnp.exp(jax.random.uniform(jax.random.fold_in(own, axis_at), (blocks,), jnp.float32, low / len(cuts), high / len(cuts)))
        level = level * jnp.repeat(draws, shape[axis_at] // blocks).reshape([-1 if axis == axis_at else 1 for axis in range(len(shape))])
    return level


def noise(rng, shape, scale, bound, cuts=(), held_as=jnp.bfloat16):
    result = scale * jax.random.normal(rng, shape, jnp.float32)
    if cuts:
        result = result * level_of(rng, shape, cuts, -0.22, 0.18)
    return jnp.clip(result, -bound, bound).astype(held_as)


def setup_inputs(seed: int = 0) -> dict:
    splits = jax.random.split(jax.random.key(seed), 19)
    tokens = noise(splits[0], (NSEQ, SEQ, D), 1.0, 6.0, ((0, 8), (1, 4)))
    cotangent = noise(splits[1], (NSEQ, SEQ, D), 1.0, 6.0, ((0, 8), (1, 4)))
    lengths = draw_lengths(jax.random.fold_in(splits[18], 71), 0)
    query_weight = noise(splits[3], (D, D), D ** -0.5, 0.21875, ((0, 32),))
    key_weight = noise(splits[4], (D, D), D ** -0.5, 0.21875, ((0, 32),))
    value_weight = noise(splits[5], (D, D), D ** -0.5, 0.21875, ((0, 32),))
    output_weight = noise(splits[6], (D, D), (D // 64) ** -0.5, 1.75, ((0, 32),))
    up_weight = noise(splits[7], (D, FF), D ** -0.5, 0.21875, ((0, 32),))
    down_weight = noise(splits[8], (FF, D), FF ** -0.5, 0.109375, ((0, 32),))
    query_bias = noise(splits[9], (D,), 0.3, 2.0, ((0, 32),))
    value_bias = noise(splits[10], (D,), 0.3, 2.0, ((0, 32),))
    output_bias = noise(splits[11], (D,), 0.3, 2.0, ((0, 32),))
    up_bias = noise(splits[12], (FF,), 0.3, 2.0, ((0, 32),))
    down_bias = noise(splits[13], (D,), 0.3, 2.0, ((0, 32),))
    attn_gain = jnp.clip(1.0 + 0.1 * jax.random.normal(splits[14], (D,), jnp.float32), 0.5, 1.5).astype(jnp.bfloat16)
    attn_shift = noise(splits[15], (D,), 0.3, 2.0, ((0, 32),))
    ffn_gain = jnp.clip(1.0 + 0.1 * jax.random.normal(splits[16], (D,), jnp.float32), 0.5, 1.5).astype(jnp.bfloat16)
    ffn_shift = noise(splits[17], (D,), 0.3, 2.0, ((0, 32),))
    return dict(tokens=tokens, cotangent=cotangent, lengths=lengths, query_weight=query_weight, key_weight=key_weight, value_weight=value_weight, output_weight=output_weight, up_weight=up_weight, down_weight=down_weight, query_bias=query_bias, value_bias=value_bias, output_bias=output_bias, up_bias=up_bias, down_bias=down_bias, attn_gain=attn_gain, attn_shift=attn_shift, ffn_gain=ffn_gain, ffn_shift=ffn_shift)


@jax.custom_vjp
def low(v):
    return lax.optimization_barrier(v.astype(jnp.bfloat16)).astype(jnp.float32)

@jax.custom_vjp
def low_back(v):
    return v

def low_keep(v):
    return (low(v), None)

def low_pass(kept, grad):
    return (grad,)

def back_keep(v):
    return (v, None)

def back_low(kept, grad):
    return (low(grad),)
low.defvjp(low_keep, low_pass)
low_back.defvjp(back_keep, back_low)
highest = lax.Precision.HIGHEST

def product(left, right):
    return jnp.dot(left, right, precision=highest)

def layer_norm(values, gain, shift):
    center = lax.optimization_barrier(jnp.mean(values, axis=-1, keepdims=True))
    offset = values - center
    spread = lax.optimization_barrier(jnp.mean(offset * offset, axis=-1, keepdims=True))
    return offset * lax.rsqrt(spread + 1e-12) * gain + shift

def one_sequence(inputs, length, params):
    query_weight, key_weight, value_weight, output_weight, up_weight, down_weight, query_bias, value_bias, output_bias, up_bias, down_bias, attn_gain, attn_shift, ffn_gain, ffn_shift = params
    queries = low_back(low(product(inputs, query_weight) + query_bias))
    keys_all = low_back(low(product(inputs, key_weight)))
    values_all = low_back(low(product(inputs, value_weight) + value_bias))
    layout = (SEQ, HEADS, HEAD)
    scores = jnp.einsum('qhd,khd->hqk', queries.reshape(layout), keys_all.reshape(layout), precision=highest) * 0.125
    scores = low_back(scores)
    valid = jnp.arange(SEQ, dtype=jnp.int32) < length
    masked = jnp.where(valid[None, None, :], scores, -1e+30)
    largest = lax.optimization_barrier(jnp.max(masked, axis=-1, keepdims=True))
    expo = jnp.exp(masked - largest)
    probs = expo / lax.optimization_barrier(jnp.sum(expo, axis=-1, keepdims=True))
    context = jnp.einsum('hqk,khd->qhd', low(probs), values_all.reshape(layout), precision=highest).reshape(SEQ, D)
    context = low_back(low(context))
    attended = low_back(product(context, output_weight) + output_bias)
    hidden = layer_norm(inputs + attended, attn_gain, attn_shift)
    upward = low_back(product(low(hidden), up_weight) + up_bias)
    active = low(jax.nn.gelu(upward, approximate=True))
    downward = low_back(product(active, down_weight) + down_bias)
    return layer_norm(hidden + downward, ffn_gain, ffn_shift)

def reference(tokens, cotangent, lengths, query_weight, key_weight, value_weight, output_weight, up_weight, down_weight, query_bias, value_bias, output_bias, up_bias, down_bias, attn_gain, attn_shift, ffn_gain, ffn_shift):
    params = tuple((item.astype(jnp.float32) for item in (query_weight, key_weight, value_weight, output_weight, up_weight, down_weight, query_bias, value_bias, output_bias, up_bias, down_bias, attn_gain, attn_shift, ffn_gain, ffn_shift)))

    def forward(inputs, weights):

        def per_sequence(pair):
            return one_sequence(pair[0], pair[1], weights)
        return lax.map(jax.checkpoint(per_sequence), (inputs, lengths))
    outputs, pull = jax.vjp(forward, tokens.astype(jnp.float32), params)
    input_grad, weight_grads = pull(cotangent.astype(jnp.float32))
    return (outputs.astype(jnp.bfloat16), input_grad, weight_grads[0], weight_grads[1], weight_grads[2], weight_grads[3], weight_grads[4], weight_grads[5], weight_grads[6], weight_grads[7], weight_grads[8], weight_grads[9], weight_grads[10], weight_grads[11], weight_grads[12], weight_grads[13], weight_grads[14])
```

```python
import functools

import jax
import jax.numpy as jnp
from jax import lax
from jax.experimental import pallas as pl
from jax.experimental.pallas import tpu as pltpu
from jax.sharding import Mesh
from jax.sharding import PartitionSpec as P

HEADS = 12
LANES = 128
PER_TILE = 2
SCORE_SCALE = 0.125 * 1.4426950408889634
MASKED = -1e30
ALL = ("pair", "core", "blk")
VMEM_LIMIT = 56 << 20


def shifted(array, axis, by):
    length = lax.axis_size(axis)
    return lax.ppermute(array, axis, [(i, (i + by) % length) for i in range(length)])


def matmul(left, right):
    return jnp.dot(left, right, preferred_element_type=jnp.float32)


def times_trans(left, right):
    return lax.dot_general(
        left, right, (((1,), (1,)), ((), ())), preferred_element_type=jnp.float32
    )


def trans_times(left, right):
    return lax.dot_general(
        left, right, (((0,), (0,)), ((), ())), preferred_element_type=jnp.float32
    )


def layer_norm(values, gain, shift):
    center = jnp.mean(values, axis=-1, keepdims=True)
    offset = values - center
    spread = jnp.mean(offset * offset, axis=-1, keepdims=True)
    return offset * lax.rsqrt(spread + 1e-12) * gain + shift


def gelu_tanh(values):
    return jax.nn.gelu(values, approximate=True)


def ring_body(
    tokens,
    cotangent,
    lengths,
    query_weight,
    key_weight,
    value_weight,
    output_weight,
    up_weight,
    down_weight,
    query_bias,
    value_bias,
    output_bias,
    up_bias,
    down_bias,
    attn_gain,
    attn_shift,
    ffn_gain,
    ffn_shift,
):
    seqs, stretch, width = tokens.shape
    rows = seqs * stretch
    heads = HEADS
    head = width // heads
    gathered = (
        lax.all_gather(query_weight, ("dp", "blk"), axis=0, tiled=True),
        lax.all_gather(key_weight, ("dp", "blk"), axis=0, tiled=True),
        lax.all_gather(value_weight, ("dp", "blk"), axis=0, tiled=True),
        lax.all_gather(output_weight, ("dp", "blk"), axis=0, tiled=True),
        lax.all_gather(up_weight, ("dp", "blk"), axis=0, tiled=True),
        lax.all_gather(down_weight, ("dp", "blk"), axis=0, tiled=True),
        lax.all_gather(query_bias, ("dp", "blk"), axis=0, tiled=True),
        lax.all_gather(value_bias, ("dp", "blk"), axis=0, tiled=True),
        lax.all_gather(output_bias, ("dp", "blk"), axis=0, tiled=True),
        lax.all_gather(up_bias, ("dp", "blk"), axis=0, tiled=True),
        lax.all_gather(down_bias, ("dp", "blk"), axis=0, tiled=True),
        lax.all_gather(attn_gain, ("dp", "blk"), axis=0, tiled=True),
        lax.all_gather(attn_shift, ("dp", "blk"), axis=0, tiled=True),
        lax.all_gather(ffn_gain, ("dp", "blk"), axis=0, tiled=True),
        lax.all_gather(ffn_shift, ("dp", "blk"), axis=0, tiled=True),
    )
    query_full, key_full, value_full, output_full, upper_full, lower_full = gathered[:6]
    (
        bias_query,
        bias_value,
        bias_output,
        bias_upper,
        bias_lower,
        gain_one,
        shift_one,
        gain_two,
        shift_two,
    ) = [item.astype(jnp.float32) for item in gathered[6:]]
    flat = tokens.reshape(rows, width)
    queries = (matmul(flat, query_full) + bias_query).astype(jnp.bfloat16)
    keys_own = matmul(flat, key_full).astype(jnp.bfloat16)
    values_own = (matmul(flat, value_full) + bias_value).astype(jnp.bfloat16)
    query_heads = queries.reshape(seqs, stretch, heads, head)
    own_block = lax.axis_index("blk")
    cycle_size = lax.axis_size("blk")
    start = jnp.int32(0)
    key_piece = lax.all_gather(keys_own.reshape(seqs, stretch, width), "blk", axis=1, tiled=True)
    value_piece = lax.all_gather(
        values_own.reshape(seqs, stretch, width), "blk", axis=1, tiled=True
    )
    count = key_piece.shape[1]
    span = min(count, stretch)
    row_max = jnp.full((seqs, stretch, heads), -1e30, jnp.float32)
    row_total = jnp.zeros((seqs, stretch, heads), jnp.float32)
    accum = jnp.zeros((seqs, stretch, heads, head), jnp.float32)
    for part_no in range(count // span):
        key_heads = key_piece[:, part_no * span : (part_no + 1) * span].reshape(
            seqs, span, heads, head
        )
        value_heads = value_piece[:, part_no * span : (part_no + 1) * span].reshape(
            seqs, span, heads, head
        )
        positions = start + part_no * span + jnp.arange(span, dtype=jnp.int32)
        valid = positions[None, :] < lengths[:, None]
        scores = (
            jnp.einsum(
                "sqhd,skhd->sqhk", query_heads, key_heads, preferred_element_type=jnp.float32
            )
            * 0.125
        )
        scores = jnp.where(valid[:, None, None, :], scores, -jnp.inf)
        new_max = jnp.maximum(row_max, jnp.max(scores, axis=-1))
        expo = jnp.exp(scores - new_max[..., None])
        factor = jnp.exp(row_max - new_max)
        row_total = row_total * factor + jnp.sum(expo, axis=-1)
        accum = accum * factor[..., None] + jnp.einsum(
            "sqhk,skhd->sqhd",
            expo.astype(jnp.bfloat16),
            value_heads,
            preferred_element_type=jnp.float32,
        )
        row_max = new_max
    row_max, row_total, accum = (row_max, row_total, accum)
    log_total = row_max + jnp.log(row_total)
    context_full = accum / row_total[..., None]
    context = context_full.reshape(rows, width).astype(jnp.bfloat16)
    attended = matmul(context, output_full) + bias_output
    hidden, norm_one_back = jax.vjp(
        layer_norm, flat.astype(jnp.float32) + attended, gain_one, shift_one
    )
    hidden_low = hidden.astype(jnp.bfloat16)
    upward = matmul(hidden_low, upper_full) + bias_upper
    active_full, gelu_back = jax.vjp(gelu_tanh, upward)
    active = active_full.astype(jnp.bfloat16)
    downward = matmul(active, lower_full) + bias_lower
    output_full32, norm_two_back = jax.vjp(layer_norm, hidden + downward, gain_two, shift_two)
    layer_out = output_full32.astype(jnp.bfloat16).reshape(seqs, stretch, width)
    query_back, key_back, value_back, output_back, upper_back, lower_back = (
        lax.all_gather(query_weight, ("dp", "blk"), axis=0, tiled=True),
        lax.all_gather(key_weight, ("dp", "blk"), axis=0, tiled=True),
        lax.all_gather(value_weight, ("dp", "blk"), axis=0, tiled=True),
        lax.all_gather(output_weight, ("dp", "blk"), axis=0, tiled=True),
        lax.all_gather(up_weight, ("dp", "blk"), axis=0, tiled=True),
        lax.all_gather(down_weight, ("dp", "blk"), axis=0, tiled=True),
    )
    grad_outer = cotangent.reshape(rows, width).astype(jnp.float32)
    grad_res_two, grad_gain_two, grad_shift_two = norm_two_back(grad_outer)
    grad_down = grad_res_two.astype(jnp.bfloat16)
    grad_lower_bias = jnp.sum(grad_down, axis=0, dtype=jnp.float32)
    grad_lower = trans_times(active, grad_down)
    grad_active = times_trans(grad_down, lower_back)
    (grad_upward,) = gelu_back(grad_active)
    grad_up = grad_upward.astype(jnp.bfloat16)
    grad_upper_bias = jnp.sum(grad_up, axis=0, dtype=jnp.float32)
    grad_upper = trans_times(hidden_low, grad_up)
    grad_hidden = grad_res_two + times_trans(grad_up, upper_back)
    grad_res_one, grad_gain_one, grad_shift_one = norm_one_back(grad_hidden)
    grad_attended = grad_res_one.astype(jnp.bfloat16)
    grad_output_bias = jnp.sum(grad_attended, axis=0, dtype=jnp.float32)
    grad_output = trans_times(context, grad_attended)
    grad_context = times_trans(grad_attended, output_back).astype(jnp.bfloat16)
    context_grad_heads = grad_context.reshape(seqs, stretch, heads, head)
    delta = jnp.sum(context_grad_heads.astype(jnp.float32) * context_full, axis=-1)

    def contribute(key_value, source, pair_grad, query_grad):
        key_heads = key_value[0]
        value_heads = key_value[1]
        positions = source * stretch + jnp.arange(stretch, dtype=jnp.int32)
        valid = positions[None, :] < lengths[:, None]
        scores = (
            jnp.einsum(
                "sqhd,skhd->sqhk", query_heads, key_heads, preferred_element_type=jnp.float32
            )
            * 0.125
        )
        probs = jnp.where(valid[:, None, None, :], jnp.exp(scores - log_total[..., None]), 0.0)
        grad_probs = jnp.einsum(
            "sqhd,skhd->sqhk", context_grad_heads, value_heads, preferred_element_type=jnp.float32
        )
        grad_scores = (probs * (grad_probs - delta[..., None])).astype(jnp.bfloat16)
        query_grad = (
            query_grad
            + jnp.einsum(
                "sqhk,skhd->sqhd", grad_scores, key_heads, preferred_element_type=jnp.float32
            )
            * 0.125
        )
        key_part = (
            jnp.einsum(
                "sqhk,sqhd->skhd", grad_scores, query_heads, preferred_element_type=jnp.float32
            )
            * 0.125
        )
        value_part = jnp.einsum(
            "sqhk,sqhd->skhd",
            probs.astype(jnp.bfloat16),
            context_grad_heads,
            preferred_element_type=jnp.float32,
        )
        pair_grad = pair_grad + jnp.stack([key_part, value_part])
        return (pair_grad, query_grad)

    def rotate_grads(pair_grad):
        return shifted(pair_grad.astype(jnp.bfloat16), "blk", 1).astype(pair_grad.dtype)

    key_value_own = jnp.stack(
        [
            keys_own.reshape(seqs, stretch, heads, head),
            values_own.reshape(seqs, stretch, heads, head),
        ]
    )
    pair_grad, query_grad = contribute(
        key_value_own,
        own_block,
        jnp.zeros((2, seqs, stretch, heads, head), jnp.float32),
        jnp.zeros((seqs, stretch, heads, head), jnp.float32),
    )

    def cycle_turn(turn, state):
        key_value_now, pair_now, query_now = state
        key_value_now = shifted(key_value_now, "blk", 1)
        pair_now = rotate_grads(pair_now)
        source = (own_block - turn) % cycle_size
        pair_now, query_now = contribute(key_value_now, source, pair_now, query_now)
        return (key_value_now, pair_now, query_now)

    final_state = lax.fori_loop(1, cycle_size, cycle_turn, (key_value_own, pair_grad, query_grad))
    pair_home = rotate_grads(final_state[1])
    grad_queries = final_state[2].reshape(rows, width).astype(jnp.bfloat16)
    grad_keys = pair_home[0].reshape(rows, width).astype(jnp.bfloat16)
    grad_values = pair_home[1].reshape(rows, width).astype(jnp.bfloat16)
    grad_query = trans_times(flat, grad_queries)
    grad_key = trans_times(flat, grad_keys)
    grad_value = trans_times(flat, grad_values)
    grad_query_bias = jnp.sum(grad_queries, axis=0, dtype=jnp.float32)
    grad_value_bias = jnp.sum(grad_values, axis=0, dtype=jnp.float32)
    tokens_grad = (
        grad_res_one
        + times_trans(grad_queries, query_back)
        + times_trans(grad_keys, key_back)
        + times_trans(grad_values, value_back)
    ).reshape(seqs, stretch, width)
    shares = (
        lax.psum_scatter(grad_query, ("dp", "blk"), scatter_dimension=0, tiled=True),
        lax.psum_scatter(grad_key, ("dp", "blk"), scatter_dimension=0, tiled=True),
        lax.psum_scatter(grad_value, ("dp", "blk"), scatter_dimension=0, tiled=True),
        lax.psum_scatter(grad_output, ("dp", "blk"), scatter_dimension=0, tiled=True),
        lax.psum_scatter(grad_upper, ("dp", "blk"), scatter_dimension=0, tiled=True),
        lax.psum_scatter(grad_lower, ("dp", "blk"), scatter_dimension=0, tiled=True),
        lax.psum_scatter(grad_query_bias, ("dp", "blk"), scatter_dimension=0, tiled=True),
        lax.psum_scatter(grad_value_bias, ("dp", "blk"), scatter_dimension=0, tiled=True),
        lax.psum_scatter(grad_output_bias, ("dp", "blk"), scatter_dimension=0, tiled=True),
        lax.psum_scatter(grad_upper_bias, ("dp", "blk"), scatter_dimension=0, tiled=True),
        lax.psum_scatter(grad_lower_bias, ("dp", "blk"), scatter_dimension=0, tiled=True),
        lax.psum_scatter(grad_gain_one, ("dp", "blk"), scatter_dimension=0, tiled=True),
        lax.psum_scatter(grad_shift_one, ("dp", "blk"), scatter_dimension=0, tiled=True),
        lax.psum_scatter(grad_gain_two, ("dp", "blk"), scatter_dimension=0, tiled=True),
        lax.psum_scatter(grad_shift_two, ("dp", "blk"), scatter_dimension=0, tiled=True),
    )
    return (layer_out, tokens_grad) + tuple(shares)


def dot_f32(left, right, dims):
    return lax.dot_general(left, right, (dims, ((), ())), preferred_element_type=jnp.float32)


NT = ((1,), (1,))
NN = ((1,), (0,))


def split_three(values):
    high = values.astype(jnp.bfloat16).astype(jnp.float32)
    rest = values - high
    mid = rest.astype(jnp.bfloat16).astype(jnp.float32)
    return high, mid, rest - mid


def spread_three(lane, base, values, into):
    for step, part in enumerate(split_three(values)):
        into = jnp.where(lane == base + step, part, into)
    return into


def fill_keys(info_ref, keys, values, key_aug, value_aug, value_fill, chunk):
    length = keys.shape[0]
    lane = lax.broadcasted_iota(jnp.int32, (chunk, LANES), 1)
    row = lax.broadcasted_iota(jnp.int32, (chunk, LANES), 0)
    for part in range(length // chunk):
        at = slice(part * chunk, (part + 1) * chunk)
        off = (lane == 3) & (row + info_ref[1 + part] >= info_ref[0])
        mask = jnp.where(off, MASKED, 0.0)
        for one in range(PER_TILE):
            mine = lane // (LANES // PER_TILE) == one
            base = 4 * one
            minus = (lane >= base) & (lane < base + 3)
            key_aug[one, at, :LANES] = jnp.where(mine, keys[at], jnp.zeros((), keys.dtype))
            key_aug[one, at, LANES:] = jnp.where(minus, -1.0, mask).astype(jnp.bfloat16)
            value_aug[one, at, :LANES] = jnp.where(mine, values[at], jnp.zeros((), keys.dtype))
            if value_fill:
                value_aug[one, at, LANES:] = jnp.ones((chunk, LANES), jnp.bfloat16)
            else:
                value_aug[one, at, LANES:] = jnp.where(minus, -1.0, 0.0).astype(jnp.bfloat16)


def attend_kernel(span, info_ref, query_ref, key_ref, value_ref, out_ref, aux_ref, key_aug, value_aug):
    length = key_ref.shape[0]
    tile = query_ref.shape[0]
    lane = lax.broadcasted_iota(jnp.int32, (1, LANES), 1)

    @pl.when(pl.program_id(1) == 0)
    def _():
        fill_keys(info_ref, key_ref, value_ref, key_aug, value_aug, True, length // 8)

    one_lane = jnp.where(lane == 3, 1.0, 0.0)
    flag = jnp.broadcast_to(one_lane.astype(jnp.bfloat16), (tile, LANES))
    query = jnp.concatenate([query_ref[...], flag], axis=1)
    pieces = [slice(at, at + span) for at in range(0, length, span)]
    scores, peaks = [], []
    for one in range(PER_TILE):
        peak = None
        row = []
        for at in pieces:
            score = dot_f32(query, key_aug[one, at], NT)
            row.append(score)
            for low in range(0, span, LANES):
                part = score[:, low : low + LANES]
                peak = part if peak is None else jnp.maximum(peak, part)
        scores.append(row)
        peaks.append(jnp.max(peak, axis=1, keepdims=True))
    out = None
    aux = one_lane
    for one in range(PER_TILE):
        total = None
        for at, score in zip(pieces, scores[one]):
            expo = jnp.exp2((score - peaks[one]) * SCORE_SCALE).astype(jnp.bfloat16)
            part = dot_f32(expo, value_aug[one, at], NN)
            total = part if total is None else total + part
        weight = total[:, LANES:]
        part = total[:, :LANES] / weight
        out = part if out is None else out + part
        log_total = jnp.log2(weight) * (1.0 / SCORE_SCALE) + peaks[one]
        aux = spread_three(lane, 4 * one, log_total, aux)
    out_ref[...] = out
    aux_ref[...] = aux.astype(jnp.bfloat16)


def attend(qkv, info, tile, span):
    length, width = qkv.shape[0], qkv.shape[1] // 3
    tiles = width // LANES
    query_spec = pl.BlockSpec((tile, LANES), lambda pair, at: (at, pair))
    return pl.pallas_call(
        functools.partial(attend_kernel, span),
        grid=(tiles, length // tile),
        in_specs=[
            pl.BlockSpec(memory_space=pltpu.SMEM),
            query_spec,
            pl.BlockSpec((length, LANES), lambda pair, at: (0, tiles + pair)),
            pl.BlockSpec((length, LANES), lambda pair, at: (0, 2 * tiles + pair)),
        ],
        out_specs=[query_spec, query_spec],
        out_shape=[
            jax.ShapeDtypeStruct((length, width), jnp.float32),
            jax.ShapeDtypeStruct((length, width), jnp.bfloat16),
        ],
        scratch_shapes=[pltpu.VMEM((PER_TILE, length, 2 * LANES), jnp.bfloat16)] * 2,
        compiler_params=pltpu.CompilerParams(vmem_limit_bytes=VMEM_LIMIT),
        cost_estimate=pl.CostEstimate(
            flops=16 * length * length * width,
            bytes_accessed=12 * length * width,
            transcendentals=length * length * width // 64,
        ),
        name="attend",
    )(info, qkv, qkv, qkv)


def attend_back_kernel(
    span, info_ref, query_ref, key_ref, value_ref, grad_ref, out_ref, aux_ref,
    query_grad_ref, key_grad_ref, value_grad_ref, key_aug, value_aug, key_cols, key_sum, value_sum,
):
    length = key_ref.shape[0]
    tile = query_ref.shape[0]
    wide = LANES // PER_TILE
    lane = lax.broadcasted_iota(jnp.int32, (1, LANES), 1)

    @pl.when(pl.program_id(1) == 0)
    def _():
        fill_keys(info_ref, key_ref, value_ref, key_aug, value_aug, False, length // 8)
        key_cols[...] = key_ref[...].T
        key_sum[...] = jnp.zeros_like(key_sum)
        value_sum[...] = jnp.zeros_like(value_sum)

    plain, grad = query_ref[...], grad_ref[...]
    query = jnp.concatenate([plain, aux_ref[...]], axis=1)
    product = grad.astype(jnp.float32) * out_ref[...]
    delta = jnp.zeros((tile, LANES), jnp.float32)
    for one in range(PER_TILE):
        own = jnp.sum(jnp.where(lane // wide == one, product, 0.0), axis=1, keepdims=True)
        delta = spread_three(lane, 4 * one, own, delta)
    grad_aug = jnp.concatenate([grad, delta.astype(jnp.bfloat16)], axis=1)
    nothing = jnp.zeros((), plain.dtype)
    query_rows = []
    for one in range(PER_TILE):
        mine = lane // wide == one
        query_own = jnp.where(mine, plain, nothing)
        grad_own = jnp.where(mine, grad, nothing)
        total = None
        for low in range(0, length, span):
            at = slice(low, low + span)
            score = dot_f32(key_aug[one, at], query, NT)
            grad_probs = dot_f32(value_aug[one, at], grad_aug, NT)
            probs = jnp.exp2(score * SCORE_SCALE)
            grad_scores = (probs * grad_probs).astype(jnp.bfloat16)
            value_sum[at] += dot_f32(probs.astype(jnp.bfloat16), grad_own, NN)
            key_sum[at] += dot_f32(grad_scores, query_own, NN)
            part = dot_f32(key_cols[wide * one : wide * (one + 1), at], grad_scores, NN)
            total = part if total is None else total + part
        query_rows.append(total)
    query_grad_ref[...] = (jnp.concatenate(query_rows, axis=0).T * 0.125).astype(jnp.bfloat16)

    @pl.when(pl.program_id(1) == pl.num_programs(1) - 1)
    def _():
        key_grad_ref[...] = (key_sum[...] * 0.125).astype(jnp.bfloat16)
        value_grad_ref[...] = value_sum[...].astype(jnp.bfloat16)


def attend_back(qkv, grad, out, aux, info, tile, span):
    length, width = qkv.shape[0], qkv.shape[1] // 3
    tiles = width // LANES
    query_spec = pl.BlockSpec((tile, LANES), lambda pair, at: (at, pair))
    whole = pl.BlockSpec((length, LANES), lambda pair, at: (0, pair))
    result = jax.ShapeDtypeStruct((length, width), jnp.bfloat16)
    return pl.pallas_call(
        functools.partial(attend_back_kernel, span),
        grid=(tiles, length // tile),
        in_specs=[
            pl.BlockSpec(memory_space=pltpu.SMEM),
            query_spec,
            pl.BlockSpec((length, LANES), lambda pair, at: (0, tiles + pair)),
            pl.BlockSpec((length, LANES), lambda pair, at: (0, 2 * tiles + pair)),
            query_spec,
            query_spec,
            query_spec,
        ],
        out_specs=[query_spec, whole, whole],
        out_shape=[result] * 3,
        scratch_shapes=[pltpu.VMEM((PER_TILE, length, 2 * LANES), jnp.bfloat16)] * 2
        + [pltpu.VMEM((LANES, length), jnp.bfloat16)]
        + [pltpu.VMEM((length, LANES), jnp.float32)] * 2,
        compiler_params=pltpu.CompilerParams(vmem_limit_bytes=VMEM_LIMIT),
        cost_estimate=pl.CostEstimate(
            flops=40 * length * length * width,
            bytes_accessed=22 * length * width,
            transcendentals=length * length * width // 64,
        ),
        name="attend_back",
    )(info, qkv, qkv, qkv, grad, out, aux)


def body(
    tokens,
    cotangent,
    lengths,
    query_weight,
    key_weight,
    value_weight,
    output_weight,
    up_weight,
    down_weight,
    query_bias,
    value_bias,
    output_bias,
    up_bias,
    down_bias,
    attn_gain,
    attn_shift,
    ffn_gain,
    ffn_shift,
):
    seqs, stretch, width = tokens.shape
    rows = seqs * stretch
    n_pair, n_core, n_blk = (lax.axis_size(axis) for axis in ALL)
    devices = n_pair * n_core * n_blk
    core, blk = lax.axis_index("core"), lax.axis_index("blk")
    half, cols = stretch // 2, width // 2
    own_rows = n_blk * half
    share = query_weight.shape[0]
    bf16, f32 = jnp.bfloat16, jnp.float32

    def exchange_table(step, back):
        table = []
        for pair in range(n_pair):
            for src_core in range(n_core):
                for src in range(n_blk):
                    piece = src ^ step
                    sender = (pair * n_core + src_core) * n_blk + src
                    target = (pair * n_core + piece % 2) * n_blk + seqs * src_core + piece // 2
                    table.append((target, sender) if back else (sender, target))
        return table

    def to_sequence(array):
        pieces = array.reshape(n_blk, half, array.shape[-1])
        return [
            lax.ppermute(
                lax.dynamic_index_in_dim(pieces, blk ^ step, 0, keepdims=False),
                ALL,
                exchange_table(step, False),
            )
            for step in range(n_blk)
        ]

    def from_sequence(chunks):
        got = [lax.ppermute(c, ALL, exchange_table(step, True)) for step, c in enumerate(chunks)]
        bit = 1
        while bit < n_blk:
            flip = (blk & bit) != 0
            got = [jnp.where(flip, got[at ^ bit], got[at]) for at in range(n_blk)]
            bit *= 2
        return jnp.concatenate(got, axis=0)

    def other_core(array):
        return lax.ppermute(array, "core", [(0, 1), (1, 0)])

    def columns(array, which):
        return lax.dynamic_slice_in_dim(array, which * cols, cols, axis=-1)

    def small_block(items, lanes):
        flat = jnp.concatenate([item.reshape(item.shape[0], -1) for item in items], axis=1)
        flat = jnp.pad(flat, ((0, 0), (0, lanes - flat.shape[1])))
        return jnp.pad(flat[:, None, :], ((0, 0), (0, 7), (0, 0)))

    coded = jnp.stack([lengths // 16, lengths % 16]).astype(bf16)
    first = jnp.concatenate(
        [query_weight, key_weight, value_weight]
        + [small_block([query_bias[None], value_bias[None], coded.reshape(1, -1)], width)[0]],
        axis=0,
    )
    second = jnp.concatenate(
        [output_weight]
        + [up_weight[:, at : at + width] for at in range(0, up_weight.shape[1], width)]
        + [down_weight]
        + [
            small_block(
                [
                    item[None]
                    for item in (
                        output_bias, up_bias, down_bias, attn_gain, attn_shift, ffn_gain, ffn_shift
                    )
                ],
                width,
            )[0]
        ],
        axis=0,
    )
    first = lax.all_gather(first, ALL, axis=0)
    second = lax.all_gather(second, ALL, axis=0)
    mine = columns(first[:, : 3 * share], core).reshape(devices, 3, share, cols)
    qkv_weight = mine.transpose(0, 2, 1, 3).reshape(width, 3 * cols)
    small = first[:, 3 * share]
    bias_query = columns(small[:, :share].reshape(width), core)
    bias_value = columns(small[:, share : 2 * share].reshape(width), core)
    qkv_bias = jnp.concatenate([bias_query, jnp.zeros_like(bias_query), bias_value]).astype(f32)
    code = small[:, 2 * share : 2 * share + 2 * seqs].astype(jnp.int32)
    code = code.reshape(n_pair, n_core, n_blk, 2, seqs)[:, :, 0]
    code = code[:, :, 0] * 16 + code[:, :, 1]
    own_length = code.reshape(n_pair, n_core * seqs)[lax.axis_index("pair"), blk]

    arrived = to_sequence(tokens)
    own_tokens = jnp.concatenate(arrived, axis=0)
    sequence = jnp.concatenate([own_tokens, other_core(own_tokens)], axis=0)
    starts = []
    for side in (core, 1 - core):
        piece = 2 * (blk % seqs) + side
        starts += [(piece ^ step) * stretch + side * half for step in range(n_blk)]
    info = jnp.stack([own_length] + starts).astype(jnp.int32)

    qkv = (matmul(sequence, qkv_weight) + qkv_bias).astype(bf16)
    context_seq, aux = attend(qkv, info, 512, 512)
    context_low = context_seq.astype(bf16)
    kept, crossed = context_low[:own_rows], other_core(context_low[own_rows:])
    joined = jnp.concatenate(
        [jnp.where(core == 0, kept, crossed), jnp.where(core == 0, crossed, kept)], axis=1
    )
    context = from_sequence([joined[at : at + half] for at in range(0, own_rows, half)])

    output_full = second[:, :share].reshape(width, width)
    fold = up_weight.shape[1] // width
    up_rows = second[:, share : (1 + fold) * share].reshape(devices, fold, share, width)
    upper_full = up_rows.transpose(0, 2, 1, 3).reshape(width, fold * width)
    lower_full = second[:, (1 + fold) * share : (1 + 2 * fold) * share].reshape(fold * width, width)
    small = second[:, (1 + 2 * fold) * share].astype(f32)
    vectors, at = [], 0
    for item in (output_bias, up_bias, down_bias, attn_gain, attn_shift, ffn_gain, ffn_shift):
        vectors.append(small[:, at : at + item.shape[0]].reshape(-1))
        at += item.shape[0]
    bias_output, bias_upper, bias_lower, gain_one, shift_one, gain_two, shift_two = vectors

    flat = tokens.reshape(rows, width)
    attended = matmul(context, output_full) + bias_output
    hidden, norm_one_back = jax.vjp(layer_norm, flat.astype(f32) + attended, gain_one, shift_one)
    hidden_low = hidden.astype(bf16)
    upward = matmul(hidden_low, upper_full) + bias_upper
    active_full, gelu_back = jax.vjp(gelu_tanh, upward)
    active = active_full.astype(bf16)
    downward = matmul(active, lower_full) + bias_lower
    output_full32, norm_two_back = jax.vjp(layer_norm, hidden + downward, gain_two, shift_two)
    layer_out = output_full32.astype(bf16).reshape(seqs, stretch, width)

    grad_outer = cotangent.reshape(rows, width).astype(f32)
    grad_res_two, grad_gain_two, grad_shift_two = norm_two_back(grad_outer)
    grad_down = grad_res_two.astype(bf16)
    grad_active = times_trans(grad_down, lower_full)
    (grad_upward,) = gelu_back(grad_active)
    grad_up = grad_upward.astype(bf16)
    grad_hidden = grad_res_two + times_trans(grad_up, upper_full)
    grad_res_one, grad_gain_one, grad_shift_one = norm_one_back(grad_hidden)
    grad_attended = grad_res_one.astype(bf16)
    grad_context = times_trans(grad_attended, output_full).astype(bf16)

    own_grad = jnp.concatenate(
        to_sequence(grad_context.reshape(seqs, stretch, width)), axis=0
    )
    context_grad = jnp.concatenate(
        [columns(own_grad, core), other_core(columns(own_grad, 1 - core))], axis=0
    )

    grad_lower = trans_times(active, grad_down)
    grad_upper = trans_times(hidden_low, grad_up)
    grad_output = trans_times(context, grad_attended)
    grad_upper = grad_upper.reshape(devices, share, fold, width).transpose(0, 2, 1, 3)
    small_grads = small_block(
        [
            item.reshape(devices, -1)
            for item in (
                jnp.sum(grad_attended, axis=0, dtype=f32),
                jnp.sum(grad_up, axis=0, dtype=f32),
                jnp.sum(grad_down, axis=0, dtype=f32),
                grad_gain_one,
                grad_shift_one,
                grad_gain_two,
                grad_shift_two,
            )
        ],
        width,
    )
    second_grads = jnp.concatenate(
        [
            grad_output.reshape(devices, share, width).astype(bf16),
            grad_upper.reshape(devices, fold * share, width).astype(bf16),
            grad_lower.reshape(devices, fold * share, width).astype(bf16),
            small_grads.astype(bf16),
        ],
        axis=1,
    )
    second_grads = lax.psum_scatter(second_grads, ALL, scatter_dimension=0)

    query_grad, key_grad, value_grad = attend_back(
        qkv, context_grad, context_seq, aux, info, 512, 512
    )
    grad_seq = jnp.concatenate([query_grad, key_grad, value_grad], axis=1)
    partial = times_trans(grad_seq, qkv_weight)
    summed = (partial[:own_rows] + other_core(partial[own_rows:].astype(bf16)).astype(f32)).astype(bf16)
    returned = from_sequence([summed[at : at + half] for at in range(0, own_rows, half)])
    tokens_grad = (grad_res_one + returned.astype(f32)).reshape(seqs, stretch, width)

    def by_owner(array):
        array = array.reshape((n_pair, n_core, n_blk) + array.shape[1:])
        return jnp.moveaxis(array, 1, 2).reshape((n_pair * n_blk, n_core) + array.shape[3:])

    grad_qkv = trans_times(sequence, grad_seq).astype(bf16).reshape(devices, share, 3 * cols)
    bias_sums = [
        lax.dynamic_update_slice_in_dim(
            jnp.zeros((width,), f32), jnp.sum(item, axis=0, dtype=f32), core * cols, 0
        ).reshape(devices, share)
        for item in (query_grad, value_grad)
    ]
    first_grads = jnp.concatenate(
        [
            by_owner(grad_qkv).reshape(n_pair * n_blk, n_core * share, 3 * cols),
            by_owner(small_block(bias_sums, 3 * cols)).reshape(n_pair * n_blk, 16, 3 * cols).astype(bf16),
        ],
        axis=1,
    )
    first_grads = lax.psum_scatter(first_grads, ("pair", "blk"), scatter_dimension=0)

    def for_core(which):
        block = lax.dynamic_slice_in_dim(first_grads, which * share, share, axis=0)
        extra = lax.dynamic_slice_in_dim(first_grads, n_core * share + which * 8, 8, axis=0)
        return jnp.concatenate([block, extra], axis=0)

    kept, crossed = for_core(core), other_core(for_core(1 - core))
    bias_both = (kept[share].astype(f32) + crossed[share].astype(f32))
    left = jnp.where(core == 0, kept, crossed)[:share].astype(f32)
    right = jnp.where(core == 0, crossed, kept)[:share].astype(f32)
    projections = tuple(
        jnp.concatenate([left[:, at : at + cols], right[:, at : at + cols]], axis=1)
        for at in range(0, 3 * cols, cols)
    )
    second_grads = second_grads.astype(f32)
    out_weight_grad = second_grads[:share]
    up_weight_grad = jnp.concatenate(
        [second_grads[at : at + share] for at in range(share, (1 + fold) * share, share)], axis=1
    )
    down_weight_grad = second_grads[(1 + fold) * share : (1 + 2 * fold) * share]
    line = second_grads[(1 + 2 * fold) * share]
    vectors, at = [], 0
    for item in (output_bias, up_bias, down_bias, attn_gain, attn_shift, ffn_gain, ffn_shift):
        vectors.append(line[at : at + item.shape[0]])
        at += item.shape[0]
    return (
        (layer_out, tokens_grad)
        + projections
        + (out_weight_grad, up_weight_grad, down_weight_grad)
        + (bias_both[:share], bias_both[share : 2 * share])
        + tuple(vectors)
    )


def fits(mesh, tokens, up_weight):
    n_dp, n_blk = mesh.shape["dp"], mesh.shape["blk"]
    batch, length, width = tokens.shape
    if n_dp % 2 or batch % n_dp or 2 * (batch // n_dp) != n_blk or n_blk & (n_blk - 1):
        return False
    share = width // (n_dp * n_blk)
    fold = up_weight.shape[1] // width
    return (
        width == HEADS * 64
        and width % (4 * LANES // PER_TILE) == 0
        and up_weight.shape[1] == fold * width
        and share * n_dp * n_blk == width
        and share % 8 == 0
        and (6 + fold) * share <= width
        and length % (16 * n_blk) == 0
        and length % 512 == 0
        and length <= 4096
    )


def solution(mesh):
    n_dp, n_blk = mesh.shape["dp"], mesh.shape["blk"]

    def step(*args):
        spread = ("dp", "blk")
        one, use = ring_body, mesh
        where = {"dp": "dp", "blk": "blk", spread: spread}
        if fits(mesh, args[0], args[7]):
            one, use = body, Mesh(mesh.devices.reshape(n_dp // 2, 2, n_blk), ALL)
            where = {"dp": ("pair", "core"), "blk": "blk", spread: ALL}
        block = P(where["dp"], where["blk"], None)
        matrix = P(where[spread], None)
        vector = P(where[spread])
        return jax.shard_map(
            one,
            mesh=use,
            in_specs=(block, block, P(where["dp"])) + (matrix,) * 6 + (vector,) * 9,
            out_specs=(block, block) + (matrix,) * 6 + (vector,) * 9,
            check_vma=False,
        )(*args)

    return step
```

```python
import functools

import jax
import jax.numpy as jnp
from jax import lax
from jax.experimental import pallas as pl
from jax.experimental.pallas import tpu as pltpu
from jax.sharding import Mesh
from jax.sharding import PartitionSpec as P

HEADS = 12
LANES = 128
PER_TILE = 2
SCORE_SCALE = 0.125 * 1.4426950408889634
MASKED = -1e30
ALL = ("pair", "core", "blk")
VMEM_LIMIT = 56 << 20


def shifted(array, axis, by):
    length = lax.axis_size(axis)
    return lax.ppermute(array, axis, [(i, (i + by) % length) for i in range(length)])


def matmul(left, right):
    return jnp.dot(left, right, preferred_element_type=jnp.float32)


def times_trans(left, right):
    return lax.dot_general(
        left, right, (((1,), (1,)), ((), ())), preferred_element_type=jnp.float32
    )


def trans_times(left, right):
    return lax.dot_general(
        left, right, (((0,), (0,)), ((), ())), preferred_element_type=jnp.float32
    )


def layer_norm(values, gain, shift):
    center = jnp.mean(values, axis=-1, keepdims=True)
    offset = values - center
    spread = jnp.mean(offset * offset, axis=-1, keepdims=True)
    return offset * lax.rsqrt(spread + 1e-12) * gain + shift


def gelu_tanh(values):
    return jax.nn.gelu(values, approximate=True)


def ring_body(
    tokens,
    cotangent,
    lengths,
    query_weight,
    key_weight,
    value_weight,
    output_weight,
    up_weight,
    down_weight,
    query_bias,
    value_bias,
    output_bias,
    up_bias,
    down_bias,
    attn_gain,
    attn_shift,
    ffn_gain,
    ffn_shift,
):
    seqs, stretch, width = tokens.shape
    rows = seqs * stretch
    heads = HEADS
    head = width // heads
    gathered = (
        lax.all_gather(query_weight, ("dp", "blk"), axis=0, tiled=True),
        lax.all_gather(key_weight, ("dp", "blk"), axis=0, tiled=True),
        lax.all_gather(value_weight, ("dp", "blk"), axis=0, tiled=True),
        lax.all_gather(output_weight, ("dp", "blk"), axis=0, tiled=True),
        lax.all_gather(up_weight, ("dp", "blk"), axis=0, tiled=True),
        lax.all_gather(down_weight, ("dp", "blk"), axis=0, tiled=True),
        lax.all_gather(query_bias, ("dp", "blk"), axis=0, tiled=True),
        lax.all_gather(value_bias, ("dp", "blk"), axis=0, tiled=True),
        lax.all_gather(output_bias, ("dp", "blk"), axis=0, tiled=True),
        lax.all_gather(up_bias, ("dp", "blk"), axis=0, tiled=True),
        lax.all_gather(down_bias, ("dp", "blk"), axis=0, tiled=True),
        lax.all_gather(attn_gain, ("dp", "blk"), axis=0, tiled=True),
        lax.all_gather(attn_shift, ("dp", "blk"), axis=0, tiled=True),
        lax.all_gather(ffn_gain, ("dp", "blk"), axis=0, tiled=True),
        lax.all_gather(ffn_shift, ("dp", "blk"), axis=0, tiled=True),
    )
    query_full, key_full, value_full, output_full, upper_full, lower_full = gathered[:6]
    (
        bias_query,
        bias_value,
        bias_output,
        bias_upper,
        bias_lower,
        gain_one,
        shift_one,
        gain_two,
        shift_two,
    ) = [item.astype(jnp.float32) for item in gathered[6:]]
    flat = tokens.reshape(rows, width)
    queries = (matmul(flat, query_full) + bias_query).astype(jnp.bfloat16)
    keys_own = matmul(flat, key_full).astype(jnp.bfloat16)
    values_own = (matmul(flat, value_full) + bias_value).astype(jnp.bfloat16)
    query_heads = queries.reshape(seqs, stretch, heads, head)
    own_block = lax.axis_index("blk")
    cycle_size = lax.axis_size("blk")
    start = jnp.int32(0)
    key_piece = lax.all_gather(keys_own.reshape(seqs, stretch, width), "blk", axis=1, tiled=True)
    value_piece = lax.all_gather(
        values_own.reshape(seqs, stretch, width), "blk", axis=1, tiled=True
    )
    count = key_piece.shape[1]
    span = min(count, stretch)
    row_max = jnp.full((seqs, stretch, heads), -1e30, jnp.float32)
    row_total = jnp.zeros((seqs, stretch, heads), jnp.float32)
    accum = jnp.zeros((seqs, stretch, heads, head), jnp.float32)
    for part_no in range(count // span):
        key_heads = key_piece[:, part_no * span : (part_no + 1) * span].reshape(
            seqs, span, heads, head
        )
        value_heads = value_piece[:, part_no * span : (part_no + 1) * span].reshape(
            seqs, span, heads, head
        )
        positions = start + part_no * span + jnp.arange(span, dtype=jnp.int32)
        valid = positions[None, :] < lengths[:, None]
        scores = (
            jnp.einsum(
                "sqhd,skhd->sqhk", query_heads, key_heads, preferred_element_type=jnp.float32
            )
            * 0.125
        )
        scores = jnp.where(valid[:, None, None, :], scores, -jnp.inf)
        new_max = jnp.maximum(row_max, jnp.max(scores, axis=-1))
        expo = jnp.exp(scores - new_max[..., None])
        factor = jnp.exp(row_max - new_max)
        row_total = row_total * factor + jnp.sum(expo, axis=-1)
        accum = accum * factor[..., None] + jnp.einsum(
            "sqhk,skhd->sqhd",
            expo.astype(jnp.bfloat16),
            value_heads,
            preferred_element_type=jnp.float32,
        )
        row_max = new_max
    row_max, row_total, accum = (row_max, row_total, accum)
    log_total = row_max + jnp.log(row_total)
    context_full = accum / row_total[..., None]
    context = context_full.reshape(rows, width).astype(jnp.bfloat16)
    attended = matmul(context, output_full) + bias_output
    hidden, norm_one_back = jax.vjp(
        layer_norm, flat.astype(jnp.float32) + attended, gain_one, shift_one
    )
    hidden_low = hidden.astype(jnp.bfloat16)
    upward = matmul(hidden_low, upper_full) + bias_upper
    active_full, gelu_back = jax.vjp(gelu_tanh, upward)
    active = active_full.astype(jnp.bfloat16)
    downward = matmul(active, lower_full) + bias_lower
    output_full32, norm_two_back = jax.vjp(layer_norm, hidden + downward, gain_two, shift_two)
    layer_out = output_full32.astype(jnp.bfloat16).reshape(seqs, stretch, width)
    query_back, key_back, value_back, output_back, upper_back, lower_back = (
        lax.all_gather(query_weight, ("dp", "blk"), axis=0, tiled=True),
        lax.all_gather(key_weight, ("dp", "blk"), axis=0, tiled=True),
        lax.all_gather(value_weight, ("dp", "blk"), axis=0, tiled=True),
        lax.all_gather(output_weight, ("dp", "blk"), axis=0, tiled=True),
        lax.all_gather(up_weight, ("dp", "blk"), axis=0, tiled=True),
        lax.all_gather(down_weight, ("dp", "blk"), axis=0, tiled=True),
    )
    grad_outer = cotangent.reshape(rows, width).astype(jnp.float32)
    grad_res_two, grad_gain_two, grad_shift_two = norm_two_back(grad_outer)
    grad_down = grad_res_two.astype(jnp.bfloat16)
    grad_lower_bias = jnp.sum(grad_down, axis=0, dtype=jnp.float32)
    grad_lower = trans_times(active, grad_down)
    grad_active = times_trans(grad_down, lower_back)
    (grad_upward,) = gelu_back(grad_active)
    grad_up = grad_upward.astype(jnp.bfloat16)
    grad_upper_bias = jnp.sum(grad_up, axis=0, dtype=jnp.float32)
    grad_upper = trans_times(hidden_low, grad_up)
    grad_hidden = grad_res_two + times_trans(grad_up, upper_back)
    grad_res_one, grad_gain_one, grad_shift_one = norm_one_back(grad_hidden)
    grad_attended = grad_res_one.astype(jnp.bfloat16)
    grad_output_bias = jnp.sum(grad_attended, axis=0, dtype=jnp.float32)
    grad_output = trans_times(context, grad_attended)
    grad_context = times_trans(grad_attended, output_back).astype(jnp.bfloat16)
    context_grad_heads = grad_context.reshape(seqs, stretch, heads, head)
    delta = jnp.sum(context_grad_heads.astype(jnp.float32) * context_full, axis=-1)

    def contribute(key_value, source, pair_grad, query_grad):
        key_heads = key_value[0]
        value_heads = key_value[1]
        positions = source * stretch + jnp.arange(stretch, dtype=jnp.int32)
        valid = positions[None, :] < lengths[:, None]
        scores = (
            jnp.einsum(
                "sqhd,skhd->sqhk", query_heads, key_heads, preferred_element_type=jnp.float32
            )
            * 0.125
        )
        probs = jnp.where(valid[:, None, None, :], jnp.exp(scores - log_total[..., None]), 0.0)
        grad_probs = jnp.einsum(
            "sqhd,skhd->sqhk", context_grad_heads, value_heads, preferred_element_type=jnp.float32
        )
        grad_scores = (probs * (grad_probs - delta[..., None])).astype(jnp.bfloat16)
        query_grad = (
            query_grad
            + jnp.einsum(
                "sqhk,skhd->sqhd", grad_scores, key_heads, preferred_element_type=jnp.float32
            )
            * 0.125
        )
        key_part = (
            jnp.einsum(
                "sqhk,sqhd->skhd", grad_scores, query_heads, preferred_element_type=jnp.float32
            )
            * 0.125
        )
        value_part = jnp.einsum(
            "sqhk,sqhd->skhd",
            probs.astype(jnp.bfloat16),
            context_grad_heads,
            preferred_element_type=jnp.float32,
        )
        pair_grad = pair_grad + jnp.stack([key_part, value_part])
        return (pair_grad, query_grad)

    def rotate_grads(pair_grad):
        return shifted(pair_grad.astype(jnp.bfloat16), "blk", 1).astype(pair_grad.dtype)

    key_value_own = jnp.stack(
        [
            keys_own.reshape(seqs, stretch, heads, head),
            values_own.reshape(seqs, stretch, heads, head),
        ]
    )
    pair_grad, query_grad = contribute(
        key_value_own,
        own_block,
        jnp.zeros((2, seqs, stretch, heads, head), jnp.float32),
        jnp.zeros((seqs, stretch, heads, head), jnp.float32),
    )

    def cycle_turn(turn, state):
        key_value_now, pair_now, query_now = state
        key_value_now = shifted(key_value_now, "blk", 1)
        pair_now = rotate_grads(pair_now)
        source = (own_block - turn) % cycle_size
        pair_now, query_now = contribute(key_value_now, source, pair_now, query_now)
        return (key_value_now, pair_now, query_now)

    final_state = lax.fori_loop(1, cycle_size, cycle_turn, (key_value_own, pair_grad, query_grad))
    pair_home = rotate_grads(final_state[1])
    grad_queries = final_state[2].reshape(rows, width).astype(jnp.bfloat16)
    grad_keys = pair_home[0].reshape(rows, width).astype(jnp.bfloat16)
    grad_values = pair_home[1].reshape(rows, width).astype(jnp.bfloat16)
    grad_query = trans_times(flat, grad_queries)
    grad_key = trans_times(flat, grad_keys)
    grad_value = trans_times(flat, grad_values)
    grad_query_bias = jnp.sum(grad_queries, axis=0, dtype=jnp.float32)
    grad_value_bias = jnp.sum(grad_values, axis=0, dtype=jnp.float32)
    tokens_grad = (
        grad_res_one
        + times_trans(grad_queries, query_back)
        + times_trans(grad_keys, key_back)
        + times_trans(grad_values, value_back)
    ).reshape(seqs, stretch, width)
    shares = (
        lax.psum_scatter(grad_query, ("dp", "blk"), scatter_dimension=0, tiled=True),
        lax.psum_scatter(grad_key, ("dp", "blk"), scatter_dimension=0, tiled=True),
        lax.psum_scatter(grad_value, ("dp", "blk"), scatter_dimension=0, tiled=True),
        lax.psum_scatter(grad_output, ("dp", "blk"), scatter_dimension=0, tiled=True),
        lax.psum_scatter(grad_upper, ("dp", "blk"), scatter_dimension=0, tiled=True),
        lax.psum_scatter(grad_lower, ("dp", "blk"), scatter_dimension=0, tiled=True),
        lax.psum_scatter(grad_query_bias, ("dp", "blk"), scatter_dimension=0, tiled=True),
        lax.psum_scatter(grad_value_bias, ("dp", "blk"), scatter_dimension=0, tiled=True),
        lax.psum_scatter(grad_output_bias, ("dp", "blk"), scatter_dimension=0, tiled=True),
        lax.psum_scatter(grad_upper_bias, ("dp", "blk"), scatter_dimension=0, tiled=True),
        lax.psum_scatter(grad_lower_bias, ("dp", "blk"), scatter_dimension=0, tiled=True),
        lax.psum_scatter(grad_gain_one, ("dp", "blk"), scatter_dimension=0, tiled=True),
        lax.psum_scatter(grad_shift_one, ("dp", "blk"), scatter_dimension=0, tiled=True),
        lax.psum_scatter(grad_gain_two, ("dp", "blk"), scatter_dimension=0, tiled=True),
        lax.psum_scatter(grad_shift_two, ("dp", "blk"), scatter_dimension=0, tiled=True),
    )
    return (layer_out, tokens_grad) + tuple(shares)


def dot_f32(left, right, dims):
    return lax.dot_general(left, right, (dims, ((), ())), preferred_element_type=jnp.float32)


NT = ((1,), (1,))
NN = ((1,), (0,))


def split_three(values):
    high = values.astype(jnp.bfloat16).astype(jnp.float32)
    rest = values - high
    mid = rest.astype(jnp.bfloat16).astype(jnp.float32)
    return high, mid, rest - mid


def spread_three(lane, base, values, into):
    for step, part in enumerate(split_three(values)):
        into = jnp.where(lane == base + step, part, into)
    return into


def fill_keys(info_ref, keys, values, key_aug, value_aug, value_fill, chunk):
    length = keys.shape[0]
    lane = lax.broadcasted_iota(jnp.int32, (chunk, LANES), 1)
    row = lax.broadcasted_iota(jnp.int32, (chunk, LANES), 0)
    for part in range(length // chunk):
        at = slice(part * chunk, (part + 1) * chunk)
        off = (lane == 3) & (row + info_ref[1 + part] >= info_ref[0])
        mask = jnp.where(off, MASKED, 0.0)
        for one in range(PER_TILE):
            mine = lane // (LANES // PER_TILE) == one
            base = 4 * one
            minus = (lane >= base) & (lane < base + 3)
            key_aug[one, at, :LANES] = jnp.where(mine, keys[at], jnp.zeros((), keys.dtype))
            key_aug[one, at, LANES:] = jnp.where(minus, -1.0, mask).astype(jnp.bfloat16)
            value_aug[one, at, :LANES] = jnp.where(mine, values[at], jnp.zeros((), keys.dtype))
            if value_fill:
                value_aug[one, at, LANES:] = jnp.ones((chunk, LANES), jnp.bfloat16)
            else:
                value_aug[one, at, LANES:] = jnp.where(minus, -1.0, 0.0).astype(jnp.bfloat16)


def attend_kernel(span, info_ref, query_ref, key_ref, value_ref, out_ref, aux_ref, key_aug, value_aug):
    length = key_ref.shape[0]
    tile = query_ref.shape[0]
    lane = lax.broadcasted_iota(jnp.int32, (1, LANES), 1)

    @pl.when(pl.program_id(1) == 0)
    def _():
        fill_keys(info_ref, key_ref, value_ref, key_aug, value_aug, True, length // 8)

    one_lane = jnp.where(lane == 3, 1.0, 0.0)
    flag = jnp.broadcast_to(one_lane.astype(jnp.bfloat16), (tile, LANES))
    query = jnp.concatenate([query_ref[...], flag], axis=1)
    pieces = [slice(at, at + span) for at in range(0, length, span)]
    scores, peaks = [], []
    for one in range(PER_TILE):
        peak = None
        row = []
        for at in pieces:
            score = dot_f32(query, key_aug[one, at], NT)
            row.append(score)
            for low in range(0, span, LANES):
                part = score[:, low : low + LANES]
                peak = part if peak is None else jnp.maximum(peak, part)
        scores.append(row)
        peaks.append(jnp.max(peak, axis=1, keepdims=True))
    out = None
    aux = one_lane
    for one in range(PER_TILE):
        total = None
        for at, score in zip(pieces, scores[one]):
            expo = jnp.exp2((score - peaks[one]) * SCORE_SCALE).astype(jnp.bfloat16)
            part = dot_f32(expo, value_aug[one, at], NN)
            total = part if total is None else total + part
        weight = total[:, LANES:]
        part = total[:, :LANES] / weight
        out = part if out is None else out + part
        log_total = jnp.log2(weight) * (1.0 / SCORE_SCALE) + peaks[one]
        aux = spread_three(lane, 4 * one, log_total, aux)
    out_ref[...] = out
    aux_ref[...] = aux.astype(jnp.bfloat16)


def attend(qkv, info, tile, span):
    length, width = qkv.shape[0], qkv.shape[1] // 3
    tiles = width // LANES
    query_spec = pl.BlockSpec((tile, LANES), lambda pair, at: (at, pair))
    return pl.pallas_call(
        functools.partial(attend_kernel, span),
        grid=(tiles, length // tile),
        in_specs=[
            pl.BlockSpec(memory_space=pltpu.SMEM),
            query_spec,
            pl.BlockSpec((length, LANES), lambda pair, at: (0, tiles + pair)),
            pl.BlockSpec((length, LANES), lambda pair, at: (0, 2 * tiles + pair)),
        ],
        out_specs=[query_spec, query_spec],
        out_shape=[
            jax.ShapeDtypeStruct((length, width), jnp.float32),
            jax.ShapeDtypeStruct((length, width), jnp.bfloat16),
        ],
        scratch_shapes=[pltpu.VMEM((PER_TILE, length, 2 * LANES), jnp.bfloat16)] * 2,
        compiler_params=pltpu.CompilerParams(vmem_limit_bytes=VMEM_LIMIT),
        cost_estimate=pl.CostEstimate(
            flops=16 * length * length * width,
            bytes_accessed=12 * length * width,
            transcendentals=length * length * width // 64,
        ),
        name="attend",
    )(info, qkv, qkv, qkv)


def attend_back_kernel(
    span, info_ref, query_ref, key_ref, value_ref, grad_ref, out_ref, aux_ref,
    query_grad_ref, key_grad_ref, value_grad_ref, key_aug, value_aug, key_cols, key_sum, value_sum,
):
    length = key_ref.shape[0]
    tile = query_ref.shape[0]
    wide = LANES // PER_TILE
    lane = lax.broadcasted_iota(jnp.int32, (1, LANES), 1)

    @pl.when(pl.program_id(1) == 0)
    def _():
        fill_keys(info_ref, key_ref, value_ref, key_aug, value_aug, False, length // 8)
        key_cols[...] = key_ref[...].T
        key_sum[...] = jnp.zeros_like(key_sum)
        value_sum[...] = jnp.zeros_like(value_sum)

    plain, grad = query_ref[...], grad_ref[...]
    query = jnp.concatenate([plain, aux_ref[...]], axis=1)
    product = grad.astype(jnp.float32) * out_ref[...]
    delta = jnp.zeros((tile, LANES), jnp.float32)
    for one in range(PER_TILE):
        own = jnp.sum(jnp.where(lane // wide == one, product, 0.0), axis=1, keepdims=True)
        delta = spread_three(lane, 4 * one, own, delta)
    grad_aug = jnp.concatenate([grad, delta.astype(jnp.bfloat16)], axis=1)
    nothing = jnp.zeros((), plain.dtype)
    query_rows = []
    for one in range(PER_TILE):
        mine = lane // wide == one
        query_own = jnp.where(mine, plain, nothing)
        grad_own = jnp.where(mine, grad, nothing)
        total = None
        for low in range(0, length, span):
            at = slice(low, low + span)
            score = dot_f32(key_aug[one, at], query, NT)
            grad_probs = dot_f32(value_aug[one, at], grad_aug, NT)
            probs = jnp.exp2(score * SCORE_SCALE)
            grad_scores = (probs * grad_probs).astype(jnp.bfloat16)
            value_sum[at] += dot_f32(probs.astype(jnp.bfloat16), grad_own, NN)
            key_sum[at] += dot_f32(grad_scores, query_own, NN)
            part = dot_f32(key_cols[wide * one : wide * (one + 1), at], grad_scores, NN)
            total = part if total is None else total + part
        query_rows.append(total)
    query_grad_ref[...] = (jnp.concatenate(query_rows, axis=0).T * 0.125).astype(jnp.bfloat16)

    @pl.when(pl.program_id(1) == pl.num_programs(1) - 1)
    def _():
        key_grad_ref[...] = (key_sum[...] * 0.125).astype(jnp.bfloat16)
        value_grad_ref[...] = value_sum[...].astype(jnp.bfloat16)


def attend_back(qkv, grad, out, aux, info, tile, span):
    length, width = qkv.shape[0], qkv.shape[1] // 3
    tiles = width // LANES
    query_spec = pl.BlockSpec((tile, LANES), lambda pair, at: (at, pair))
    whole = pl.BlockSpec((length, LANES), lambda pair, at: (0, pair))
    result = jax.ShapeDtypeStruct((length, width), jnp.bfloat16)
    return pl.pallas_call(
        functools.partial(attend_back_kernel, span),
        grid=(tiles, length // tile),
        in_specs=[
            pl.BlockSpec(memory_space=pltpu.SMEM),
            query_spec,
            pl.BlockSpec((length, LANES), lambda pair, at: (0, tiles + pair)),
            pl.BlockSpec((length, LANES), lambda pair, at: (0, 2 * tiles + pair)),
            query_spec,
            query_spec,
            query_spec,
        ],
        out_specs=[query_spec, whole, whole],
        out_shape=[result] * 3,
        scratch_shapes=[pltpu.VMEM((PER_TILE, length, 2 * LANES), jnp.bfloat16)] * 2
        + [pltpu.VMEM((LANES, length), jnp.bfloat16)]
        + [pltpu.VMEM((length, LANES), jnp.float32)] * 2,
        compiler_params=pltpu.CompilerParams(vmem_limit_bytes=VMEM_LIMIT),
        cost_estimate=pl.CostEstimate(
            flops=40 * length * length * width,
            bytes_accessed=22 * length * width,
            transcendentals=length * length * width // 64,
        ),
        name="attend_back",
    )(info, qkv, qkv, qkv, grad, out, aux)


def pack_kernel(query_ref, key_ref, value_ref, output_ref, up_ref, down_ref, small_ref, first_ref, second_ref):
    share, width = query_ref.shape
    fold = up_ref.shape[1] // width
    first_ref[0] = query_ref[...]
    first_ref[1] = key_ref[...]
    first_ref[2] = value_ref[...]
    first_ref[3, :, :LANES] = small_ref[...]
    first_ref[3, :, LANES:] = jnp.zeros((share, width - LANES), first_ref.dtype)
    second_ref[0] = output_ref[...]
    for at in range(fold):
        second_ref[1 + at] = up_ref[:, at * width : (at + 1) * width]
        second_ref[1 + fold + at] = down_ref[at * share : (at + 1) * share, :]


def pack(matrices, small):
    share, width = matrices[0].shape
    fold = matrices[4].shape[1] // width
    return pl.pallas_call(
        pack_kernel,
        out_shape=[
            jax.ShapeDtypeStruct((4, share, width), jnp.bfloat16),
            jax.ShapeDtypeStruct((1 + 2 * fold, share, width), jnp.bfloat16),
        ],
        compiler_params=pltpu.CompilerParams(vmem_limit_bytes=8 << 20),
        name="pack",
    )(*matrices, small)


def unspread(pieces, width, share):
    lane = lax.broadcasted_iota(jnp.int32, (LANES, width), 1)
    row = lax.broadcasted_iota(jnp.int32, (LANES, width), 0)
    pick = jnp.where(lax.rem(lane, share) == row, 1.0, 0.0).astype(jnp.bfloat16)
    spread = dot_f32(pieces, pick, NN)
    lane = lax.broadcasted_iota(jnp.int32, (pieces.shape[0], width), 1)
    row = lax.broadcasted_iota(jnp.int32, (pieces.shape[0], width), 0)
    return jnp.sum(jnp.where(lax.div(lane, share) == row, spread, 0.0), axis=0, keepdims=True)


def project_kernel(core_ref, tokens_ref, query_ref, key_ref, value_ref, small_ref, out_ref, bias_ref):
    devices, _, share, cols = query_ref.shape
    width = devices * share

    @pl.when(pl.program_id(0) == 0)
    def _():
        for at, entry in ((0, 7), (1, 8)):
            whole = unspread(small_ref[:, 0, entry, :LANES], width, share)
            bias_ref[at : at + 1, :] = jnp.where(
                core_ref[0] == 0, whole[:, :cols], whole[:, cols:]
            )

    tokens = tokens_ref[...]
    for at, (ref, bias) in enumerate(((query_ref, 0), (key_ref, None), (value_ref, 1))):
        part = dot_f32(tokens, ref[...].reshape(width, cols), NN)
        if bias is not None:
            part = part + bias_ref[bias : bias + 1, :]
        out_ref[:, at * cols : (at + 1) * cols] = part.astype(out_ref.dtype)


def weight_columns(first, unit):
    devices, _, share, width = first.shape
    return pl.BlockSpec((devices, 1, share, width // 2), lambda at, core: (0, unit, 0, core[0]))


def project(core, sequence, first, tile):
    length, width = sequence.shape
    devices, _, share, _ = first.shape
    cols = width // 2
    return pl.pallas_call(
        project_kernel,
        grid_spec=pltpu.PrefetchScalarGridSpec(
            num_scalar_prefetch=1,
            grid=(length // tile,),
            in_specs=[pl.BlockSpec((tile, width), lambda at, core: (at, 0))]
            + [weight_columns(first, unit) for unit in range(3)]
            + [pl.BlockSpec((devices, 1, share, width), lambda at, core: (0, 3, 0, 0))],
            out_specs=pl.BlockSpec((tile, 3 * cols), lambda at, core: (at, 0)),
            scratch_shapes=[pltpu.VMEM((8, cols), jnp.float32)],
        ),
        out_shape=jax.ShapeDtypeStruct((length, 3 * cols), jnp.bfloat16),
        compiler_params=pltpu.CompilerParams(vmem_limit_bytes=VMEM_LIMIT),
        cost_estimate=pl.CostEstimate(
            flops=6 * length * width * cols, bytes_accessed=10 * length * width, transcendentals=0
        ),
        name="project",
    )(core, sequence, first, first, first, first)


def norm(values, gain, shift):
    center = jnp.mean(values, axis=1, keepdims=True)
    offset = values - center
    scale = lax.rsqrt(jnp.mean(offset * offset, axis=1, keepdims=True) + 1e-12)
    unit = offset * scale
    return unit * gain + shift, unit, scale


def norm_back(grad, gain, unit, scale):
    inner = grad * gain
    mean = jnp.mean(inner, axis=1, keepdims=True)
    return scale * (inner - mean - unit * jnp.mean(inner * unit, axis=1, keepdims=True))


def feed_kernel(
    context_ref, tokens_ref, cotangent_ref, small_ref, weights_ref,
    out_ref, active_ref, grad_down_ref, grad_up_ref, hidden_ref, res_ref, attended_ref, context_grad_ref, sum_ref,
    weight_ref, vector_ref, slope_ref, sems,
):
    devices, _, share, width = weights_ref.shape
    fold = active_ref.shape[1] // width
    group = devices // fold
    step = pl.program_id(0)
    f32, bf16 = jnp.float32, jnp.bfloat16

    def copy(unit):
        if unit <= fold:
            return pltpu.make_async_copy(weights_ref.at[:, unit], weight_ref.at[unit], sems.at[unit])
        first = group * (unit - 1 - fold)
        return pltpu.make_async_copy(
            weights_ref.at[pl.ds(first, group), pl.ds(1 + fold, fold)],
            weight_ref.at[unit].reshape(group, fold, share, width),
            sems.at[unit],
        )

    @pl.when(step == 0)
    def _():
        for unit in range(1 + 2 * fold):
            copy(unit).start()
        sum_ref[...] = jnp.zeros_like(sum_ref)
        for entry in range(7):
            spread, wide = (fold * share, fold * width) if entry == 1 else (share, width)
            vector_ref[entry : entry + 1, :wide] = unspread(
                small_ref[:, 0, entry, :LANES], wide, spread
            )

    def ready(unit):
        @pl.when(step == 0)
        def _():
            copy(unit).wait()

    def weight(unit):
        return weight_ref[unit].reshape(width, width)

    def vector(entry, low=0):
        return vector_ref[entry : entry + 1, low : low + width]

    def add_sum(entry, value):
        sum_ref[entry : entry + 1, :] += jnp.sum(value, axis=0, keepdims=True)

    ready(0)
    attended = dot_f32(context_ref[...], weight(0), NN) + vector(0)
    hidden, unit_one, scale_one = norm(tokens_ref[...].astype(f32) + attended, vector(3), vector(4))
    hidden_low = hidden.astype(bf16)
    hidden_ref[...] = hidden_low
    down = vector(2)
    for at in range(fold):
        low = at * width
        ready(1 + at)
        up = dot_f32(hidden_low, weight(1 + at), NN) + vector(1, low)
        square = up * up
        tanh = jnp.tanh(0.7978845608 * up * (1.0 + 0.044715 * square))
        half = 0.5 * (1.0 + tanh)
        active = (up * half).astype(bf16)
        rise = (0.5 * 0.7978845608) * up * (1.0 - tanh * tanh)
        slope_ref[at] = half + rise * (1.0 + (3 * 0.044715) * square)
        active_ref[:, low : low + width] = active
        ready(1 + fold + at)
        down = down + dot_f32(active, weight(1 + fold + at), NN)
    out, unit_two, scale_two = norm(hidden + down, vector(5), vector(6))
    out_ref[...] = out.astype(bf16)
    cotangent = cotangent_ref[...].astype(f32)
    add_sum(4, cotangent * unit_two)
    add_sum(5, cotangent)
    grad = norm_back(cotangent, vector(5), unit_two, scale_two)
    grad_down = grad.astype(bf16)
    grad_down_ref[...] = grad_down
    add_sum(1, grad_down.astype(f32))
    for at in range(fold):
        low = at * width
        grad_active = dot_f32(grad_down, weight(1 + fold + at), NT)
        grad_up = (grad_active * slope_ref[at]).astype(bf16)
        grad_up_ref[:, low : low + width] = grad_up
        add_sum(6 + at, grad_up.astype(f32))
        grad = grad + dot_f32(grad_up, weight(1 + at), NT)
    add_sum(2, grad * unit_one)
    add_sum(3, grad)
    res_one = norm_back(grad, vector(3), unit_one, scale_one)
    res_ref[...] = res_one
    grad_attended = res_one.astype(bf16)
    attended_ref[...] = grad_attended
    add_sum(0, grad_attended.astype(f32))
    context_grad_ref[...] = dot_f32(grad_attended, weight(0), NT).astype(bf16)


def feed(context, tokens, cotangent, first, second, tile):
    rows, width = context.shape
    devices, units, share, _ = second.shape
    fold = (units - 1) // 2
    thin = pl.BlockSpec((tile, width), lambda at: (at, 0))
    wide = pl.BlockSpec((tile, fold * width), lambda at: (at, 0))
    sums = (6 + fold + 7) // 8 * 8

    def like(columns, dtype):
        return jax.ShapeDtypeStruct((rows, columns), dtype)

    bf16, f32 = jnp.bfloat16, jnp.float32
    return pl.pallas_call(
        feed_kernel,
        grid=(rows // tile,),
        in_specs=[
            thin,
            thin,
            thin,
            pl.BlockSpec((devices, 1, share, width), lambda at: (0, 3, 0, 0)),
            pl.BlockSpec(memory_space=pl.ANY),
        ],
        out_specs=[thin, wide, thin, wide, thin, thin, thin, thin, pl.BlockSpec((sums, width), lambda at: (0, 0))],
        out_shape=[
            like(width, bf16),
            like(fold * width, bf16),
            like(width, bf16),
            like(fold * width, bf16),
            like(width, bf16),
            like(width, f32),
            like(width, bf16),
            like(width, bf16),
            jax.ShapeDtypeStruct((sums, width), f32),
        ],
        scratch_shapes=[
            pltpu.VMEM((units, devices, share, width), bf16),
            pltpu.VMEM((8, fold * width), f32),
            pltpu.VMEM((fold, tile, width), f32),
            pltpu.SemaphoreType.DMA((units,)),
        ],
        compiler_params=pltpu.CompilerParams(vmem_limit_bytes=VMEM_LIMIT),
        cost_estimate=pl.CostEstimate(
            flops=4 * rows * width * width * (1 + 2 * fold),
            bytes_accessed=rows * width * (20 + 4 * fold) + 2 * units * width * width,
            transcendentals=rows * width * fold,
        ),
        name="feed",
    )(context, tokens, cotangent, first, second)


TN = ((0,), (0,))


def weight_grad_kernel(
    active_ref, grad_down_ref, hidden_ref, grad_up_ref, context_ref, attended_ref, sum_ref, out_ref, block_ref, small_ref, sems
):
    devices, units, share, width = out_ref.shape
    fold = (units - 2) // 2
    group = devices // fold
    step = pl.program_id(0)

    def block(slot):
        return block_ref.at[slot]

    def column_copy(unit, slot):
        return pltpu.make_async_copy(block(slot), out_ref.at[:, unit], sems.at[slot])

    def row_copy(at, slot):
        return pltpu.make_async_copy(
            block(slot).reshape(group, fold, share, width),
            out_ref.at[pl.ds(group * at, group), pl.ds(1 + fold, fold)],
            sems.at[slot],
        )

    def small_copy():
        return pltpu.make_async_copy(small_ref, out_ref.at[:, 1 + 2 * fold], sems.at[2])

    def store(left, right, slot):
        block_ref[slot] = dot_f32(left, right, TN).astype(out_ref.dtype).reshape(devices, share, width)

    slot = lax.rem(step, 2)

    @pl.when(step >= 2)
    def _():
        column_copy(0, slot).wait()

    @pl.when(step == 0)
    def _():
        rows = jnp.concatenate(
            [sum_ref[...], jnp.zeros((share - sum_ref.shape[0], width), jnp.float32)], axis=0
        ).astype(out_ref.dtype)
        small_ref[...] = jnp.broadcast_to(rows[None], small_ref.shape)
        small_copy().start()
        store(context_ref[...], attended_ref[...], 0)
        column_copy(0, 0).start()

    @pl.when((step >= 1) & (step <= fold))
    def _():
        store(hidden_ref[...], grad_up_ref[...], slot)
        column_copy(step, slot).start()

    @pl.when(step > fold)
    def _():
        store(active_ref[...], grad_down_ref[...], slot)
        row_copy(step - 1 - fold, slot).start()

    @pl.when(step == 2 * fold)
    def _():
        small_copy().wait()
        column_copy(0, 0).wait()
        column_copy(0, 1).wait()


def weight_grads(active, grad_down, hidden, grad_up, context, attended, sums, devices):
    rows, width = context.shape
    fold = active.shape[1] // width
    share, units = width // devices, 2 + 2 * fold
    whole = pl.BlockSpec((rows, width), lambda at: (0, 0))
    return pl.pallas_call(
        weight_grad_kernel,
        grid=(1 + 2 * fold,),
        in_specs=[
            pl.BlockSpec((rows, width), lambda at: (0, jnp.maximum(at - 1 - fold, 0))),
            whole,
            whole,
            pl.BlockSpec((rows, width), lambda at: (0, jnp.clip(at - 1, 0, fold - 1))),
            whole,
            whole,
            pl.BlockSpec(sums.shape, lambda at: (0, 0)),
        ],
        out_specs=pl.BlockSpec(memory_space=pl.ANY),
        out_shape=jax.ShapeDtypeStruct((devices, units, share, width), jnp.bfloat16),
        scratch_shapes=[
            pltpu.VMEM((2, devices, share, width), jnp.bfloat16),
            pltpu.VMEM((devices, share, width), jnp.bfloat16),
            pltpu.SemaphoreType.DMA((3,)),
        ],
        compiler_params=pltpu.CompilerParams(vmem_limit_bytes=VMEM_LIMIT),
        cost_estimate=pl.CostEstimate(
            flops=2 * rows * width * width * (1 + 2 * fold),
            bytes_accessed=2 * (rows + devices * share) * width * units,
            transcendentals=0,
        ),
        name="weight_grads",
    )(active, grad_down, hidden, grad_up, context, attended, sums)


def finish_kernel(
    core_ref, query_grad_ref, key_grad_ref, value_grad_ref, tokens_ref, query_ref, key_ref, value_ref,
    partial_ref, out_ref, sum_ref, bias_ref,
):
    devices, _, share, cols = query_ref.shape
    width = devices * share
    step = pl.program_id(0)

    @pl.when(step == 0)
    def _():
        sum_ref[...] = jnp.zeros_like(sum_ref)
        bias_ref[...] = jnp.zeros_like(bias_ref)

    tokens = tokens_ref[...]
    total = None
    for at, (grad_ref, ref) in enumerate(
        ((query_grad_ref, query_ref), (key_grad_ref, key_ref), (value_grad_ref, value_ref))
    ):
        grad = grad_ref[...]
        here = slice(at * cols, (at + 1) * cols)
        part = dot_f32(grad, ref[...].reshape(width, cols), NT)
        total = part if total is None else total + part
        sum_ref[:, here] += dot_f32(tokens, grad, TN)
        bias_ref[0:1, here] += jnp.sum(grad.astype(jnp.float32), axis=0, keepdims=True)
    partial_ref[...] = total.astype(partial_ref.dtype)

    @pl.when(step == pl.num_programs(0) - 1)
    def _():
        out_ref[:, :share, :] = sum_ref[...].astype(out_ref.dtype).reshape(devices, share, 3 * cols)
        bias = bias_ref[...].astype(out_ref.dtype)
        out_ref[:, share:, :] = jnp.broadcast_to(bias[None], (devices, 8, 3 * cols))


def finish(core, grads, sequence, first, tile):
    length, width = sequence.shape
    devices, _, share, _ = first.shape
    cols = width // 2
    thin = pl.BlockSpec((tile, cols), lambda at, core: (at, 0))
    full = pl.BlockSpec((tile, width), lambda at, core: (at, 0))
    return pl.pallas_call(
        finish_kernel,
        grid_spec=pltpu.PrefetchScalarGridSpec(
            num_scalar_prefetch=1,
            grid=(length // tile,),
            in_specs=[thin] * 3 + [full] + [weight_columns(first, unit) for unit in range(3)],
            out_specs=[full, pl.BlockSpec((devices, share + 8, 3 * cols), lambda at, core: (0, 0, 0))],
            scratch_shapes=[
                pltpu.VMEM((width, 3 * cols), jnp.float32),
                pltpu.VMEM((8, 3 * cols), jnp.float32),
            ],
        ),
        out_shape=[
            jax.ShapeDtypeStruct((length, width), jnp.bfloat16),
            jax.ShapeDtypeStruct((devices, share + 8, 3 * cols), jnp.bfloat16),
        ],
        compiler_params=pltpu.CompilerParams(vmem_limit_bytes=VMEM_LIMIT),
        cost_estimate=pl.CostEstimate(
            flops=12 * length * width * cols, bytes_accessed=10 * length * width, transcendentals=0
        ),
        name="finish",
    )(core, *grads, sequence, first, first, first)


def body(
    tokens,
    cotangent,
    lengths,
    query_weight,
    key_weight,
    value_weight,
    output_weight,
    up_weight,
    down_weight,
    query_bias,
    value_bias,
    output_bias,
    up_bias,
    down_bias,
    attn_gain,
    attn_shift,
    ffn_gain,
    ffn_shift,
):
    seqs, stretch, width = tokens.shape
    rows = seqs * stretch
    n_pair, n_core, n_blk = (lax.axis_size(axis) for axis in ALL)
    devices = n_pair * n_core * n_blk
    pair, core, blk = (lax.axis_index(axis) for axis in ALL)
    half, cols = stretch // 2, width // 2
    own_rows = n_blk * half
    share = query_weight.shape[0]
    fold = up_weight.shape[1] // width
    bf16, f32 = jnp.bfloat16, jnp.float32

    def exchange_table(step, back):
        table = []
        for pair in range(n_pair):
            for src_core in range(n_core):
                for src in range(n_blk):
                    piece = src ^ step
                    sender = (pair * n_core + src_core) * n_blk + src
                    target = (pair * n_core + piece % 2) * n_blk + seqs * src_core + piece // 2
                    table.append((target, sender) if back else (sender, target))
        return table

    def to_sequence(array):
        pieces = array.reshape(n_blk, half, array.shape[-1])
        return [
            lax.ppermute(
                lax.dynamic_index_in_dim(pieces, blk ^ step, 0, keepdims=False),
                ALL,
                exchange_table(step, False),
            )
            for step in range(n_blk)
        ]

    def from_sequence(chunks):
        got = [lax.ppermute(c, ALL, exchange_table(step, True)) for step, c in enumerate(chunks)]
        bit = 1
        while bit < n_blk:
            flip = (blk & bit) != 0
            got = [jnp.where(flip, got[at ^ bit], got[at]) for at in range(n_blk)]
            bit *= 2
        return jnp.concatenate(got, axis=0)

    def other_core(array):
        return lax.ppermute(array, "core", [(0, 1), (1, 0)])

    def columns(array, which):
        return lax.dynamic_slice_in_dim(array, which * cols, cols, axis=-1)

    def halve(array, bit, inner):
        side = (pair & bit) // bit
        array = array.reshape((-1, 2, inner) + array.shape[1:])
        kept = lax.dynamic_index_in_dim(array, side, 1, keepdims=False)
        sent = lax.dynamic_index_in_dim(array, 1 - side, 1, keepdims=False)
        got = lax.ppermute(sent, "pair", [(at, at ^ bit) for at in range(n_pair)])
        total = (kept.astype(f32) + got.astype(f32)).astype(bf16)
        return total.reshape((-1,) + total.shape[2:])

    vectors = (output_bias, up_bias, down_bias, attn_gain, attn_shift, ffn_gain, ffn_shift)
    coded = jnp.concatenate([lengths // 16, lengths % 16]).astype(bf16)
    small = [
        jnp.pad(item, (0, LANES - item.shape[0]))
        for item in vectors + (query_bias, value_bias, coded)
    ]
    small = jnp.pad(jnp.stack(small), ((0, share - len(small)), (0, 0)))
    first, second = pack(
        (query_weight, key_weight, value_weight, output_weight, up_weight, down_weight), small
    )
    first = lax.all_gather(first, ALL, axis=0)
    second = lax.all_gather(second, ALL, axis=0)
    code = first[:, 3, 9, : 2 * seqs].astype(jnp.int32)
    code = (code[:, :seqs] * 16 + code[:, seqs:]).reshape(n_pair, n_core, n_blk, seqs)[:, :, 0]
    own_length = code.reshape(n_pair, n_core * seqs)[pair, blk]
    which = jnp.reshape(core, (1,)).astype(jnp.int32)

    arrived = to_sequence(tokens)
    own_tokens = jnp.concatenate(arrived, axis=0)
    sequence = jnp.concatenate([own_tokens, other_core(own_tokens)], axis=0)
    starts = []
    for side in (core, 1 - core):
        piece = 2 * (blk % seqs) + side
        starts += [(piece ^ step) * stretch + side * half for step in range(n_blk)]
    info = jnp.stack([own_length] + starts).astype(jnp.int32)

    qkv = project(which, sequence, first, 512)
    context_seq, aux = attend(qkv, info, 512, 512)
    context_low = context_seq.astype(bf16)
    kept, crossed = context_low[:own_rows], other_core(context_low[own_rows:])
    joined = jnp.concatenate(
        [jnp.where(core == 0, kept, crossed), jnp.where(core == 0, crossed, kept)], axis=1
    )
    context = from_sequence([joined[at : at + half] for at in range(0, own_rows, half)])

    layer_out, active, grad_down, grad_up, hidden, grad_res, grad_attended, grad_context, sums = feed(
        context, tokens.reshape(rows, width), cotangent.reshape(rows, width), first, second, 256
    )
    own_grad = jnp.concatenate(to_sequence(grad_context), axis=0)
    context_grad = jnp.concatenate(
        [columns(own_grad, core), other_core(columns(own_grad, 1 - core))], axis=0
    )

    second_grads = weight_grads(
        active, grad_down, hidden, grad_up, context, grad_attended, sums, devices
    )
    context_grad, second_grads = lax.optimization_barrier((context_grad, second_grads))
    second_grads = lax.psum_scatter(second_grads, ALL, scatter_dimension=0)

    grads = attend_back(qkv, context_grad, context_seq, aux, info, 512, 512)
    partial, first_grads = finish(which, grads, sequence, first, 512)
    crossed = other_core(partial[own_rows:])
    summed = (partial[:own_rows].astype(f32) + crossed.astype(f32)).astype(bf16)
    returned = from_sequence([summed[at : at + half] for at in range(0, own_rows, half)])
    tokens_grad = (grad_res + returned.astype(f32)).reshape(seqs, stretch, width)

    first_grads = first_grads.reshape(n_pair, n_core, n_blk, share + 8, 3 * cols)
    bits = [1 << at for at in range(n_pair.bit_length() - 1)]
    sides = []
    for side in range(n_core):
        part = first_grads[:, side]
        for bit in bits if side else bits[::-1]:
            part = halve(part, bit, 1 if side else bit)
        sides.append(part.reshape(n_blk, share + 8, 3 * cols))
    part = jnp.stack(sides, axis=1)
    total = lax.dynamic_index_in_dim(part, blk, 0, keepdims=False).astype(f32)
    for step in range(1, n_blk):
        sent = lax.dynamic_index_in_dim(part, blk ^ step, 0, keepdims=False)
        total += lax.ppermute(sent, "blk", [(at, at ^ step) for at in range(n_blk)]).astype(f32)
    total = total.astype(bf16)
    kept = lax.dynamic_index_in_dim(total, core, 0, keepdims=False)
    crossed = other_core(lax.dynamic_index_in_dim(total, 1 - core, 0, keepdims=False))
    left = jnp.where(core == 0, kept, crossed).astype(f32)
    right = jnp.where(core == 0, crossed, kept).astype(f32)
    projections = [
        jnp.concatenate([left[:, at : at + cols], right[:, at : at + cols]], axis=1)
        for at in range(0, 3 * cols, cols)
    ]
    device = (pair * n_core + core) * n_blk + blk

    def own_part(line, size):
        return lax.dynamic_slice_in_dim(line, device * size, size, axis=-1)

    second_grads = second_grads.astype(f32)
    lines = second_grads[1 + 2 * fold]
    own_lines = own_part(lines[:6], share)
    return (
        (layer_out.reshape(seqs, stretch, width), tokens_grad)
        + tuple(item[:share] for item in projections)
        + (
            second_grads[0],
            jnp.concatenate([second_grads[1 + at] for at in range(fold)], axis=1),
            second_grads[1 + fold : 1 + 2 * fold].reshape(fold * share, width),
        )
        + (own_part(projections[0][share], share), own_part(projections[2][share], share))
        + (own_lines[0], own_part(lines[6 : 6 + fold].reshape(-1), fold * share), own_lines[1])
        + (own_lines[2], own_lines[3], own_lines[4], own_lines[5])
    )


def fits(mesh, tokens, up_weight):
    n_dp, n_blk = mesh.shape["dp"], mesh.shape["blk"]
    batch, length, width = tokens.shape
    if n_dp % 2 or n_dp & (n_dp - 1) or batch % n_dp or 2 * (batch // n_dp) != n_blk or n_blk & (n_blk - 1):
        return False
    share = width // (n_dp * n_blk)
    fold = up_weight.shape[1] // width
    return (
        width == HEADS * 64
        and width % (4 * LANES // PER_TILE) == 0
        and up_weight.shape[1] == fold * width
        and share * n_dp * n_blk == width
        and share % 8 == 0
        and 16 <= share
        and fold * share <= LANES
        and (6 + fold) * share <= width
        and length % (16 * n_blk) == 0
        and length % 512 == 0
        and length <= 4096
    )


def solution(mesh):
    n_dp, n_blk = mesh.shape["dp"], mesh.shape["blk"]

    def step(*args):
        spread = ("dp", "blk")
        one, use = ring_body, mesh
        where = {"dp": "dp", "blk": "blk", spread: spread}
        if fits(mesh, args[0], args[7]):
            one, use = body, Mesh(mesh.devices.reshape(n_dp // 2, 2, n_blk), ALL)
            where = {"dp": ("pair", "core"), "blk": "blk", spread: ALL}
        block = P(where["dp"], where["blk"], None)
        matrix = P(where[spread], None)
        vector = P(where[spread])
        return jax.shard_map(
            one,
            mesh=use,
            in_specs=(block, block, P(where["dp"])) + (matrix,) * 6 + (vector,) * 9,
            out_specs=(block, block) + (matrix,) * 6 + (vector,) * 9,
            check_vma=False,
        )(*args)

    return step
```

```python
import functools

import jax
import jax.numpy as jnp
from jax import lax
from jax.experimental import pallas as pl
from jax.experimental.pallas import tpu as pltpu
from jax.sharding import Mesh
from jax.sharding import PartitionSpec as P

HEADS = 12
LANES = 128
PER_TILE = 2
SCORE_SCALE = 0.125 * 1.4426950408889634
MASKED = -1e30
ALL = ("pair", "core", "blk")
VMEM_LIMIT = 56 << 20


def shifted(array, axis, by):
    length = lax.axis_size(axis)
    return lax.ppermute(array, axis, [(i, (i + by) % length) for i in range(length)])


def matmul(left, right):
    return jnp.dot(left, right, preferred_element_type=jnp.float32)


def times_trans(left, right):
    return lax.dot_general(
        left, right, (((1,), (1,)), ((), ())), preferred_element_type=jnp.float32
    )


def trans_times(left, right):
    return lax.dot_general(
        left, right, (((0,), (0,)), ((), ())), preferred_element_type=jnp.float32
    )


def layer_norm(values, gain, shift):
    center = jnp.mean(values, axis=-1, keepdims=True)
    offset = values - center
    spread = jnp.mean(offset * offset, axis=-1, keepdims=True)
    return offset * lax.rsqrt(spread + 1e-12) * gain + shift


def gelu_tanh(values):
    return jax.nn.gelu(values, approximate=True)


def ring_body(
    tokens,
    cotangent,
    lengths,
    query_weight,
    key_weight,
    value_weight,
    output_weight,
    up_weight,
    down_weight,
    query_bias,
    value_bias,
    output_bias,
    up_bias,
    down_bias,
    attn_gain,
    attn_shift,
    ffn_gain,
    ffn_shift,
):
    seqs, stretch, width = tokens.shape
    rows = seqs * stretch
    heads = HEADS
    head = width // heads
    gathered = (
        lax.all_gather(query_weight, ("dp", "blk"), axis=0, tiled=True),
        lax.all_gather(key_weight, ("dp", "blk"), axis=0, tiled=True),
        lax.all_gather(value_weight, ("dp", "blk"), axis=0, tiled=True),
        lax.all_gather(output_weight, ("dp", "blk"), axis=0, tiled=True),
        lax.all_gather(up_weight, ("dp", "blk"), axis=0, tiled=True),
        lax.all_gather(down_weight, ("dp", "blk"), axis=0, tiled=True),
        lax.all_gather(query_bias, ("dp", "blk"), axis=0, tiled=True),
        lax.all_gather(value_bias, ("dp", "blk"), axis=0, tiled=True),
        lax.all_gather(output_bias, ("dp", "blk"), axis=0, tiled=True),
        lax.all_gather(up_bias, ("dp", "blk"), axis=0, tiled=True),
        lax.all_gather(down_bias, ("dp", "blk"), axis=0, tiled=True),
        lax.all_gather(attn_gain, ("dp", "blk"), axis=0, tiled=True),
        lax.all_gather(attn_shift, ("dp", "blk"), axis=0, tiled=True),
        lax.all_gather(ffn_gain, ("dp", "blk"), axis=0, tiled=True),
        lax.all_gather(ffn_shift, ("dp", "blk"), axis=0, tiled=True),
    )
    query_full, key_full, value_full, output_full, upper_full, lower_full = gathered[:6]
    (
        bias_query,
        bias_value,
        bias_output,
        bias_upper,
        bias_lower,
        gain_one,
        shift_one,
        gain_two,
        shift_two,
    ) = [item.astype(jnp.float32) for item in gathered[6:]]
    flat = tokens.reshape(rows, width)
    queries = (matmul(flat, query_full) + bias_query).astype(jnp.bfloat16)
    keys_own = matmul(flat, key_full).astype(jnp.bfloat16)
    values_own = (matmul(flat, value_full) + bias_value).astype(jnp.bfloat16)
    query_heads = queries.reshape(seqs, stretch, heads, head)
    own_block = lax.axis_index("blk")
    cycle_size = lax.axis_size("blk")
    start = jnp.int32(0)
    key_piece = lax.all_gather(keys_own.reshape(seqs, stretch, width), "blk", axis=1, tiled=True)
    value_piece = lax.all_gather(
        values_own.reshape(seqs, stretch, width), "blk", axis=1, tiled=True
    )
    count = key_piece.shape[1]
    span = min(count, stretch)
    row_max = jnp.full((seqs, stretch, heads), -1e30, jnp.float32)
    row_total = jnp.zeros((seqs, stretch, heads), jnp.float32)
    accum = jnp.zeros((seqs, stretch, heads, head), jnp.float32)
    for part_no in range(count // span):
        key_heads = key_piece[:, part_no * span : (part_no + 1) * span].reshape(
            seqs, span, heads, head
        )
        value_heads = value_piece[:, part_no * span : (part_no + 1) * span].reshape(
            seqs, span, heads, head
        )
        positions = start + part_no * span + jnp.arange(span, dtype=jnp.int32)
        valid = positions[None, :] < lengths[:, None]
        scores = (
            jnp.einsum(
                "sqhd,skhd->sqhk", query_heads, key_heads, preferred_element_type=jnp.float32
            )
            * 0.125
        )
        scores = jnp.where(valid[:, None, None, :], scores, -jnp.inf)
        new_max = jnp.maximum(row_max, jnp.max(scores, axis=-1))
        expo = jnp.exp(scores - new_max[..., None])
        factor = jnp.exp(row_max - new_max)
        row_total = row_total * factor + jnp.sum(expo, axis=-1)
        accum = accum * factor[..., None] + jnp.einsum(
            "sqhk,skhd->sqhd",
            expo.astype(jnp.bfloat16),
            value_heads,
            preferred_element_type=jnp.float32,
        )
        row_max = new_max
    row_max, row_total, accum = (row_max, row_total, accum)
    log_total = row_max + jnp.log(row_total)
    context_full = accum / row_total[..., None]
    context = context_full.reshape(rows, width).astype(jnp.bfloat16)
    attended = matmul(context, output_full) + bias_output
    hidden, norm_one_back = jax.vjp(
        layer_norm, flat.astype(jnp.float32) + attended, gain_one, shift_one
    )
    hidden_low = hidden.astype(jnp.bfloat16)
    upward = matmul(hidden_low, upper_full) + bias_upper
    active_full, gelu_back = jax.vjp(gelu_tanh, upward)
    active = active_full.astype(jnp.bfloat16)
    downward = matmul(active, lower_full) + bias_lower
    output_full32, norm_two_back = jax.vjp(layer_norm, hidden + downward, gain_two, shift_two)
    layer_out = output_full32.astype(jnp.bfloat16).reshape(seqs, stretch, width)
    query_back, key_back, value_back, output_back, upper_back, lower_back = (
        lax.all_gather(query_weight, ("dp", "blk"), axis=0, tiled=True),
        lax.all_gather(key_weight, ("dp", "blk"), axis=0, tiled=True),
        lax.all_gather(value_weight, ("dp", "blk"), axis=0, tiled=True),
        lax.all_gather(output_weight, ("dp", "blk"), axis=0, tiled=True),
        lax.all_gather(up_weight, ("dp", "blk"), axis=0, tiled=True),
        lax.all_gather(down_weight, ("dp", "blk"), axis=0, tiled=True),
    )
    grad_outer = cotangent.reshape(rows, width).astype(jnp.float32)
    grad_res_two, grad_gain_two, grad_shift_two = norm_two_back(grad_outer)
    grad_down = grad_res_two.astype(jnp.bfloat16)
    grad_lower_bias = jnp.sum(grad_down, axis=0, dtype=jnp.float32)
    grad_lower = trans_times(active, grad_down)
    grad_active = times_trans(grad_down, lower_back)
    (grad_upward,) = gelu_back(grad_active)
    grad_up = grad_upward.astype(jnp.bfloat16)
    grad_upper_bias = jnp.sum(grad_up, axis=0, dtype=jnp.float32)
    grad_upper = trans_times(hidden_low, grad_up)
    grad_hidden = grad_res_two + times_trans(grad_up, upper_back)
    grad_res_one, grad_gain_one, grad_shift_one = norm_one_back(grad_hidden)
    grad_attended = grad_res_one.astype(jnp.bfloat16)
    grad_output_bias = jnp.sum(grad_attended, axis=0, dtype=jnp.float32)
    grad_output = trans_times(context, grad_attended)
    grad_context = times_trans(grad_attended, output_back).astype(jnp.bfloat16)
    context_grad_heads = grad_context.reshape(seqs, stretch, heads, head)
    delta = jnp.sum(context_grad_heads.astype(jnp.float32) * context_full, axis=-1)

    def contribute(key_value, source, pair_grad, query_grad):
        key_heads = key_value[0]
        value_heads = key_value[1]
        positions = source * stretch + jnp.arange(stretch, dtype=jnp.int32)
        valid = positions[None, :] < lengths[:, None]
        scores = (
            jnp.einsum(
                "sqhd,skhd->sqhk", query_heads, key_heads, preferred_element_type=jnp.float32
            )
            * 0.125
        )
        probs = jnp.where(valid[:, None, None, :], jnp.exp(scores - log_total[..., None]), 0.0)
        grad_probs = jnp.einsum(
            "sqhd,skhd->sqhk", context_grad_heads, value_heads, preferred_element_type=jnp.float32
        )
        grad_scores = (probs * (grad_probs - delta[..., None])).astype(jnp.bfloat16)
        query_grad = (
            query_grad
            + jnp.einsum(
                "sqhk,skhd->sqhd", grad_scores, key_heads, preferred_element_type=jnp.float32
            )
            * 0.125
        )
        key_part = (
            jnp.einsum(
                "sqhk,sqhd->skhd", grad_scores, query_heads, preferred_element_type=jnp.float32
            )
            * 0.125
        )
        value_part = jnp.einsum(
            "sqhk,sqhd->skhd",
            probs.astype(jnp.bfloat16),
            context_grad_heads,
            preferred_element_type=jnp.float32,
        )
        pair_grad = pair_grad + jnp.stack([key_part, value_part])
        return (pair_grad, query_grad)

    def rotate_grads(pair_grad):
        return shifted(pair_grad.astype(jnp.bfloat16), "blk", 1).astype(pair_grad.dtype)

    key_value_own = jnp.stack(
        [
            keys_own.reshape(seqs, stretch, heads, head),
            values_own.reshape(seqs, stretch, heads, head),
        ]
    )
    pair_grad, query_grad = contribute(
        key_value_own,
        own_block,
        jnp.zeros((2, seqs, stretch, heads, head), jnp.float32),
        jnp.zeros((seqs, stretch, heads, head), jnp.float32),
    )

    def cycle_turn(turn, state):
        key_value_now, pair_now, query_now = state
        key_value_now = shifted(key_value_now, "blk", 1)
        pair_now = rotate_grads(pair_now)
        source = (own_block - turn) % cycle_size
        pair_now, query_now = contribute(key_value_now, source, pair_now, query_now)
        return (key_value_now, pair_now, query_now)

    final_state = lax.fori_loop(1, cycle_size, cycle_turn, (key_value_own, pair_grad, query_grad))
    pair_home = rotate_grads(final_state[1])
    grad_queries = final_state[2].reshape(rows, width).astype(jnp.bfloat16)
    grad_keys = pair_home[0].reshape(rows, width).astype(jnp.bfloat16)
    grad_values = pair_home[1].reshape(rows, width).astype(jnp.bfloat16)
    grad_query = trans_times(flat, grad_queries)
    grad_key = trans_times(flat, grad_keys)
    grad_value = trans_times(flat, grad_values)
    grad_query_bias = jnp.sum(grad_queries, axis=0, dtype=jnp.float32)
    grad_value_bias = jnp.sum(grad_values, axis=0, dtype=jnp.float32)
    tokens_grad = (
        grad_res_one
        + times_trans(grad_queries, query_back)
        + times_trans(grad_keys, key_back)
        + times_trans(grad_values, value_back)
    ).reshape(seqs, stretch, width)
    shares = (
        lax.psum_scatter(grad_query, ("dp", "blk"), scatter_dimension=0, tiled=True),
        lax.psum_scatter(grad_key, ("dp", "blk"), scatter_dimension=0, tiled=True),
        lax.psum_scatter(grad_value, ("dp", "blk"), scatter_dimension=0, tiled=True),
        lax.psum_scatter(grad_output, ("dp", "blk"), scatter_dimension=0, tiled=True),
        lax.psum_scatter(grad_upper, ("dp", "blk"), scatter_dimension=0, tiled=True),
        lax.psum_scatter(grad_lower, ("dp", "blk"), scatter_dimension=0, tiled=True),
        lax.psum_scatter(grad_query_bias, ("dp", "blk"), scatter_dimension=0, tiled=True),
        lax.psum_scatter(grad_value_bias, ("dp", "blk"), scatter_dimension=0, tiled=True),
        lax.psum_scatter(grad_output_bias, ("dp", "blk"), scatter_dimension=0, tiled=True),
        lax.psum_scatter(grad_upper_bias, ("dp", "blk"), scatter_dimension=0, tiled=True),
        lax.psum_scatter(grad_lower_bias, ("dp", "blk"), scatter_dimension=0, tiled=True),
        lax.psum_scatter(grad_gain_one, ("dp", "blk"), scatter_dimension=0, tiled=True),
        lax.psum_scatter(grad_shift_one, ("dp", "blk"), scatter_dimension=0, tiled=True),
        lax.psum_scatter(grad_gain_two, ("dp", "blk"), scatter_dimension=0, tiled=True),
        lax.psum_scatter(grad_shift_two, ("dp", "blk"), scatter_dimension=0, tiled=True),
    )
    return (layer_out, tokens_grad) + tuple(shares)


def dot_f32(left, right, dims):
    return lax.dot_general(left, right, (dims, ((), ())), preferred_element_type=jnp.float32)


NT = ((1,), (1,))
NN = ((1,), (0,))


def split_three(values):
    high = values.astype(jnp.bfloat16).astype(jnp.float32)
    rest = values - high
    mid = rest.astype(jnp.bfloat16).astype(jnp.float32)
    return high, mid, rest - mid


def spread_three(lane, base, values, into):
    for step, part in enumerate(split_three(values)):
        into = jnp.where(lane == base + step, part, into)
    return into


def fill_keys(info_ref, keys, values, key_aug, value_aug, value_fill, chunk):
    length = keys.shape[0]
    lane = lax.broadcasted_iota(jnp.int32, (chunk, LANES), 1)
    row = lax.broadcasted_iota(jnp.int32, (chunk, LANES), 0)
    for part in range(length // chunk):
        at = slice(part * chunk, (part + 1) * chunk)
        off = (lane == 3) & (row + info_ref[1 + part] >= info_ref[0])
        mask = jnp.where(off, MASKED, 0.0)
        for one in range(PER_TILE):
            mine = lane // (LANES // PER_TILE) == one
            base = 4 * one
            minus = (lane >= base) & (lane < base + 3)
            key_aug[one, at, :LANES] = jnp.where(mine, keys[at], jnp.zeros((), keys.dtype))
            key_aug[one, at, LANES:] = jnp.where(minus, -1.0, mask).astype(jnp.bfloat16)
            value_aug[one, at, :LANES] = jnp.where(mine, values[at], jnp.zeros((), keys.dtype))
            if value_fill:
                value_aug[one, at, LANES:] = jnp.ones((chunk, LANES), jnp.bfloat16)
            else:
                value_aug[one, at, LANES:] = jnp.where(minus, -1.0, 0.0).astype(jnp.bfloat16)


def attend_kernel(
    span, info_ref, query_ref, key_ref, value_ref, low_ref, out_ref, aux_ref, key_aug, value_aug
):
    length = key_ref.shape[0]
    tile = query_ref.shape[0]
    lane = lax.broadcasted_iota(jnp.int32, (1, LANES), 1)

    @pl.when(pl.program_id(1) == 0)
    def _():
        fill_keys(info_ref, key_ref, value_ref, key_aug, value_aug, True, length // 8)

    one_lane = jnp.where(lane == 3, 1.0, 0.0)
    flag = jnp.broadcast_to(one_lane.astype(jnp.bfloat16), (tile, LANES))
    query = jnp.concatenate([query_ref[...], flag], axis=1)
    pieces = [slice(at, at + span) for at in range(0, length, span)]
    scores, peaks = [], []
    for one in range(PER_TILE):
        peak = None
        row = []
        for at in pieces:
            score = dot_f32(query, key_aug[one, at], NT)
            row.append(score)
            for low in range(0, span, LANES):
                part = score[:, low : low + LANES]
                peak = part if peak is None else jnp.maximum(peak, part)
        scores.append(row)
        peaks.append(jnp.max(peak, axis=1, keepdims=True))
    out = None
    aux = one_lane
    for one in range(PER_TILE):
        total = None
        for at, score in zip(pieces, scores[one]):
            expo = jnp.exp2((score - peaks[one]) * SCORE_SCALE).astype(jnp.bfloat16)
            part = dot_f32(expo, value_aug[one, at], NN)
            total = part if total is None else total + part
        weight = total[:, LANES:]
        part = total[:, :LANES] / weight
        out = part if out is None else out + part
        log_total = jnp.log2(weight) * (1.0 / SCORE_SCALE) + peaks[one]
        aux = spread_three(lane, 4 * one, log_total, aux)
    low_ref[...] = out.astype(jnp.bfloat16)
    out_ref[...] = out
    aux_ref[...] = aux.astype(jnp.bfloat16)


def attend(qkv, info, part, parts, tile, span):
    length, width = qkv.shape[0], qkv.shape[1] // 3
    tiles, rows = width // LANES, length // parts
    first = part * (rows // tile)
    query_spec = pl.BlockSpec((tile, LANES), lambda pair, at: (at, pair))
    return pl.pallas_call(
        functools.partial(attend_kernel, span),
        grid=(tiles, rows // tile),
        in_specs=[
            pl.BlockSpec(memory_space=pltpu.SMEM),
            pl.BlockSpec((tile, LANES), lambda pair, at: (first + at, pair)),
            pl.BlockSpec((length, LANES), lambda pair, at: (0, tiles + pair)),
            pl.BlockSpec((length, LANES), lambda pair, at: (0, 2 * tiles + pair)),
        ],
        out_specs=[query_spec] * 3,
        out_shape=[
            jax.ShapeDtypeStruct((rows, width), jnp.bfloat16),
            jax.ShapeDtypeStruct((rows, width), jnp.float32),
            jax.ShapeDtypeStruct((rows, width), jnp.bfloat16),
        ],
        scratch_shapes=[pltpu.VMEM((PER_TILE, length, 2 * LANES), jnp.bfloat16)] * 2,
        compiler_params=pltpu.CompilerParams(vmem_limit_bytes=VMEM_LIMIT),
        cost_estimate=pl.CostEstimate(
            flops=16 * rows * length * width,
            bytes_accessed=12 * length * width,
            transcendentals=rows * length * width // 64,
        ),
        name="attend",
    )(info, qkv, qkv, qkv)


def attend_back_kernel(span, per_part, info_ref, query_ref, key_ref, value_ref, *refs):
    parts = (len(refs) - 8) // 3
    groups = [refs[at * parts : (at + 1) * parts] for at in range(3)]
    query_grad_ref, key_grad_ref, value_grad_ref, key_aug, value_aug, key_cols, key_sum, value_sum = (
        refs[3 * parts :]
    )
    length = key_ref.shape[0]
    tile = query_ref.shape[0]
    wide = LANES // PER_TILE
    lane = lax.broadcasted_iota(jnp.int32, (1, LANES), 1)
    step = pl.program_id(1)

    @pl.when(step == 0)
    def _():
        fill_keys(info_ref, key_ref, value_ref, key_aug, value_aug, False, length // 8)
        key_cols[...] = key_ref[...].T
        key_sum[...] = jnp.zeros_like(key_sum)
        value_sum[...] = jnp.zeros_like(value_sum)

    grad, out, aux = (group[0][...] for group in groups)
    for part in range(1, parts):
        here = step >= part * per_part
        grad, out, aux = (
            jnp.where(here, group[part][...], item) for group, item in zip(groups, (grad, out, aux))
        )
    plain = query_ref[...]
    query = jnp.concatenate([plain, aux], axis=1)
    product = grad.astype(jnp.float32) * out
    delta = jnp.zeros((tile, LANES), jnp.float32)
    for one in range(PER_TILE):
        own = jnp.sum(jnp.where(lane // wide == one, product, 0.0), axis=1, keepdims=True)
        delta = spread_three(lane, 4 * one, own, delta)
    grad_aug = jnp.concatenate([grad, delta.astype(jnp.bfloat16)], axis=1)
    nothing = jnp.zeros((), plain.dtype)
    query_rows = []
    for one in range(PER_TILE):
        mine = lane // wide == one
        query_own = jnp.where(mine, plain, nothing)
        grad_own = jnp.where(mine, grad, nothing)
        total = None
        for low in range(0, length, span):
            at = slice(low, low + span)
            score = dot_f32(key_aug[one, at], query, NT)
            grad_probs = dot_f32(value_aug[one, at], grad_aug, NT)
            probs = jnp.exp2(score * SCORE_SCALE)
            grad_scores = (probs * grad_probs).astype(jnp.bfloat16)
            value_sum[at] += dot_f32(probs.astype(jnp.bfloat16), grad_own, NN)
            key_sum[at] += dot_f32(grad_scores, query_own, NN)
            part = dot_f32(key_cols[wide * one : wide * (one + 1), at], grad_scores, NN)
            total = part if total is None else total + part
        query_rows.append(total)
    query_grad_ref[...] = (jnp.concatenate(query_rows, axis=0).T * 0.125).astype(jnp.bfloat16)

    @pl.when(step == pl.num_programs(1) - 1)
    def _():
        key_grad_ref[...] = (key_sum[...] * 0.125).astype(jnp.bfloat16)
        value_grad_ref[...] = value_sum[...].astype(jnp.bfloat16)


def attend_back(qkv, grads, outs, auxes, info, first, count, tile, span):
    length, width = qkv.shape[0], qkv.shape[1] // 3
    tiles, parts = width // LANES, len(grads)
    per_part = length // parts // tile

    def part_spec(part):
        low = part * per_part
        return pl.BlockSpec(
            (tile, LANES), lambda pair, at: (jnp.clip(at - low, 0, per_part - 1), first + pair)
        )

    result = jax.ShapeDtypeStruct((length, count * LANES), jnp.bfloat16)
    whole = pl.BlockSpec((length, LANES), lambda pair, at: (0, pair))
    return pl.pallas_call(
        functools.partial(attend_back_kernel, span, per_part),
        grid=(count, length // tile),
        in_specs=[
            pl.BlockSpec(memory_space=pltpu.SMEM),
            pl.BlockSpec((tile, LANES), lambda pair, at: (at, first + pair)),
            pl.BlockSpec((length, LANES), lambda pair, at: (0, tiles + first + pair)),
            pl.BlockSpec((length, LANES), lambda pair, at: (0, 2 * tiles + first + pair)),
        ]
        + [part_spec(part) for part in range(parts)] * 3,
        out_specs=[pl.BlockSpec((tile, LANES), lambda pair, at: (at, pair)), whole, whole],
        out_shape=[result] * 3,
        scratch_shapes=[pltpu.VMEM((PER_TILE, length, 2 * LANES), jnp.bfloat16)] * 2
        + [pltpu.VMEM((LANES, length), jnp.bfloat16)]
        + [pltpu.VMEM((length, LANES), jnp.float32)] * 2,
        compiler_params=pltpu.CompilerParams(vmem_limit_bytes=VMEM_LIMIT),
        cost_estimate=pl.CostEstimate(
            flops=40 * count * LANES * length * length,
            bytes_accessed=22 * length * width,
            transcendentals=count * length * length * 2,
        ),
        name="attend_back",
    )(info, qkv, qkv, qkv, *grads, *outs, *auxes)


def pack_kernel(count, core_ref, *refs):
    query, key, value, output, up, down = refs[:6]
    vectors = refs[6 : 6 + count]
    mine_ref, theirs_ref, second_ref, held_ref, wide_ref = refs[6 + count : 11 + count]
    lines = refs[11 + count : 11 + 2 * count]
    sems, line_sems = refs[11 + 2 * count :]
    share, width = query.shape
    cols = width // 2
    fold = up.shape[1] // width
    copies = [
        pltpu.make_async_copy(item, held_ref.at[at], sems.at[at])
        for at, item in enumerate((query, key, value))
    ]
    copies += [
        pltpu.make_async_copy(item, line, line_sems.at[at])
        for at, (item, line) in enumerate(zip(vectors, lines))
    ]
    later = [pltpu.make_async_copy(output, second_ref.at[0], sems.at[3])]
    for at in range(fold):
        later.append(
            pltpu.make_async_copy(
                down.at[pl.ds(at * share, share)],
                second_ref.at[1 + fold + at],
                sems.at[4 + at],
            )
        )
    later.append(pltpu.make_async_copy(up, wide_ref, sems.at[4 + fold]))
    for copy in copies + later:
        copy.start()
    for copy in copies:
        copy.wait()
    first_core = core_ref[0] == 0
    for at in range(3):
        left, right = held_ref[at, :, :cols], held_ref[at, :, cols:]
        here = slice(at * share, (at + 1) * share)
        mine_ref[here] = jnp.where(first_core, left, right)
        theirs_ref[here] = jnp.where(first_core, right, left)
    for ref in (mine_ref, theirs_ref):
        ref[3 * share :] = jnp.zeros((8, cols), ref.dtype)
        for at, line in enumerate(lines):
            low = at // 8 * LANES
            ref[3 * share + at % 8, low : low + line.shape[0]] = line[...]
    for copy in later:
        copy.wait()
    for at in range(fold):
        second_ref[1 + at] = wide_ref[:, at * width : (at + 1) * width]


def pack(core, matrices, vectors):
    share, width = matrices[0].shape
    cols = width // 2
    fold = matrices[4].shape[1] // width
    count = len(vectors)
    block = jax.ShapeDtypeStruct((3 * share + 8, cols), jnp.bfloat16)
    inside = pl.BlockSpec(memory_space=pltpu.VMEM)
    return pl.pallas_call(
        functools.partial(pack_kernel, count),
        in_specs=[pl.BlockSpec(memory_space=pltpu.SMEM)]
        + [pl.BlockSpec(memory_space=pl.ANY)] * (6 + count),
        out_specs=[inside] * 3,
        out_shape=[
            block,
            block,
            jax.ShapeDtypeStruct((1 + 2 * fold, share, width), jnp.bfloat16),
        ],
        scratch_shapes=[pltpu.VMEM((3, share, width), jnp.bfloat16)]
        + [pltpu.VMEM(matrices[4].shape, jnp.bfloat16)]
        + [pltpu.VMEM(item.shape, item.dtype) for item in vectors]
        + [pltpu.SemaphoreType.DMA((5 + fold,)), pltpu.SemaphoreType.DMA((count,))],
        compiler_params=pltpu.CompilerParams(vmem_limit_bytes=VMEM_LIMIT),
        name="pack",
    )(core, *matrices, *vectors)


def unspread(gathered_ref, first_row, entry, width, share):
    low = entry // 8 * LANES
    pieces = gathered_ref[:, first_row + entry % 8, low : low + LANES]
    lane = lax.broadcasted_iota(jnp.int32, (LANES, width), 1)
    row = lax.broadcasted_iota(jnp.int32, (LANES, width), 0)
    pick = jnp.where(lax.rem(lane, share) == row, 1.0, 0.0).astype(jnp.bfloat16)
    spread = dot_f32(pieces, pick, NN)
    lane = lax.broadcasted_iota(jnp.int32, (pieces.shape[0], width), 1)
    row = lax.broadcasted_iota(jnp.int32, (pieces.shape[0], width), 0)
    return jnp.sum(jnp.where(lax.div(lane, share) == row, spread, 0.0), axis=0, keepdims=True)


def own_weight(gathered_ref, at, share):
    devices, _, cols = gathered_ref.shape
    return gathered_ref[:, at * share : (at + 1) * share, :].reshape(devices * share, cols)


def project_kernel(share, core_ref, tokens_ref, gathered_ref, out_ref, bias_ref):
    devices, _, cols = gathered_ref.shape

    @pl.when(pl.program_id(0) == 0)
    def _():
        for at in range(2):
            whole = unspread(gathered_ref, 3 * share, at, devices * share, share)
            bias_ref[at : at + 1, :] = jnp.where(
                core_ref[0] == 0, whole[:, :cols], whole[:, cols:]
            )

    tokens = tokens_ref[...]
    for at, bias in enumerate((0, None, 1)):
        part = dot_f32(tokens, own_weight(gathered_ref, at, share), NN)
        if bias is not None:
            part = part + bias_ref[bias : bias + 1, :]
        out_ref[:, at * cols : (at + 1) * cols] = part.astype(out_ref.dtype)


def project(core, sequence, gathered, tile):
    length, width = sequence.shape
    devices, _, cols = gathered.shape
    return pl.pallas_call(
        functools.partial(project_kernel, width // devices),
        grid_spec=pltpu.PrefetchScalarGridSpec(
            num_scalar_prefetch=1,
            grid=(length // tile,),
            in_specs=[
                pl.BlockSpec((tile, width), lambda at, core: (at, 0)),
                pl.BlockSpec(gathered.shape, lambda at, core: (0, 0, 0)),
            ],
            out_specs=pl.BlockSpec((tile, 3 * cols), lambda at, core: (at, 0)),
            scratch_shapes=[pltpu.VMEM((8, cols), jnp.float32)],
        ),
        out_shape=jax.ShapeDtypeStruct((length, 3 * cols), jnp.bfloat16),
        compiler_params=pltpu.CompilerParams(vmem_limit_bytes=VMEM_LIMIT),
        cost_estimate=pl.CostEstimate(
            flops=6 * length * width * cols, bytes_accessed=10 * length * width, transcendentals=0
        ),
        name="project",
    )(core, sequence, gathered)


def norm(values, gain, shift):
    center = jnp.mean(values, axis=1, keepdims=True)
    offset = values - center
    scale = lax.rsqrt(jnp.mean(offset * offset, axis=1, keepdims=True) + 1e-12)
    unit = offset * scale
    return unit * gain + shift, unit, scale


def norm_back(grad, gain, unit, scale):
    inner = grad * gain
    mean = jnp.mean(inner, axis=1, keepdims=True)
    return scale * (inner - mean - unit * jnp.mean(inner * unit, axis=1, keepdims=True))


def feed_kernel(
    kept, index_ref, context_ref, tokens_ref, cotangent_ref, small_ref, weights_ref, *refs
):
    feed_rows(context_ref, tokens_ref, cotangent_ref, small_ref, weights_ref, *refs[kept:])


def feed_rows(
    context_ref, tokens_ref, cotangent_ref, small_ref, weights_ref,
    out_ref, active_ref, grad_down_ref, grad_up_ref, hidden_ref, res_ref, attended_ref, context_grad_ref, sum_ref,
    weight_ref, vector_ref, slope_ref, sems,
):
    devices, _, share, width = weights_ref.shape
    fold = active_ref.shape[1] // width
    group = devices // fold
    step = pl.program_id(0)
    f32, bf16 = jnp.float32, jnp.bfloat16

    def copy(unit):
        if unit <= fold:
            return pltpu.make_async_copy(weights_ref.at[:, unit], weight_ref.at[unit], sems.at[unit])
        first = group * (unit - 1 - fold)
        return pltpu.make_async_copy(
            weights_ref.at[pl.ds(first, group), pl.ds(1 + fold, fold)],
            weight_ref.at[unit].reshape(group, fold, share, width),
            sems.at[unit],
        )

    @pl.when(step == 0)
    def _():
        for unit in range(1 + 2 * fold):
            copy(unit).start()
        sum_ref[...] = jnp.zeros_like(sum_ref)
        for entry in range(7):
            times = fold if entry == 1 else 1
            vector_ref[entry : entry + 1, : times * width] = unspread(
                small_ref, 0, 2 + entry, times * width, times * share
            )

    def ready(unit):
        @pl.when(step == 0)
        def _():
            copy(unit).wait()

    def weight(unit):
        return weight_ref[unit].reshape(width, width)

    def vector(entry, low=0):
        return vector_ref[entry : entry + 1, low : low + width]

    def add_sum(entry, value):
        sum_ref[entry : entry + 1, :] += jnp.sum(value, axis=0, keepdims=True)

    ready(0)
    attended = dot_f32(context_ref[...], weight(0), NN) + vector(0)
    hidden, unit_one, scale_one = norm(tokens_ref[...].astype(f32) + attended, vector(3), vector(4))
    hidden_low = hidden.astype(bf16)
    hidden_ref[...] = hidden_low
    down = vector(2)
    for at in range(fold):
        low = at * width
        ready(1 + at)
        up = dot_f32(hidden_low, weight(1 + at), NN) + vector(1, low)
        square = up * up
        tanh = jnp.tanh(0.7978845608 * up * (1.0 + 0.044715 * square))
        half = 0.5 * (1.0 + tanh)
        active = (up * half).astype(bf16)
        rise = (0.5 * 0.7978845608) * up * (1.0 - tanh * tanh)
        slope_ref[at] = half + rise * (1.0 + (3 * 0.044715) * square)
        active_ref[:, low : low + width] = active
        ready(1 + fold + at)
        down = down + dot_f32(active, weight(1 + fold + at), NN)
    out, unit_two, scale_two = norm(hidden + down, vector(5), vector(6))
    out_ref[...] = out.astype(bf16)
    cotangent = cotangent_ref[...].astype(f32)
    add_sum(4, cotangent * unit_two)
    add_sum(5, cotangent)
    grad = norm_back(cotangent, vector(5), unit_two, scale_two)
    grad_down = grad.astype(bf16)
    grad_down_ref[...] = grad_down
    add_sum(1, grad_down.astype(f32))
    for at in range(fold):
        low = at * width
        grad_active = dot_f32(grad_down, weight(1 + fold + at), NT)
        grad_up = (grad_active * slope_ref[at]).astype(bf16)
        grad_up_ref[:, low : low + width] = grad_up
        add_sum(6 + at, grad_up.astype(f32))
        grad = grad + dot_f32(grad_up, weight(1 + at), NT)
    add_sum(2, grad * unit_one)
    add_sum(3, grad)
    res_one = norm_back(grad, vector(3), unit_one, scale_one)
    res_ref[...] = res_one
    grad_attended = res_one.astype(bf16)
    attended_ref[...] = grad_attended
    add_sum(0, grad_attended.astype(f32))
    context_grad_ref[...] = dot_f32(grad_attended, weight(0), NT).astype(bf16)


def feed(index, context, tokens, cotangent, gathered, second, kept, tile):
    rows, width = context.shape
    seqs = tokens.shape[0]
    devices, units, share, _ = second.shape
    fold = (units - 1) // 2
    thin = pl.BlockSpec((tile, width), lambda at, index: (at, 0))
    placed = pl.BlockSpec((None, tile, width), lambda at, index: (index[0], at, 0))
    wide = pl.BlockSpec((tile, fold * width), lambda at, index: (at, 0))
    sums = (6 + fold + 7) // 8 * 8

    def like(columns, dtype):
        return jax.ShapeDtypeStruct((rows, columns), dtype)

    bf16, f32 = jnp.bfloat16, jnp.float32
    return pl.pallas_call(
        functools.partial(feed_kernel, len(kept)),
        grid_spec=pltpu.PrefetchScalarGridSpec(
            num_scalar_prefetch=1,
            grid=(rows // tile,),
            in_specs=[
                thin,
                placed,
                placed,
                pl.BlockSpec((devices, 8, width // 2), lambda at, index: (0, 3 * share // 8, 0)),
                pl.BlockSpec(memory_space=pl.ANY),
            ]
            + [pl.BlockSpec(memory_space=pl.ANY)] * len(kept),
            out_specs=[placed, wide, thin, wide, thin, thin, thin, thin]
            + [pl.BlockSpec((sums, width), lambda at, index: (0, 0))],
            scratch_shapes=[
                pltpu.VMEM((units, devices, share, width), bf16),
                pltpu.VMEM((8, fold * width), f32),
                pltpu.VMEM((fold, tile, width), f32),
                pltpu.SemaphoreType.DMA((units,)),
            ],
        ),
        out_shape=[
            jax.ShapeDtypeStruct((seqs, rows, width), bf16),
            like(fold * width, bf16),
            like(width, bf16),
            like(fold * width, bf16),
            like(width, bf16),
            like(width, f32),
            like(width, bf16),
            like(width, bf16),
            jax.ShapeDtypeStruct((sums, width), f32),
        ],
        input_output_aliases={6: 0} if kept else {},
        compiler_params=pltpu.CompilerParams(vmem_limit_bytes=VMEM_LIMIT),
        cost_estimate=pl.CostEstimate(
            flops=4 * rows * width * width * (1 + 2 * fold),
            bytes_accessed=rows * width * (20 + 4 * fold) + 2 * units * width * width,
            transcendentals=rows * width * fold,
        ),
        name="feed",
    )(index, context, tokens, cotangent, gathered, second, *kept)


TN = ((0,), (0,))


def up_grad_kernel(parts, core_ref, *refs):
    groups = [refs[at * parts : (at + 1) * parts] for at in range(4)]
    context, attended, hidden, grad_up = groups
    keep_ref, send_ref = refs[4 * parts :]
    n_pair, n_blk, _, share, width = keep_ref.shape

    def store(left, right):
        total = None
        for one, other in zip(left, right):
            part = dot_f32(one[...], other[...], TN)
            total = part if total is None else total + part
        total = total.astype(keep_ref.dtype).reshape(n_pair, 2, n_blk, 1, share, width)
        low, high = total[:, 0], total[:, 1]
        keep_ref[...] = jnp.where(core_ref[0] == 0, low, high)
        send_ref[...] = jnp.where(core_ref[0] == 0, high, low)

    @pl.when(pl.program_id(0) == 0)
    def _():
        store(context, attended)

    @pl.when(pl.program_id(0) > 0)
    def _():
        store(hidden, grad_up)


def up_grads(core, parts, sizes):
    n_pair, n_blk = sizes
    rows, width = parts[0][0].shape
    fold = parts[0][3].shape[1] // width
    share, units = width // (2 * n_pair * n_blk), 1 + fold
    whole = pl.BlockSpec((rows, width), lambda at, core: (0, 0))
    wide = pl.BlockSpec((rows, width), lambda at, core: (0, jnp.maximum(at - 1, 0)))
    result = jax.ShapeDtypeStruct((n_pair, n_blk, units, share, width), jnp.bfloat16)
    block = pl.BlockSpec((n_pair, n_blk, 1, share, width), lambda at, core: (0, 0, at, 0, 0))
    return pl.pallas_call(
        functools.partial(up_grad_kernel, len(parts)),
        grid_spec=pltpu.PrefetchScalarGridSpec(
            num_scalar_prefetch=1,
            grid=(units,),
            in_specs=[spec for spec in (whole, whole, whole, wide) for _ in parts],
            out_specs=[block, block],
        ),
        out_shape=[result, result],
        compiler_params=pltpu.CompilerParams(vmem_limit_bytes=VMEM_LIMIT),
        cost_estimate=pl.CostEstimate(
            flops=2 * len(parts) * rows * width * width * units,
            bytes_accessed=2 * (len(parts) * rows + width) * width * units,
            transcendentals=0,
        ),
        name="up_grads",
    )(core, *[part[at] for at in range(4) for part in parts])


def down_grad_kernel(parts, core_ref, *refs):
    groups = [refs[at * parts : (at + 1) * parts] for at in range(3)]
    active, grad_down, sums = groups
    keep_ref, send_ref = refs[3 * parts :]
    _, n_blk, units, share, width = keep_ref.shape
    fold = units - 1
    total = None
    for one, other in zip(active, grad_down):
        part = dot_f32(one[...], other[...], TN)
        total = part if total is None else total + part
    total = total.astype(keep_ref.dtype).reshape(2, n_blk, fold, share, width)
    low, high = total[0], total[1]
    keep_ref[0, :, :fold] = jnp.where(core_ref[0] == 0, low, high)
    send_ref[0, :, :fold] = jnp.where(core_ref[0] == 0, high, low)
    total = sums[0][...]
    for item in sums[1:]:
        total = total + item[...]
    pad = jnp.zeros((share - total.shape[0], width), jnp.float32)
    lines = jnp.concatenate([total, pad], axis=0).astype(keep_ref.dtype)
    lines = jnp.broadcast_to(lines[None], (n_blk, share, width))
    keep_ref[0, :, fold] = lines
    send_ref[0, :, fold] = lines


def down_grads(core, parts, sizes):
    n_pair, n_blk = sizes
    rows, width = parts[0][1].shape
    fold = parts[0][0].shape[1] // width
    share, units = width // (2 * n_pair * n_blk), 1 + fold
    result = jax.ShapeDtypeStruct((n_pair, n_blk, units, share, width), jnp.bfloat16)
    block = pl.BlockSpec((1, n_blk, units, share, width), lambda at, core: (at, 0, 0, 0, 0))
    whole = pl.BlockSpec((rows, width), lambda at, core: (0, 0))
    wide = pl.BlockSpec((rows, width), lambda at, core: (0, at))
    sums = pl.BlockSpec(parts[0][2].shape, lambda at, core: (0, 0))
    return pl.pallas_call(
        functools.partial(down_grad_kernel, len(parts)),
        grid_spec=pltpu.PrefetchScalarGridSpec(
            num_scalar_prefetch=1,
            grid=(n_pair,),
            in_specs=[spec for spec in (wide, whole, sums) for _ in parts],
            out_specs=[block, block],
        ),
        out_shape=[result, result],
        compiler_params=pltpu.CompilerParams(vmem_limit_bytes=VMEM_LIMIT),
        cost_estimate=pl.CostEstimate(
            flops=2 * len(parts) * rows * width * width * fold,
            bytes_accessed=2 * (len(parts) * rows + width) * width * units,
            transcendentals=0,
        ),
        name="down_grads",
    )(core, *[part[at] for at in range(3) for part in parts])


def own_grads_kernel(query_ref, key_ref, value_ref, tokens_ref, out_ref, sum_ref, bias_ref):
    devices, high, wide = out_ref.shape
    cols, share = wide // 3, high - 8
    step = pl.program_id(0)

    @pl.when(step == 0)
    def _():
        sum_ref[...] = jnp.zeros_like(sum_ref)
        bias_ref[...] = jnp.zeros_like(bias_ref)

    tokens = tokens_ref[...]
    for at, grad_ref in enumerate((query_ref, key_ref, value_ref)):
        grad = grad_ref[...]
        here = slice(at * cols, (at + 1) * cols)
        sum_ref[:, here] += dot_f32(tokens, grad, TN)
        bias_ref[0:1, here] += jnp.sum(grad.astype(jnp.float32), axis=0, keepdims=True)

    @pl.when(step == pl.num_programs(0) - 1)
    def _():
        out_ref[:, :share, :] = sum_ref[...].astype(out_ref.dtype).reshape(devices, share, wide)
        bias = bias_ref[...].astype(out_ref.dtype)
        out_ref[:, share:, :] = jnp.broadcast_to(bias[None], (devices, 8, wide))


def own_grads(grads, sequence, devices, tile):
    length, width = sequence.shape
    share, wide = width // devices, 3 * (width // 2)
    return pl.pallas_call(
        own_grads_kernel,
        grid=(length // tile,),
        in_specs=[pl.BlockSpec((tile, wide // 3), lambda at: (at, 0))] * 3
        + [pl.BlockSpec((tile, width), lambda at: (at, 0))],
        out_specs=pl.BlockSpec((devices, share + 8, wide), lambda at: (0, 0, 0)),
        scratch_shapes=[pltpu.VMEM((width, wide), jnp.float32), pltpu.VMEM((8, wide), jnp.float32)],
        out_shape=jax.ShapeDtypeStruct((devices, share + 8, wide), jnp.bfloat16),
        compiler_params=pltpu.CompilerParams(vmem_limit_bytes=VMEM_LIMIT),
        cost_estimate=pl.CostEstimate(
            flops=2 * length * width * wide, bytes_accessed=6 * length * width, transcendentals=0
        ),
        name="own_grads",
    )(*grads, sequence)


def tokens_grad_kernel(share, query_ref, key_ref, value_ref, gathered_ref, own_ref, other_ref):
    total = None
    for at, grad_ref in enumerate((query_ref, key_ref, value_ref)):
        part = dot_f32(grad_ref[...], own_weight(gathered_ref, at, share), NT)
        total = part if total is None else total + part
    step = lax.rem(pl.program_id(0), 2)

    @pl.when(step == 0)
    def _():
        own_ref[...] = total.astype(own_ref.dtype)

    @pl.when(step == 1)
    def _():
        other_ref[...] = total.astype(other_ref.dtype)


def tokens_grads(grads, gathered, tile):
    devices, high, cols = gathered.shape
    length, width, share = grads[0].shape[0], 2 * cols, (high - 8) // 3
    turn = pl.BlockSpec((tile, width), lambda at: (at // 2, 0))
    half = jax.ShapeDtypeStruct((length // 2, width), jnp.bfloat16)
    return pl.pallas_call(
        functools.partial(tokens_grad_kernel, share),
        grid=(length // tile,),
        in_specs=[pl.BlockSpec((tile, cols), lambda at: (at, 0))] * 3
        + [pl.BlockSpec(gathered.shape, lambda at: (0, 0, 0))],
        out_specs=[turn, turn],
        out_shape=[half, half],
        compiler_params=pltpu.CompilerParams(vmem_limit_bytes=VMEM_LIMIT),
        cost_estimate=pl.CostEstimate(
            flops=6 * length * width * cols, bytes_accessed=6 * length * width, transcendentals=0
        ),
        name="tokens_grads",
    )(*grads, gathered)


def body(
    tokens,
    cotangent,
    lengths,
    query_weight,
    key_weight,
    value_weight,
    output_weight,
    up_weight,
    down_weight,
    query_bias,
    value_bias,
    output_bias,
    up_bias,
    down_bias,
    attn_gain,
    attn_shift,
    ffn_gain,
    ffn_shift,
):
    seqs, stretch, width = tokens.shape
    rows = seqs * stretch
    n_pair, n_core, n_blk = (lax.axis_size(axis) for axis in ALL)
    devices = n_pair * n_core * n_blk
    pair, core, blk = (lax.axis_index(axis) for axis in ALL)
    half, cols = stretch // 2, width // 2
    own_rows = n_blk * half
    share = query_weight.shape[0]
    fold = up_weight.shape[1] // width
    bf16, f32 = jnp.bfloat16, jnp.float32

    def table(step, own, back):
        moves = []
        for pair in range(n_pair):
            for src_core in range(n_core):
                for src in range(n_blk):
                    piece = src ^ step
                    side = piece % 2 if own else 1 - piece % 2
                    sender = (pair * n_core + src_core) * n_blk + src
                    target = (pair * n_core + side) * n_blk + seqs * src_core + piece // 2
                    moves.append((target, sender) if back else (sender, target))
        return moves

    def move(array, step, own=True, back=False):
        return lax.ppermute(array, ALL, table(step, own, back))

    def after(array, *others):
        return lax.optimization_barrier((array, others))[0]

    def other_core(array):
        return lax.ppermute(array, "core", [(0, 1), (1, 0)])

    def columns(array, which):
        return lax.dynamic_slice_in_dim(array, which * cols, cols, axis=-1)

    def swap(flip, one, two):
        return jnp.where(flip, two, one), jnp.where(flip, one, two)

    def ordered(me, items):
        bit = 1
        while bit < len(items):
            flip = (me & bit) != 0
            items = [jnp.where(flip, items[at ^ bit], items[at]) for at in range(len(items))]
            bit *= 2
        return items

    def others(array, axis, size):
        return [
            lax.ppermute(array, axis, [(at, at ^ step) for at in range(size)])
            for step in range(1, size)
        ]

    which = jnp.reshape(core, (1,)).astype(jnp.int32)
    mine, theirs, second = pack(
        which,
        (query_weight, key_weight, value_weight, output_weight, up_weight, down_weight),
        (query_bias, value_bias, output_bias, up_bias, down_bias)
        + (attn_gain, attn_shift, ffn_gain, ffn_shift),
    )
    gathered = jnp.stack(swap(core == 1, mine, other_core(theirs)))
    gathered = jnp.stack(ordered(blk, [gathered] + others(gathered, "blk", n_blk)), axis=1)
    tokens_moved, second = after(tokens, gathered), after(second, gathered)
    gathered = jnp.stack(ordered(pair, [gathered] + others(gathered, "pair", n_pair)))
    gathered = gathered.reshape(devices, 3 * share + 8, cols)
    second = lax.all_gather(second, ALL, axis=0)
    both = jnp.concatenate(swap(core == 1, lengths, other_core(lengths)))
    own_length = lax.dynamic_index_in_dim(both, blk, 0, keepdims=False)

    parts = n_blk // 2
    pieces = tokens_moved.reshape(n_blk, half, width)
    arrived = [
        move(lax.dynamic_index_in_dim(pieces, blk ^ step, 0, keepdims=False), step)
        for step in range(n_blk)
    ]
    crossed = other_core(after(jnp.concatenate(arrived, axis=0), gathered))
    sequence, starts = [], []
    for part in range(parts):
        sequence += arrived[2 * part : 2 * part + 2]
        sequence.append(crossed[2 * part * half : 2 * (part + 1) * half])
        for side in (core, 1 - core):
            piece = 2 * (blk % seqs) + side
            for step in (2 * part, 2 * part + 1):
                starts.append((piece ^ step) * stretch + side * half)
    sequence = jnp.concatenate(sequence, axis=0)
    info = jnp.stack([own_length] + starts).astype(jnp.int32)
    odd = blk % 2 == 1

    def quarters(array):
        return [[array[low : low + half, at : at + cols] for at in (0, cols)] for low in (0, half)]

    def after_all(items, *others):
        return lax.optimization_barrier((items, others))[0]

    qkv = project(which, sequence, gathered, 512)
    attended, returning = [], []
    for part in range(parts):
        query_side = after(qkv, attended[-1]) if part else qkv
        attended.append(attend(query_side, info, part, parts, 512, 512))
        low = attended[-1][0]
        pieces = [low[at : at + half] for at in range(0, 4 * half, half)]
        own = [move(pieces[at], 2 * part + at, True, True) for at in range(2)]
        far = [move(pieces[2 + at], 2 * part + at, False, True) for at in range(2)]
        returning.append(own + far)

    fed, context, context_grads, kept = [], [], [], ()
    for part in range(parts):
        moved = after_all(returning[part], fed[-1] if part else attended[-1])
        own, far = moved[:2], moved[2:]
        top = jnp.concatenate([swap(odd, *own)[0], swap(odd, *far)[0]], axis=1)
        bottom = jnp.concatenate([swap(odd, *far)[1], swap(odd, *own)[1]], axis=1)
        context.append(jnp.concatenate([top, bottom], axis=0))
        index = jnp.reshape((blk // 2) ^ part, (1,)).astype(jnp.int32)
        fed.append(feed(index, context[part], tokens, cotangent, gathered, second, kept, 256))
        kept = (fed[-1][0],)
        (top_left, top_right), (low_left, low_right) = quarters(fed[-1][7])
        own = swap(odd, top_left, low_right)
        far = swap(odd, top_right, low_left)
        context_grads.append(
            [move(own[at], 2 * part + at, True) for at in range(2)]
            + [move(far[at], 2 * part + at, False) for at in range(2)]
        )
    layer_out = kept[0]

    early, late = context_grads[0], context_grads[1]
    early, context[0] = lax.optimization_barrier((early, context[0]))
    up_keep, up_send = up_grads(
        which,
        [(context[part], item[6], item[4], item[3]) for part, item in enumerate(fed)],
        (n_pair, n_blk),
    )
    own, up_keep = lax.optimization_barrier((late[:2], up_keep))
    down_keep, down_send = down_grads(
        which, [(item[1], item[2], after(item[8], up_keep, own)) for item in fed], (n_pair, n_blk)
    )
    far, down_keep = lax.optimization_barrier((late[2:], down_keep))
    total = jnp.concatenate(
        [
            (keep.astype(f32) + other_core(send).astype(f32)).astype(bf16)
            for keep, send in ((up_keep, up_send), (down_keep, down_send))
        ],
        axis=2,
    )
    second_grads = lax.psum_scatter(total, "pair", scatter_dimension=0)
    context_grads = [jnp.concatenate(early, axis=0), jnp.concatenate(own + far, axis=0)]
    context_grads[0] = after(context_grads[0], total)
    outs, auxes = [item[1] for item in attended], [item[2] for item in attended]
    grads = attend_back(qkv, context_grads, outs, auxes, info, 0, cols // LANES, 512, 512)

    second_grads, grads = lax.optimization_barrier((second_grads, grads))
    second_grads = lax.psum_scatter(second_grads, "blk", scatter_dimension=0)
    first_grads = own_grads(grads, sequence, devices, 512)
    own, far = tokens_grads([after(item, first_grads) for item in grads], gathered, 512)
    summed = (own.astype(f32) + other_core(far).astype(f32)).astype(bf16)
    moved = [
        move(summed[step * half : (step + 1) * half], step, True, True) for step in range(n_blk)
    ]

    def to_sum(array, axis, me, size):
        terms = [lax.dynamic_index_in_dim(array, me, 0, keepdims=False)]
        for step in range(1, size):
            sent = lax.dynamic_index_in_dim(array, me ^ step, 0, keepdims=False)
            terms.append(lax.ppermute(sent, axis, [(at, at ^ step) for at in range(size)]))
        return terms

    def add(terms):
        total = terms[0].astype(f32)
        for term in terms[1:]:
            total += term.astype(f32)
        return total.astype(bf16)

    first_grads = first_grads.reshape(n_pair, n_core, n_blk, share + 8, 3 * cols)
    terms, moved[:2] = lax.optimization_barrier(
        (to_sum(first_grads, "pair", pair, n_pair), moved[:2])
    )
    terms = to_sum(jnp.moveaxis(add(terms), 1, 0), "blk", blk, n_blk)
    returned = []
    for part in range(parts):
        back = jnp.concatenate(swap(odd, *moved[2 * part : 2 * part + 2]), axis=0)
        returned.append(fed[part][5] + back.astype(f32))
    tokens_grad = jnp.stack(swap(blk >= 2, *returned))
    terms, tokens_grad = lax.optimization_barrier((terms, tokens_grad))
    total = add(terms)
    kept = lax.dynamic_index_in_dim(total, core, 0, keepdims=False)
    crossed = other_core(lax.dynamic_index_in_dim(total, 1 - core, 0, keepdims=False))
    left = jnp.where(core == 0, kept, crossed).astype(f32)
    right = jnp.where(core == 0, crossed, kept).astype(f32)
    projections = [
        jnp.concatenate([left[:, at : at + cols], right[:, at : at + cols]], axis=1)
        for at in range(0, 3 * cols, cols)
    ]
    device = (pair * n_core + core) * n_blk + blk

    def own_part(line, size):
        return lax.dynamic_slice_in_dim(line, device * size, size, axis=-1)

    second_grads = second_grads.astype(f32)
    lines = second_grads[1 + 2 * fold]
    own_lines = own_part(lines[:6], share)
    return (
        (layer_out, tokens_grad)
        + tuple(item[:share] for item in projections)
        + (
            second_grads[0],
            jnp.concatenate([second_grads[1 + at] for at in range(fold)], axis=1),
            second_grads[1 + fold : 1 + 2 * fold].reshape(fold * share, width),
        )
        + (own_part(projections[0][share], share), own_part(projections[2][share], share))
        + (own_lines[0], own_part(lines[6 : 6 + fold].reshape(-1), fold * share), own_lines[1])
        + (own_lines[2], own_lines[3], own_lines[4], own_lines[5])
    )


def fits(mesh, tokens, up_weight):
    n_dp, n_blk = mesh.shape["dp"], mesh.shape["blk"]
    batch, length, width = tokens.shape
    if n_dp % 2 or n_dp & (n_dp - 1) or batch % n_dp or 2 * (batch // n_dp) != n_blk or n_blk != 4:
        return False
    share = width // (n_dp * n_blk)
    fold = up_weight.shape[1] // width
    return (
        width == HEADS * 64
        and width % (4 * LANES // PER_TILE) == 0
        and up_weight.shape[1] == fold * width
        and share * n_dp * n_blk == width
        and share % 8 == 0
        and 16 <= share
        and (8 + fold) * share <= width // 2
        and fold == n_dp // 2
        and length % (16 * n_blk) == 0
        and length % 512 == 0
        and length <= 4096
    )


def solution(mesh):
    n_dp, n_blk = mesh.shape["dp"], mesh.shape["blk"]

    def step(*args):
        spread = ("dp", "blk")
        one, use = ring_body, mesh
        where = {"dp": "dp", "blk": "blk", spread: spread}
        if fits(mesh, args[0], args[7]):
            one, use = body, Mesh(mesh.devices.reshape(n_dp // 2, 2, n_blk), ALL)
            where = {"dp": ("pair", "core"), "blk": "blk", spread: ALL}
        block = P(where["dp"], where["blk"], None)
        matrix = P(where[spread], None)
        vector = P(where[spread])
        return jax.shard_map(
            one,
            mesh=use,
            in_specs=(block, block, P(where["dp"])) + (matrix,) * 6 + (vector,) * 9,
            out_specs=(block, block) + (matrix,) * 6 + (vector,) * 9,
            check_vma=False,
        )(*args)

    return step
```

```python
import functools

import jax
import jax.numpy as jnp
from jax import lax
from jax.experimental import pallas as pl
from jax.experimental.pallas import tpu as pltpu
from jax.sharding import Mesh
from jax.sharding import PartitionSpec as P

HEADS = 12
LANES = 128
PER_TILE = 2
SCORE_SCALE = 0.125 * 1.4426950408889634
MASKED = -1e30
ALL = ("pair", "core", "blk")
VMEM_LIMIT = 56 << 20


def shifted(array, axis, by):
    length = lax.axis_size(axis)
    return lax.ppermute(array, axis, [(i, (i + by) % length) for i in range(length)])


def matmul(left, right):
    return jnp.dot(left, right, preferred_element_type=jnp.float32)


def times_trans(left, right):
    return lax.dot_general(
        left, right, (((1,), (1,)), ((), ())), preferred_element_type=jnp.float32
    )


def trans_times(left, right):
    return lax.dot_general(
        left, right, (((0,), (0,)), ((), ())), preferred_element_type=jnp.float32
    )


def layer_norm(values, gain, shift):
    center = jnp.mean(values, axis=-1, keepdims=True)
    offset = values - center
    spread = jnp.mean(offset * offset, axis=-1, keepdims=True)
    return offset * lax.rsqrt(spread + 1e-12) * gain + shift


def gelu_tanh(values):
    return jax.nn.gelu(values, approximate=True)


def ring_body(
    tokens,
    cotangent,
    lengths,
    query_weight,
    key_weight,
    value_weight,
    output_weight,
    up_weight,
    down_weight,
    query_bias,
    value_bias,
    output_bias,
    up_bias,
    down_bias,
    attn_gain,
    attn_shift,
    ffn_gain,
    ffn_shift,
):
    seqs, stretch, width = tokens.shape
    rows = seqs * stretch
    heads = HEADS
    head = width // heads
    gathered = (
        lax.all_gather(query_weight, ("dp", "blk"), axis=0, tiled=True),
        lax.all_gather(key_weight, ("dp", "blk"), axis=0, tiled=True),
        lax.all_gather(value_weight, ("dp", "blk"), axis=0, tiled=True),
        lax.all_gather(output_weight, ("dp", "blk"), axis=0, tiled=True),
        lax.all_gather(up_weight, ("dp", "blk"), axis=0, tiled=True),
        lax.all_gather(down_weight, ("dp", "blk"), axis=0, tiled=True),
        lax.all_gather(query_bias, ("dp", "blk"), axis=0, tiled=True),
        lax.all_gather(value_bias, ("dp", "blk"), axis=0, tiled=True),
        lax.all_gather(output_bias, ("dp", "blk"), axis=0, tiled=True),
        lax.all_gather(up_bias, ("dp", "blk"), axis=0, tiled=True),
        lax.all_gather(down_bias, ("dp", "blk"), axis=0, tiled=True),
        lax.all_gather(attn_gain, ("dp", "blk"), axis=0, tiled=True),
        lax.all_gather(attn_shift, ("dp", "blk"), axis=0, tiled=True),
        lax.all_gather(ffn_gain, ("dp", "blk"), axis=0, tiled=True),
        lax.all_gather(ffn_shift, ("dp", "blk"), axis=0, tiled=True),
    )
    query_full, key_full, value_full, output_full, upper_full, lower_full = gathered[:6]
    (
        bias_query,
        bias_value,
        bias_output,
        bias_upper,
        bias_lower,
        gain_one,
        shift_one,
        gain_two,
        shift_two,
    ) = [item.astype(jnp.float32) for item in gathered[6:]]
    flat = tokens.reshape(rows, width)
    queries = (matmul(flat, query_full) + bias_query).astype(jnp.bfloat16)
    keys_own = matmul(flat, key_full).astype(jnp.bfloat16)
    values_own = (matmul(flat, value_full) + bias_value).astype(jnp.bfloat16)
    query_heads = queries.reshape(seqs, stretch, heads, head)
    own_block = lax.axis_index("blk")
    cycle_size = lax.axis_size("blk")
    start = jnp.int32(0)
    key_piece = lax.all_gather(keys_own.reshape(seqs, stretch, width), "blk", axis=1, tiled=True)
    value_piece = lax.all_gather(
        values_own.reshape(seqs, stretch, width), "blk", axis=1, tiled=True
    )
    count = key_piece.shape[1]
    span = min(count, stretch)
    row_max = jnp.full((seqs, stretch, heads), -1e30, jnp.float32)
    row_total = jnp.zeros((seqs, stretch, heads), jnp.float32)
    accum = jnp.zeros((seqs, stretch, heads, head), jnp.float32)
    for part_no in range(count // span):
        key_heads = key_piece[:, part_no * span : (part_no + 1) * span].reshape(
            seqs, span, heads, head
        )
        value_heads = value_piece[:, part_no * span : (part_no + 1) * span].reshape(
            seqs, span, heads, head
        )
        positions = start + part_no * span + jnp.arange(span, dtype=jnp.int32)
        valid = positions[None, :] < lengths[:, None]
        scores = (
            jnp.einsum(
                "sqhd,skhd->sqhk", query_heads, key_heads, preferred_element_type=jnp.float32
            )
            * 0.125
        )
        scores = jnp.where(valid[:, None, None, :], scores, -jnp.inf)
        new_max = jnp.maximum(row_max, jnp.max(scores, axis=-1))
        expo = jnp.exp(scores - new_max[..., None])
        factor = jnp.exp(row_max - new_max)
        row_total = row_total * factor + jnp.sum(expo, axis=-1)
        accum = accum * factor[..., None] + jnp.einsum(
            "sqhk,skhd->sqhd",
            expo.astype(jnp.bfloat16),
            value_heads,
            preferred_element_type=jnp.float32,
        )
        row_max = new_max
    row_max, row_total, accum = (row_max, row_total, accum)
    log_total = row_max + jnp.log(row_total)
    context_full = accum / row_total[..., None]
    context = context_full.reshape(rows, width).astype(jnp.bfloat16)
    attended = matmul(context, output_full) + bias_output
    hidden, norm_one_back = jax.vjp(
        layer_norm, flat.astype(jnp.float32) + attended, gain_one, shift_one
    )
    hidden_low = hidden.astype(jnp.bfloat16)
    upward = matmul(hidden_low, upper_full) + bias_upper
    active_full, gelu_back = jax.vjp(gelu_tanh, upward)
    active = active_full.astype(jnp.bfloat16)
    downward = matmul(active, lower_full) + bias_lower
    output_full32, norm_two_back = jax.vjp(layer_norm, hidden + downward, gain_two, shift_two)
    layer_out = output_full32.astype(jnp.bfloat16).reshape(seqs, stretch, width)
    query_back, key_back, value_back, output_back, upper_back, lower_back = (
        lax.all_gather(query_weight, ("dp", "blk"), axis=0, tiled=True),
        lax.all_gather(key_weight, ("dp", "blk"), axis=0, tiled=True),
        lax.all_gather(value_weight, ("dp", "blk"), axis=0, tiled=True),
        lax.all_gather(output_weight, ("dp", "blk"), axis=0, tiled=True),
        lax.all_gather(up_weight, ("dp", "blk"), axis=0, tiled=True),
        lax.all_gather(down_weight, ("dp", "blk"), axis=0, tiled=True),
    )
    grad_outer = cotangent.reshape(rows, width).astype(jnp.float32)
    grad_res_two, grad_gain_two, grad_shift_two = norm_two_back(grad_outer)
    grad_down = grad_res_two.astype(jnp.bfloat16)
    grad_lower_bias = jnp.sum(grad_down, axis=0, dtype=jnp.float32)
    grad_lower = trans_times(active, grad_down)
    grad_active = times_trans(grad_down, lower_back)
    (grad_upward,) = gelu_back(grad_active)
    grad_up = grad_upward.astype(jnp.bfloat16)
    grad_upper_bias = jnp.sum(grad_up, axis=0, dtype=jnp.float32)
    grad_upper = trans_times(hidden_low, grad_up)
    grad_hidden = grad_res_two + times_trans(grad_up, upper_back)
    grad_res_one, grad_gain_one, grad_shift_one = norm_one_back(grad_hidden)
    grad_attended = grad_res_one.astype(jnp.bfloat16)
    grad_output_bias = jnp.sum(grad_attended, axis=0, dtype=jnp.float32)
    grad_output = trans_times(context, grad_attended)
    grad_context = times_trans(grad_attended, output_back).astype(jnp.bfloat16)
    context_grad_heads = grad_context.reshape(seqs, stretch, heads, head)
    delta = jnp.sum(context_grad_heads.astype(jnp.float32) * context_full, axis=-1)

    def contribute(key_value, source, pair_grad, query_grad):
        key_heads = key_value[0]
        value_heads = key_value[1]
        positions = source * stretch + jnp.arange(stretch, dtype=jnp.int32)
        valid = positions[None, :] < lengths[:, None]
        scores = (
            jnp.einsum(
                "sqhd,skhd->sqhk", query_heads, key_heads, preferred_element_type=jnp.float32
            )
            * 0.125
        )
        probs = jnp.where(valid[:, None, None, :], jnp.exp(scores - log_total[..., None]), 0.0)
        grad_probs = jnp.einsum(
            "sqhd,skhd->sqhk", context_grad_heads, value_heads, preferred_element_type=jnp.float32
        )
        grad_scores = (probs * (grad_probs - delta[..., None])).astype(jnp.bfloat16)
        query_grad = (
            query_grad
            + jnp.einsum(
                "sqhk,skhd->sqhd", grad_scores, key_heads, preferred_element_type=jnp.float32
            )
            * 0.125
        )
        key_part = (
            jnp.einsum(
                "sqhk,sqhd->skhd", grad_scores, query_heads, preferred_element_type=jnp.float32
            )
            * 0.125
        )
        value_part = jnp.einsum(
            "sqhk,sqhd->skhd",
            probs.astype(jnp.bfloat16),
            context_grad_heads,
            preferred_element_type=jnp.float32,
        )
        pair_grad = pair_grad + jnp.stack([key_part, value_part])
        return (pair_grad, query_grad)

    def rotate_grads(pair_grad):
        return shifted(pair_grad.astype(jnp.bfloat16), "blk", 1).astype(pair_grad.dtype)

    key_value_own = jnp.stack(
        [
            keys_own.reshape(seqs, stretch, heads, head),
            values_own.reshape(seqs, stretch, heads, head),
        ]
    )
    pair_grad, query_grad = contribute(
        key_value_own,
        own_block,
        jnp.zeros((2, seqs, stretch, heads, head), jnp.float32),
        jnp.zeros((seqs, stretch, heads, head), jnp.float32),
    )

    def cycle_turn(turn, state):
        key_value_now, pair_now, query_now = state
        key_value_now = shifted(key_value_now, "blk", 1)
        pair_now = rotate_grads(pair_now)
        source = (own_block - turn) % cycle_size
        pair_now, query_now = contribute(key_value_now, source, pair_now, query_now)
        return (key_value_now, pair_now, query_now)

    final_state = lax.fori_loop(1, cycle_size, cycle_turn, (key_value_own, pair_grad, query_grad))
    pair_home = rotate_grads(final_state[1])
    grad_queries = final_state[2].reshape(rows, width).astype(jnp.bfloat16)
    grad_keys = pair_home[0].reshape(rows, width).astype(jnp.bfloat16)
    grad_values = pair_home[1].reshape(rows, width).astype(jnp.bfloat16)
    grad_query = trans_times(flat, grad_queries)
    grad_key = trans_times(flat, grad_keys)
    grad_value = trans_times(flat, grad_values)
    grad_query_bias = jnp.sum(grad_queries, axis=0, dtype=jnp.float32)
    grad_value_bias = jnp.sum(grad_values, axis=0, dtype=jnp.float32)
    tokens_grad = (
        grad_res_one
        + times_trans(grad_queries, query_back)
        + times_trans(grad_keys, key_back)
        + times_trans(grad_values, value_back)
    ).reshape(seqs, stretch, width)
    shares = (
        lax.psum_scatter(grad_query, ("dp", "blk"), scatter_dimension=0, tiled=True),
        lax.psum_scatter(grad_key, ("dp", "blk"), scatter_dimension=0, tiled=True),
        lax.psum_scatter(grad_value, ("dp", "blk"), scatter_dimension=0, tiled=True),
        lax.psum_scatter(grad_output, ("dp", "blk"), scatter_dimension=0, tiled=True),
        lax.psum_scatter(grad_upper, ("dp", "blk"), scatter_dimension=0, tiled=True),
        lax.psum_scatter(grad_lower, ("dp", "blk"), scatter_dimension=0, tiled=True),
        lax.psum_scatter(grad_query_bias, ("dp", "blk"), scatter_dimension=0, tiled=True),
        lax.psum_scatter(grad_value_bias, ("dp", "blk"), scatter_dimension=0, tiled=True),
        lax.psum_scatter(grad_output_bias, ("dp", "blk"), scatter_dimension=0, tiled=True),
        lax.psum_scatter(grad_upper_bias, ("dp", "blk"), scatter_dimension=0, tiled=True),
        lax.psum_scatter(grad_lower_bias, ("dp", "blk"), scatter_dimension=0, tiled=True),
        lax.psum_scatter(grad_gain_one, ("dp", "blk"), scatter_dimension=0, tiled=True),
        lax.psum_scatter(grad_shift_one, ("dp", "blk"), scatter_dimension=0, tiled=True),
        lax.psum_scatter(grad_gain_two, ("dp", "blk"), scatter_dimension=0, tiled=True),
        lax.psum_scatter(grad_shift_two, ("dp", "blk"), scatter_dimension=0, tiled=True),
    )
    return (layer_out, tokens_grad) + tuple(shares)


def dot_f32(left, right, dims):
    return lax.dot_general(left, right, (dims, ((), ())), preferred_element_type=jnp.float32)


NT = ((1,), (1,))
NN = ((1,), (0,))


def split_three(values):
    high = values.astype(jnp.bfloat16).astype(jnp.float32)
    rest = values - high
    mid = rest.astype(jnp.bfloat16).astype(jnp.float32)
    return high, mid, rest - mid


def spread_three(lane, base, values, into):
    for step, part in enumerate(split_three(values)):
        into = jnp.where(lane == base + step, part, into)
    return into


def fill_keys(info_ref, keys, values, key_aug, value_aug, value_fill, chunk):
    length = keys.shape[0]
    lane = lax.broadcasted_iota(jnp.int32, (chunk, LANES), 1)
    row = lax.broadcasted_iota(jnp.int32, (chunk, LANES), 0)
    for part in range(length // chunk):
        at = slice(part * chunk, (part + 1) * chunk)
        off = (lane == 3) & (row + info_ref[1 + part] >= info_ref[0])
        mask = jnp.where(off, MASKED, 0.0)
        for one in range(PER_TILE):
            mine = lane // (LANES // PER_TILE) == one
            base = 4 * one
            minus = (lane >= base) & (lane < base + 3)
            key_aug[one, at, :LANES] = jnp.where(mine, keys[at], jnp.zeros((), keys.dtype))
            key_aug[one, at, LANES:] = jnp.where(minus, -1.0, mask).astype(jnp.bfloat16)
            value_aug[one, at, :LANES] = jnp.where(mine, values[at], jnp.zeros((), keys.dtype))
            if value_fill:
                value_aug[one, at, LANES:] = jnp.ones((chunk, LANES), jnp.bfloat16)
            else:
                value_aug[one, at, LANES:] = jnp.where(minus, -1.0, 0.0).astype(jnp.bfloat16)


def attend_kernel(
    span, info_ref, query_ref, key_ref, value_ref, low_ref, out_ref, aux_ref, key_aug, value_aug
):
    length = key_ref.shape[0]
    tile = query_ref.shape[0]
    lane = lax.broadcasted_iota(jnp.int32, (1, LANES), 1)

    @pl.when(pl.program_id(1) == 0)
    def _():
        fill_keys(info_ref, key_ref, value_ref, key_aug, value_aug, True, length // 8)

    one_lane = jnp.where(lane == 3, 1.0, 0.0)
    flag = jnp.broadcast_to(one_lane.astype(jnp.bfloat16), (tile, LANES))
    query = jnp.concatenate([query_ref[...], flag], axis=1)
    pieces = [slice(at, at + span) for at in range(0, length, span)]
    scores, peaks = [], []
    for one in range(PER_TILE):
        peak = None
        row = []
        for at in pieces:
            score = dot_f32(query, key_aug[one, at], NT)
            row.append(score)
            for low in range(0, span, LANES):
                part = score[:, low : low + LANES]
                peak = part if peak is None else jnp.maximum(peak, part)
        scores.append(row)
        peaks.append(jnp.max(peak, axis=1, keepdims=True))
    out = None
    aux = one_lane
    for one in range(PER_TILE):
        total = None
        for at, score in zip(pieces, scores[one]):
            expo = jnp.exp2((score - peaks[one]) * SCORE_SCALE).astype(jnp.bfloat16)
            part = dot_f32(expo, value_aug[one, at], NN)
            total = part if total is None else total + part
        weight = total[:, LANES:]
        part = total[:, :LANES] / weight
        out = part if out is None else out + part
        log_total = jnp.log2(weight) * (1.0 / SCORE_SCALE) + peaks[one]
        aux = spread_three(lane, 4 * one, log_total, aux)
    low_ref[...] = out.astype(jnp.bfloat16)
    out_ref[...] = out
    aux_ref[...] = aux.astype(jnp.bfloat16)


def attend(qkv, info, part, parts, tile, span):
    length, width = qkv.shape[0], qkv.shape[1] // 3
    tiles, rows = width // LANES, length // parts
    first = part * (rows // tile)
    query_spec = pl.BlockSpec((tile, LANES), lambda pair, at: (at, pair))
    return pl.pallas_call(
        functools.partial(attend_kernel, span),
        grid=(tiles, rows // tile),
        in_specs=[
            pl.BlockSpec(memory_space=pltpu.SMEM),
            pl.BlockSpec((tile, LANES), lambda pair, at: (first + at, pair)),
            pl.BlockSpec((length, LANES), lambda pair, at: (0, tiles + pair)),
            pl.BlockSpec((length, LANES), lambda pair, at: (0, 2 * tiles + pair)),
        ],
        out_specs=[query_spec] * 3,
        out_shape=[
            jax.ShapeDtypeStruct((rows, width), jnp.bfloat16),
            jax.ShapeDtypeStruct((rows, width), jnp.float32),
            jax.ShapeDtypeStruct((rows, width), jnp.bfloat16),
        ],
        scratch_shapes=[pltpu.VMEM((PER_TILE, length, 2 * LANES), jnp.bfloat16)] * 2,
        compiler_params=pltpu.CompilerParams(vmem_limit_bytes=VMEM_LIMIT),
        cost_estimate=pl.CostEstimate(
            flops=16 * rows * length * width,
            bytes_accessed=12 * length * width,
            transcendentals=rows * length * width // 64,
        ),
        name="attend",
    )(info, qkv, qkv, qkv)


def attend_back_kernel(span, per_part, info_ref, query_ref, key_ref, value_ref, *refs):
    parts = (len(refs) - 8) // 3
    groups = [refs[at * parts : (at + 1) * parts] for at in range(3)]
    query_grad_ref, key_grad_ref, value_grad_ref, key_aug, value_aug, key_cols, key_sum, value_sum = (
        refs[3 * parts :]
    )
    length = key_ref.shape[0]
    tile = query_ref.shape[0]
    wide = LANES // PER_TILE
    lane = lax.broadcasted_iota(jnp.int32, (1, LANES), 1)
    step = pl.program_id(1)

    @pl.when(step == 0)
    def _():
        fill_keys(info_ref, key_ref, value_ref, key_aug, value_aug, False, length // 8)
        key_cols[...] = key_ref[...].T
        key_sum[...] = jnp.zeros_like(key_sum)
        value_sum[...] = jnp.zeros_like(value_sum)

    grad, out, aux = (group[0][...] for group in groups)
    for part in range(1, parts):
        here = step >= part * per_part
        grad, out, aux = (
            jnp.where(here, group[part][...], item) for group, item in zip(groups, (grad, out, aux))
        )
    plain = query_ref[...]
    query = jnp.concatenate([plain, aux], axis=1)
    product = grad.astype(jnp.float32) * out
    delta = jnp.zeros((tile, LANES), jnp.float32)
    for one in range(PER_TILE):
        own = jnp.sum(jnp.where(lane // wide == one, product, 0.0), axis=1, keepdims=True)
        delta = spread_three(lane, 4 * one, own, delta)
    grad_aug = jnp.concatenate([grad, delta.astype(jnp.bfloat16)], axis=1)
    nothing = jnp.zeros((), plain.dtype)
    query_rows = []
    for one in range(PER_TILE):
        mine = lane // wide == one
        query_own = jnp.where(mine, plain, nothing)
        grad_own = jnp.where(mine, grad, nothing)
        total = None
        for low in range(0, length, span):
            at = slice(low, low + span)
            score = dot_f32(key_aug[one, at], query, NT)
            grad_probs = dot_f32(value_aug[one, at], grad_aug, NT)
            probs = jnp.exp2(score * SCORE_SCALE)
            grad_scores = (probs * grad_probs).astype(jnp.bfloat16)
            value_sum[at] += dot_f32(probs.astype(jnp.bfloat16), grad_own, NN)
            key_sum[at] += dot_f32(grad_scores, query_own, NN)
            part = dot_f32(key_cols[wide * one : wide * (one + 1), at], grad_scores, NN)
            total = part if total is None else total + part
        query_rows.append(total)
    query_grad_ref[...] = (jnp.concatenate(query_rows, axis=0).T * 0.125).astype(jnp.bfloat16)

    @pl.when(step == pl.num_programs(1) - 1)
    def _():
        key_grad_ref[...] = (key_sum[...] * 0.125).astype(jnp.bfloat16)
        value_grad_ref[...] = value_sum[...].astype(jnp.bfloat16)


def attend_back(qkv, grads, outs, auxes, info, first, count, tile, span):
    length, width = qkv.shape[0], qkv.shape[1] // 3
    tiles, parts = width // LANES, len(grads)
    per_part = length // parts // tile

    def part_spec(part):
        low = part * per_part
        return pl.BlockSpec(
            (tile, LANES), lambda pair, at: (jnp.clip(at - low, 0, per_part - 1), first + pair)
        )

    result = jax.ShapeDtypeStruct((length, count * LANES), jnp.bfloat16)
    whole = pl.BlockSpec((length, LANES), lambda pair, at: (0, pair))
    return pl.pallas_call(
        functools.partial(attend_back_kernel, span, per_part),
        grid=(count, length // tile),
        in_specs=[
            pl.BlockSpec(memory_space=pltpu.SMEM),
            pl.BlockSpec((tile, LANES), lambda pair, at: (at, first + pair)),
            pl.BlockSpec((length, LANES), lambda pair, at: (0, tiles + first + pair)),
            pl.BlockSpec((length, LANES), lambda pair, at: (0, 2 * tiles + first + pair)),
        ]
        + [part_spec(part) for part in range(parts)] * 3,
        out_specs=[pl.BlockSpec((tile, LANES), lambda pair, at: (at, pair)), whole, whole],
        out_shape=[result] * 3,
        scratch_shapes=[pltpu.VMEM((PER_TILE, length, 2 * LANES), jnp.bfloat16)] * 2
        + [pltpu.VMEM((LANES, length), jnp.bfloat16)]
        + [pltpu.VMEM((length, LANES), jnp.float32)] * 2,
        compiler_params=pltpu.CompilerParams(vmem_limit_bytes=VMEM_LIMIT),
        cost_estimate=pl.CostEstimate(
            flops=40 * count * LANES * length * length,
            bytes_accessed=22 * length * width,
            transcendentals=count * length * length * 2,
        ),
        name="attend_back",
    )(info, qkv, qkv, qkv, *grads, *outs, *auxes)


def pack_kernel(count, core_ref, *refs):
    query, key, value, output, up, down = refs[:6]
    vectors = refs[6 : 6 + count]
    mine_ref, theirs_ref, second_ref, held_ref, wide_ref = refs[6 + count : 11 + count]
    lines = refs[11 + count : 11 + 2 * count]
    sems, line_sems = refs[11 + 2 * count :]
    share, width = query.shape
    cols = width // 2
    fold = up.shape[1] // width
    copies = [
        pltpu.make_async_copy(item, held_ref.at[at], sems.at[at])
        for at, item in enumerate((query, key, value))
    ]
    copies += [
        pltpu.make_async_copy(item, line, line_sems.at[at])
        for at, (item, line) in enumerate(zip(vectors, lines))
    ]
    later = [pltpu.make_async_copy(output, second_ref.at[0], sems.at[3])]
    for at in range(fold):
        later.append(
            pltpu.make_async_copy(
                down.at[pl.ds(at * share, share)],
                second_ref.at[1 + fold + at],
                sems.at[4 + at],
            )
        )
    later.append(pltpu.make_async_copy(up, wide_ref, sems.at[4 + fold]))
    for copy in copies + later:
        copy.start()
    for copy in copies:
        copy.wait()
    first_core = core_ref[0] == 0
    for at in range(3):
        left, right = held_ref[at, :, :cols], held_ref[at, :, cols:]
        here = slice(at * share, (at + 1) * share)
        mine_ref[here] = jnp.where(first_core, left, right)
        theirs_ref[here] = jnp.where(first_core, right, left)
    for ref in (mine_ref, theirs_ref):
        ref[3 * share :] = jnp.zeros((8, cols), ref.dtype)
        for at, line in enumerate(lines):
            low = at // 8 * LANES
            ref[3 * share + at % 8, low : low + line.shape[0]] = line[...]
    for copy in later:
        copy.wait()
    for at in range(fold):
        second_ref[1 + at] = wide_ref[:, at * width : (at + 1) * width]


def pack(core, matrices, vectors):
    share, width = matrices[0].shape
    cols = width // 2
    fold = matrices[4].shape[1] // width
    count = len(vectors)
    block = jax.ShapeDtypeStruct((3 * share + 8, cols), jnp.bfloat16)
    inside = pl.BlockSpec(memory_space=pltpu.VMEM)
    return pl.pallas_call(
        functools.partial(pack_kernel, count),
        in_specs=[pl.BlockSpec(memory_space=pltpu.SMEM)]
        + [pl.BlockSpec(memory_space=pl.ANY)] * (6 + count),
        out_specs=[inside] * 3,
        out_shape=[
            block,
            block,
            jax.ShapeDtypeStruct((1 + 2 * fold, share, width), jnp.bfloat16),
        ],
        scratch_shapes=[pltpu.VMEM((3, share, width), jnp.bfloat16)]
        + [pltpu.VMEM(matrices[4].shape, jnp.bfloat16)]
        + [pltpu.VMEM(item.shape, item.dtype) for item in vectors]
        + [pltpu.SemaphoreType.DMA((5 + fold,)), pltpu.SemaphoreType.DMA((count,))],
        compiler_params=pltpu.CompilerParams(vmem_limit_bytes=VMEM_LIMIT),
        name="pack",
    )(core, *matrices, *vectors)


def by_device(gathered_ref, rows, columns=slice(None)):
    n_pair, n_blk, n_core = gathered_ref.shape[:3]
    return jnp.concatenate(
        [
            gathered_ref[pair, blk, core, rows, columns]
            for pair in range(n_pair)
            for core in range(n_core)
            for blk in range(n_blk)
        ],
        axis=0,
    )


def unspread(gathered_ref, first_row, entry, width, share):
    low, row = entry // 8 * LANES, first_row + entry % 8
    pieces = by_device(gathered_ref, slice(row, row + 1), slice(low, low + LANES))
    lane = lax.broadcasted_iota(jnp.int32, (LANES, width), 1)
    row = lax.broadcasted_iota(jnp.int32, (LANES, width), 0)
    pick = jnp.where(lax.rem(lane, share) == row, 1.0, 0.0).astype(jnp.bfloat16)
    spread = dot_f32(pieces, pick, NN)
    lane = lax.broadcasted_iota(jnp.int32, (pieces.shape[0], width), 1)
    row = lax.broadcasted_iota(jnp.int32, (pieces.shape[0], width), 0)
    return jnp.sum(jnp.where(lax.div(lane, share) == row, spread, 0.0), axis=0, keepdims=True)


def own_weight(gathered_ref, at, share):
    return by_device(gathered_ref, slice(at * share, (at + 1) * share))


def block_rows(core_ref, own_ref, other_ref):
    own, other = own_ref[...], other_ref[...]
    first = core_ref[0] == 0
    return jnp.concatenate([jnp.where(first, own, other), jnp.where(first, other, own)], axis=0)


def block_specs(half, width):
    return [
        pl.BlockSpec((half, width), lambda at, core: (at, 0)),
        pl.BlockSpec((half, width), lambda at, core: (at + 1 - 2 * lax.rem(at, 2), 0)),
    ]


def project_kernel(share, core_ref, own_ref, other_ref, gathered_ref, out_ref, bias_ref):
    cols = gathered_ref.shape[4]

    @pl.when(pl.program_id(0) == 0)
    def _():
        for at in range(2):
            whole = unspread(gathered_ref, 3 * share, at, 2 * cols, share)
            bias_ref[at : at + 1, :] = jnp.where(
                core_ref[0] == 0, whole[:, :cols], whole[:, cols:]
            )

    tokens = block_rows(core_ref, own_ref, other_ref)
    for at, bias in enumerate((0, None, 1)):
        part = dot_f32(tokens, own_weight(gathered_ref, at, share), NN)
        if bias is not None:
            part = part + bias_ref[bias : bias + 1, :]
        out_ref[:, at * cols : (at + 1) * cols] = part.astype(out_ref.dtype)


def project(core, own, other, gathered, half):
    length, width = 2 * own.shape[0], own.shape[1]
    cols, share = width // 2, (gathered.shape[3] - 8) // 3
    return pl.pallas_call(
        functools.partial(project_kernel, share),
        grid_spec=pltpu.PrefetchScalarGridSpec(
            num_scalar_prefetch=1,
            grid=(length // (2 * half),),
            in_specs=block_specs(half, width)
            + [pl.BlockSpec(gathered.shape, lambda at, core: (0,) * 5)],
            out_specs=pl.BlockSpec((2 * half, 3 * cols), lambda at, core: (at, 0)),
            scratch_shapes=[pltpu.VMEM((8, cols), jnp.float32)],
        ),
        out_shape=jax.ShapeDtypeStruct((length, 3 * cols), jnp.bfloat16),
        compiler_params=pltpu.CompilerParams(vmem_limit_bytes=VMEM_LIMIT),
        cost_estimate=pl.CostEstimate(
            flops=6 * length * width * cols, bytes_accessed=10 * length * width, transcendentals=0
        ),
        name="project",
    )(core, own, other, gathered)


def norm(values, gain, shift):
    center = jnp.mean(values, axis=1, keepdims=True)
    offset = values - center
    scale = lax.rsqrt(jnp.mean(offset * offset, axis=1, keepdims=True) + 1e-12)
    unit = offset * scale
    return unit * gain + shift, unit, scale


def norm_back(grad, gain, unit, scale):
    inner = grad * gain
    mean = jnp.mean(inner, axis=1, keepdims=True)
    return scale * (inner - mean - unit * jnp.mean(inner * unit, axis=1, keepdims=True))


def feed_kernel(
    kept, index_ref, context_ref, tokens_ref, cotangent_ref, small_ref, weights_ref, *refs
):
    feed_rows(context_ref, tokens_ref, cotangent_ref, small_ref, weights_ref, *refs[kept:])


def feed_rows(
    context_ref, tokens_ref, cotangent_ref, small_ref, weights_ref,
    out_ref, active_ref, grad_down_ref, grad_up_ref, hidden_ref, res_ref, attended_ref, context_grad_ref, sum_ref,
    weight_ref, vector_ref, slope_ref, sems,
):
    devices, _, share, width = weights_ref.shape
    fold = active_ref.shape[1] // width
    group = devices // fold
    step = pl.program_id(0)
    f32, bf16 = jnp.float32, jnp.bfloat16

    def copy(unit):
        if unit <= fold:
            return pltpu.make_async_copy(weights_ref.at[:, unit], weight_ref.at[unit], sems.at[unit])
        first = group * (unit - 1 - fold)
        return pltpu.make_async_copy(
            weights_ref.at[pl.ds(first, group), pl.ds(1 + fold, fold)],
            weight_ref.at[unit].reshape(group, fold, share, width),
            sems.at[unit],
        )

    @pl.when(step == 0)
    def _():
        for unit in range(1 + 2 * fold):
            copy(unit).start()
        sum_ref[...] = jnp.zeros_like(sum_ref)
        for entry in range(7):
            times = fold if entry == 1 else 1
            vector_ref[entry : entry + 1, : times * width] = unspread(
                small_ref, 0, 2 + entry, times * width, times * share
            )

    def ready(unit):
        @pl.when(step == 0)
        def _():
            copy(unit).wait()

    def weight(unit):
        return weight_ref[unit].reshape(width, width)

    def vector(entry, low=0):
        return vector_ref[entry : entry + 1, low : low + width]

    def add_sum(entry, value):
        sum_ref[entry : entry + 1, :] += jnp.sum(value, axis=0, keepdims=True)

    ready(0)
    attended = dot_f32(context_ref[...], weight(0), NN) + vector(0)
    hidden, unit_one, scale_one = norm(tokens_ref[...].astype(f32) + attended, vector(3), vector(4))
    hidden_low = hidden.astype(bf16)
    hidden_ref[...] = hidden_low
    down = vector(2)
    for at in range(fold):
        low = at * width
        ready(1 + at)
        up = dot_f32(hidden_low, weight(1 + at), NN) + vector(1, low)
        square = up * up
        tanh = jnp.tanh(0.7978845608 * up * (1.0 + 0.044715 * square))
        half = 0.5 * (1.0 + tanh)
        active = (up * half).astype(bf16)
        rise = (0.5 * 0.7978845608) * up * (1.0 - tanh * tanh)
        slope_ref[at] = half + rise * (1.0 + (3 * 0.044715) * square)
        active_ref[:, low : low + width] = active
        ready(1 + fold + at)
        down = down + dot_f32(active, weight(1 + fold + at), NN)
    out, unit_two, scale_two = norm(hidden + down, vector(5), vector(6))
    out_ref[...] = out.astype(bf16)
    cotangent = cotangent_ref[...].astype(f32)
    add_sum(4, cotangent * unit_two)
    add_sum(5, cotangent)
    grad = norm_back(cotangent, vector(5), unit_two, scale_two)
    grad_down = grad.astype(bf16)
    grad_down_ref[...] = grad_down
    add_sum(1, grad_down.astype(f32))
    for at in range(fold):
        low = at * width
        grad_active = dot_f32(grad_down, weight(1 + fold + at), NT)
        grad_up = (grad_active * slope_ref[at]).astype(bf16)
        grad_up_ref[:, low : low + width] = grad_up
        add_sum(6 + at, grad_up.astype(f32))
        grad = grad + dot_f32(grad_up, weight(1 + at), NT)
    add_sum(2, grad * unit_one)
    add_sum(3, grad)
    res_one = norm_back(grad, vector(3), unit_one, scale_one)
    res_ref[...] = res_one
    grad_attended = res_one.astype(bf16)
    attended_ref[...] = grad_attended
    add_sum(0, grad_attended.astype(f32))
    context_grad_ref[...] = dot_f32(grad_attended, weight(0), NT).astype(bf16)


def feed(index, context, tokens, cotangent, gathered, second, kept, tile):
    rows, width = context.shape
    seqs = tokens.shape[0]
    devices, units, share, _ = second.shape
    fold = (units - 1) // 2
    thin = pl.BlockSpec((tile, width), lambda at, index: (at, 0))
    placed = pl.BlockSpec((None, tile, width), lambda at, index: (index[0], at, 0))
    wide = pl.BlockSpec((tile, fold * width), lambda at, index: (at, 0))
    sums = (6 + fold + 7) // 8 * 8

    def like(columns, dtype):
        return jax.ShapeDtypeStruct((rows, columns), dtype)

    bf16, f32 = jnp.bfloat16, jnp.float32
    return pl.pallas_call(
        functools.partial(feed_kernel, len(kept)),
        grid_spec=pltpu.PrefetchScalarGridSpec(
            num_scalar_prefetch=1,
            grid=(rows // tile,),
            in_specs=[
                thin,
                placed,
                placed,
                pl.BlockSpec(
                    gathered.shape[:3] + (8, width // 2),
                    lambda at, index: (0, 0, 0, 3 * share // 8, 0),
                ),
                pl.BlockSpec(memory_space=pl.ANY),
            ]
            + [pl.BlockSpec(memory_space=pl.ANY)] * len(kept),
            out_specs=[placed, wide, thin, wide, thin, thin, thin, thin]
            + [pl.BlockSpec((sums, width), lambda at, index: (0, 0))],
            scratch_shapes=[
                pltpu.VMEM((units, devices, share, width), bf16),
                pltpu.VMEM((8, fold * width), f32),
                pltpu.VMEM((fold, tile, width), f32),
                pltpu.SemaphoreType.DMA((units,)),
            ],
        ),
        out_shape=[
            jax.ShapeDtypeStruct((seqs, rows, width), bf16),
            like(fold * width, bf16),
            like(width, bf16),
            like(fold * width, bf16),
            like(width, bf16),
            like(width, f32),
            like(width, bf16),
            like(width, bf16),
            jax.ShapeDtypeStruct((sums, width), f32),
        ],
        input_output_aliases={6: 0} if kept else {},
        compiler_params=pltpu.CompilerParams(vmem_limit_bytes=VMEM_LIMIT),
        cost_estimate=pl.CostEstimate(
            flops=4 * rows * width * width * (1 + 2 * fold),
            bytes_accessed=rows * width * (20 + 4 * fold) + 2 * units * width * width,
            transcendentals=rows * width * fold,
        ),
        name="feed",
    )(index, context, tokens, cotangent, gathered, second, *kept)


TN = ((0,), (0,))


def weight_grad_kernel(parts, *refs):
    groups = [refs[at * parts : (at + 1) * parts] for at in range(7)]
    active, grad_down, hidden, grad_up, context, attended, sums = groups
    out_ref, block_ref, small_ref, sems = refs[7 * parts :]
    devices, units, share, width = out_ref.shape
    fold = (units - 2) // 2
    group = devices // fold
    step = pl.program_id(0)
    slot = lax.rem(step, 2)

    def column_copy(unit, slot):
        return pltpu.make_async_copy(block_ref.at[slot], out_ref.at[:, unit], sems.at[slot])

    def row_copy(at, slot):
        return pltpu.make_async_copy(
            block_ref.at[slot].reshape(group, fold, share, width),
            out_ref.at[pl.ds(group * at, group), pl.ds(1 + fold, fold)],
            sems.at[slot],
        )

    def small_copy():
        return pltpu.make_async_copy(small_ref, out_ref.at[:, 1 + 2 * fold], sems.at[2])

    def store(left, right, slot):
        total = None
        for one, other in zip(left, right):
            part = dot_f32(one[...], other[...], TN)
            total = part if total is None else total + part
        block_ref[slot] = total.astype(block_ref.dtype).reshape(devices, share, width)

    @pl.when(step >= 2)
    def _():
        column_copy(0, slot).wait()

    @pl.when(step == 0)
    def _():
        total = sums[0][...]
        for item in sums[1:]:
            total = total + item[...]
        pad = jnp.zeros((share - total.shape[0], width), jnp.float32)
        lines = jnp.concatenate([total, pad], axis=0).astype(small_ref.dtype)
        small_ref[...] = jnp.broadcast_to(lines[None], small_ref.shape)
        small_copy().start()
        store(context, attended, 0)
        column_copy(0, 0).start()

    @pl.when((step >= 1) & (step <= fold))
    def _():
        store(hidden, grad_up, slot)
        column_copy(step, slot).start()

    @pl.when(step > fold)
    def _():
        store(active, grad_down, slot)
        row_copy(step - 1 - fold, slot).start()

    @pl.when(step == 2 * fold)
    def _():
        small_copy().wait()
        column_copy(0, 0).wait()
        column_copy(0, 1).wait()


def weight_grads(parts, devices):
    rows, width = parts[0][4].shape
    fold = parts[0][0].shape[1] // width
    share, units = width // devices, 2 + 2 * fold
    whole = pl.BlockSpec((rows, width), lambda at: (0, 0))
    active = pl.BlockSpec((rows, width), lambda at: (0, jnp.maximum(at - 1 - fold, 0)))
    up = pl.BlockSpec((rows, width), lambda at: (0, jnp.clip(at - 1, 0, fold - 1)))
    sums = pl.BlockSpec(parts[0][6].shape, lambda at: (0, 0))
    specs = [active, whole, whole, up, whole, whole, sums]
    return pl.pallas_call(
        functools.partial(weight_grad_kernel, len(parts)),
        grid=(1 + 2 * fold,),
        in_specs=[spec for spec in specs for _ in parts],
        out_specs=pl.BlockSpec(memory_space=pl.ANY),
        scratch_shapes=[
            pltpu.VMEM((2, devices, share, width), jnp.bfloat16),
            pltpu.VMEM((devices, share, width), jnp.bfloat16),
            pltpu.SemaphoreType.DMA((3,)),
        ],
        out_shape=jax.ShapeDtypeStruct((devices, units, share, width), jnp.bfloat16),
        compiler_params=pltpu.CompilerParams(vmem_limit_bytes=VMEM_LIMIT),
        cost_estimate=pl.CostEstimate(
            flops=2 * len(parts) * rows * width * width * (1 + 2 * fold),
            bytes_accessed=2 * (len(parts) * rows + width) * width * units,
            transcendentals=0,
        ),
        name="weight_grads",
    )(*[part[at] for at in range(7) for part in parts])


def own_grads_kernel(
    core_ref, query_ref, key_ref, value_ref, own_ref, other_ref, out_ref, sum_ref, bias_ref
):
    devices, high, wide = out_ref.shape
    cols, share = wide // 3, high - 8
    step = pl.program_id(0)

    @pl.when(step == 0)
    def _():
        sum_ref[...] = jnp.zeros_like(sum_ref)
        bias_ref[...] = jnp.zeros_like(bias_ref)

    tokens = block_rows(core_ref, own_ref, other_ref)
    for at, grad_ref in enumerate((query_ref, key_ref, value_ref)):
        grad = grad_ref[...]
        here = slice(at * cols, (at + 1) * cols)
        sum_ref[:, here] += dot_f32(tokens, grad, TN)
        bias_ref[0:1, here] += jnp.sum(grad.astype(jnp.float32), axis=0, keepdims=True)

    @pl.when(step == pl.num_programs(0) - 1)
    def _():
        out_ref[:, :share, :] = sum_ref[...].astype(out_ref.dtype).reshape(devices, share, wide)
        bias = bias_ref[...].astype(out_ref.dtype)
        out_ref[:, share:, :] = jnp.broadcast_to(bias[None], (devices, 8, wide))


def own_grads(core, grads, own, other, devices, half):
    length, width = 2 * own.shape[0], own.shape[1]
    share, wide = width // devices, 3 * (width // 2)
    grad_spec = pl.BlockSpec((2 * half, wide // 3), lambda at, core: (at, 0))
    return pl.pallas_call(
        own_grads_kernel,
        grid_spec=pltpu.PrefetchScalarGridSpec(
            num_scalar_prefetch=1,
            grid=(length // (2 * half),),
            in_specs=[grad_spec] * 3 + block_specs(half, width),
            out_specs=pl.BlockSpec((devices, share + 8, wide), lambda at, core: (0, 0, 0)),
            scratch_shapes=[
                pltpu.VMEM((width, wide), jnp.float32),
                pltpu.VMEM((8, wide), jnp.float32),
            ],
        ),
        out_shape=jax.ShapeDtypeStruct((devices, share + 8, wide), jnp.bfloat16),
        compiler_params=pltpu.CompilerParams(vmem_limit_bytes=VMEM_LIMIT),
        cost_estimate=pl.CostEstimate(
            flops=2 * length * width * wide, bytes_accessed=6 * length * width, transcendentals=0
        ),
        name="own_grads",
    )(core, *grads, own, other)


def tokens_grad_kernel(
    share, core_ref, query_ref, key_ref, value_ref, gathered_ref, own_ref, other_ref
):
    total = None
    for at, grad_ref in enumerate((query_ref, key_ref, value_ref)):
        part = dot_f32(grad_ref[...], own_weight(gathered_ref, at, share), NT)
        total = part if total is None else total + part
    half = own_ref.shape[0]
    total = total.astype(own_ref.dtype)
    first = core_ref[0] == 0
    own_ref[...] = jnp.where(first, total[:half], total[half:])
    other_ref[...] = jnp.where(first, total[half:], total[:half])


def tokens_grads(core, grads, gathered, half):
    length, width = grads[0].shape[0], 2 * gathered.shape[4]
    cols, share = width // 2, (gathered.shape[3] - 8) // 3
    rows = jax.ShapeDtypeStruct((length // 2, width), jnp.bfloat16)
    return pl.pallas_call(
        functools.partial(tokens_grad_kernel, share),
        grid_spec=pltpu.PrefetchScalarGridSpec(
            num_scalar_prefetch=1,
            grid=(length // (2 * half),),
            in_specs=[pl.BlockSpec((2 * half, cols), lambda at, core: (at, 0))] * 3
            + [pl.BlockSpec(gathered.shape, lambda at, core: (0,) * 5)],
            out_specs=block_specs(half, width),
        ),
        out_shape=[rows, rows],
        compiler_params=pltpu.CompilerParams(vmem_limit_bytes=VMEM_LIMIT),
        cost_estimate=pl.CostEstimate(
            flops=6 * length * width * cols, bytes_accessed=6 * length * width, transcendentals=0
        ),
        name="tokens_grads",
    )(core, *grads, gathered)


def body(
    tokens,
    cotangent,
    lengths,
    query_weight,
    key_weight,
    value_weight,
    output_weight,
    up_weight,
    down_weight,
    query_bias,
    value_bias,
    output_bias,
    up_bias,
    down_bias,
    attn_gain,
    attn_shift,
    ffn_gain,
    ffn_shift,
):
    seqs, stretch, width = tokens.shape
    rows = seqs * stretch
    n_pair, n_core, n_blk = (lax.axis_size(axis) for axis in ALL)
    devices = n_pair * n_core * n_blk
    pair, core, blk = (lax.axis_index(axis) for axis in ALL)
    half, cols = stretch // 2, width // 2
    own_rows = n_blk * half
    share = query_weight.shape[0]
    fold = up_weight.shape[1] // width
    bf16, f32 = jnp.bfloat16, jnp.float32

    def table(step, back):
        moves = []
        for pair in range(n_pair):
            for src_core in range(n_core):
                for src in range(n_blk):
                    piece = src ^ step
                    sender = (pair * n_core + src_core) * n_blk + src
                    target = (pair * n_core + piece % 2) * n_blk + seqs * src_core + piece // 2
                    moves.append((target, sender) if back else (sender, target))
        return moves

    def move(array, step, back=False):
        return lax.ppermute(array, ALL, table(step, back))

    def after(array, *others):
        return lax.optimization_barrier((array, others))[0]

    def other_core(array):
        return lax.ppermute(array, "core", [(0, 1), (1, 0)])

    def columns(array, which):
        return lax.dynamic_slice_in_dim(array, which * cols, cols, axis=-1)

    def swap(flip, one, two):
        return jnp.where(flip, two, one), jnp.where(flip, one, two)

    def ordered(me, items):
        bit = 1
        while bit < len(items):
            flip = (me & bit) != 0
            items = [jnp.where(flip, items[at ^ bit], items[at]) for at in range(len(items))]
            bit *= 2
        return items

    def others(array, axis, size):
        return [
            lax.ppermute(array, axis, [(at, at ^ step) for at in range(size)])
            for step in range(1, size)
        ]

    which = jnp.reshape(core, (1,)).astype(jnp.int32)
    mine, theirs, second = pack(
        which,
        (query_weight, key_weight, value_weight, output_weight, up_weight, down_weight),
        (query_bias, value_bias, output_bias, up_bias, down_bias)
        + (attn_gain, attn_shift, ffn_gain, ffn_shift),
    )
    gathered = jnp.stack(swap(core == 1, mine, other_core(theirs)))
    gathered = jnp.stack(ordered(blk, [gathered] + others(gathered, "blk", n_blk)))
    tokens_moved = after(tokens, gathered)
    seconds = lax.all_gather(second, "blk", axis=0)
    pieces = tokens_moved.reshape(n_blk, half, width)
    arrived = [
        move(lax.dynamic_index_in_dim(pieces, blk ^ step, 0, keepdims=False), step)
        for step in range(n_blk)
    ]
    terms, arrived[:2] = lax.optimization_barrier(
        ([gathered] + others(gathered, "pair", n_pair), arrived[:2])
    )
    gathered = jnp.stack(ordered(pair, terms))
    second = lax.all_gather(after(seconds, gathered), ("pair", "core"), axis=0)
    second = second.reshape((devices,) + second.shape[2:])
    both = jnp.concatenate(swap(core == 1, lengths, other_core(lengths)))
    own_length = lax.dynamic_index_in_dim(both, blk, 0, keepdims=False)

    parts = n_blk // 2
    piece = 2 * (blk % seqs) + core
    info = jnp.stack(
        [own_length] + [(piece ^ (at // 2)) * stretch + at % 2 * half for at in range(2 * n_blk)]
    ).astype(jnp.int32)
    own_tokens = after(jnp.concatenate(arrived, axis=0), gathered, info)
    other_tokens = other_core(own_tokens)
    odd = blk % 2 == 1

    def after_all(items, *others):
        return lax.optimization_barrier((items, others))[0]

    qkv = project(which, own_tokens, other_tokens, gathered, half)
    attended, returning = [], []
    for part in range(parts):
        query_side = after(qkv, attended[-1]) if part else qkv
        attended.append(attend(query_side, info, part, parts, 512, 512))
        low = attended[-1][0]
        returning.append(
            [move(low[at * stretch : (at + 1) * stretch], 2 * part + at, True) for at in range(2)]
        )

    fed, context, context_grads, kept = [], [], [], ()
    for part in range(parts):
        moved = after_all(returning[part], fed[-1] if part else attended[-1])
        context.append(jnp.concatenate(swap(odd, *moved), axis=1))
        index = jnp.reshape((blk // 2) ^ part, (1,)).astype(jnp.int32)
        fed.append(feed(index, context[part], tokens, cotangent, gathered, second, kept, 256))
        kept = (fed[-1][0],)
        sides = swap(odd, fed[-1][7][:, :cols], fed[-1][7][:, cols:])
        context_grads.append([move(side, 2 * part + at) for at, side in enumerate(sides)])
    layer_out = kept[0]

    early, late = context_grads[0], context_grads[1]
    early, context[0] = lax.optimization_barrier((early, context[0]))
    second_grads = weight_grads(
        [
            (item[1], item[2], item[4], item[3], context[part], item[6], item[8])
            for part, item in enumerate(fed)
        ],
        devices,
    )
    late, second_grads = lax.optimization_barrier((late, second_grads))
    total = second_grads
    second_grads = lax.psum_scatter(
        second_grads.reshape((n_pair * n_core, n_blk) + second_grads.shape[1:]),
        ("pair", "core"),
        scatter_dimension=0,
    )
    context_grads = [jnp.concatenate(early, axis=0), jnp.concatenate(late, axis=0)]
    context_grads[0] = after(context_grads[0], total)
    outs, auxes = [item[1] for item in attended], [item[2] for item in attended]
    grads = attend_back(qkv, context_grads, outs, auxes, info, 0, cols // LANES, 512, 512)

    own, far = tokens_grads(which, grads, gathered, half)
    summed = (own.astype(f32) + other_core(far).astype(f32)).astype(bf16)
    moved = [move(summed[step * half : (step + 1) * half], step, True) for step in range(n_blk)]
    second_grads, summed = lax.optimization_barrier((second_grads, summed))
    second_grads = lax.psum_scatter(second_grads, "blk", scatter_dimension=0)
    first_grads = own_grads(
        which, [after(item, summed) for item in grads], own_tokens, other_tokens, devices, half
    )
    first_grads, moved[0] = lax.optimization_barrier((first_grads, moved[0]))

    def to_sum(array, axis, me, size):
        terms = [lax.dynamic_index_in_dim(array, me, 0, keepdims=False)]
        for step in range(1, size):
            sent = lax.dynamic_index_in_dim(array, me ^ step, 0, keepdims=False)
            terms.append(lax.ppermute(sent, axis, [(at, at ^ step) for at in range(size)]))
        return terms

    def add(terms):
        total = terms[0].astype(f32)
        for term in terms[1:]:
            total += term.astype(f32)
        return total.astype(bf16)

    first_grads = first_grads.reshape(n_pair, n_core, n_blk, share + 8, 3 * cols)
    total = add(to_sum(first_grads, "pair", pair, n_pair))
    moved[1:], total = lax.optimization_barrier((moved[1:], total))
    terms = to_sum(jnp.moveaxis(total, 1, 0), "blk", blk, n_blk)
    returned = []
    for part in range(parts):
        back = jnp.concatenate(swap(odd, *moved[2 * part : 2 * part + 2]), axis=0)
        returned.append(fed[part][5] + back.astype(f32))
    tokens_grad = jnp.stack(swap(blk >= 2, *returned))

    device = (pair * n_core + core) * n_blk + blk

    def own_part(line, size):
        return lax.dynamic_slice_in_dim(line, device * size, size, axis=-1)

    second_grads = second_grads.astype(f32)
    lines = second_grads[1 + 2 * fold]
    own_lines = own_part(lines[:6], share)
    late = (
        second_grads[0],
        jnp.concatenate([second_grads[1 + at] for at in range(fold)], axis=1),
        second_grads[1 + fold : 1 + 2 * fold].reshape(fold * share, width),
        own_part(lines[6 : 6 + fold].reshape(-1), fold * share),
    ) + tuple(own_lines[at] for at in range(6))
    terms, tokens_grad, late = lax.optimization_barrier((terms, tokens_grad, late))
    total = add(terms)
    kept = lax.dynamic_index_in_dim(total, core, 0, keepdims=False)
    crossed = other_core(lax.dynamic_index_in_dim(total, 1 - core, 0, keepdims=False))
    left, right = (item.astype(f32) for item in swap(core == 1, kept, crossed))
    projections = [
        jnp.concatenate([left[:, at : at + cols], right[:, at : at + cols]], axis=1)
        for at in range(0, 3 * cols, cols)
    ]
    return (
        (layer_out, tokens_grad)
        + tuple(item[:share] for item in projections)
        + late[:3]
        + (own_part(projections[0][share], share), own_part(projections[2][share], share))
        + (late[4], late[3], late[5], late[6], late[7], late[8], late[9])
    )


def fits(mesh, tokens, up_weight):
    n_dp, n_blk = mesh.shape["dp"], mesh.shape["blk"]
    batch, length, width = tokens.shape
    if n_dp % 2 or n_dp & (n_dp - 1) or batch % n_dp or 2 * (batch // n_dp) != n_blk or n_blk != 4:
        return False
    share = width // (n_dp * n_blk)
    fold = up_weight.shape[1] // width
    return (
        width == HEADS * 64
        and width % (4 * LANES // PER_TILE) == 0
        and up_weight.shape[1] == fold * width
        and share * n_dp * n_blk == width
        and share % 8 == 0
        and 16 <= share
        and (8 + fold) * share <= width // 2
        and fold == n_dp // 2
        and length % (16 * n_blk) == 0
        and length % 512 == 0
        and length <= 4096
    )


def solution(mesh):
    n_dp, n_blk = mesh.shape["dp"], mesh.shape["blk"]

    def step(*args):
        spread = ("dp", "blk")
        one, use = ring_body, mesh
        where = {"dp": "dp", "blk": "blk", spread: spread}
        if fits(mesh, args[0], args[7]):
            one, use = body, Mesh(mesh.devices.reshape(n_dp // 2, 2, n_blk), ALL)
            where = {"dp": ("pair", "core"), "blk": "blk", spread: ALL}
        block = P(where["dp"], where["blk"], None)
        matrix = P(where[spread], None)
        vector = P(where[spread])
        return jax.shard_map(
            one,
            mesh=use,
            in_specs=(block, block, P(where["dp"])) + (matrix,) * 6 + (vector,) * 9,
            out_specs=(block, block) + (matrix,) * 6 + (vector,) * 9,
            check_vma=False,
        )(*args)

    return step
```

```python
import functools

import jax
import jax.numpy as jnp
from jax import lax
from jax.experimental import pallas as pl
from jax.experimental.pallas import tpu as pltpu
from jax.sharding import Mesh
from jax.sharding import PartitionSpec as P

HEADS = 12
LANES = 128
PER_TILE = 2
SCORE_SCALE = 0.125 * 1.4426950408889634
MASKED = -1e30
ALL = ("pair", "core", "blk")
VMEM_LIMIT = 56 << 20


def shifted(array, axis, by):
    length = lax.axis_size(axis)
    return lax.ppermute(array, axis, [(i, (i + by) % length) for i in range(length)])


def matmul(left, right):
    return jnp.dot(left, right, preferred_element_type=jnp.float32)


def times_trans(left, right):
    return lax.dot_general(
        left, right, (((1,), (1,)), ((), ())), preferred_element_type=jnp.float32
    )


def trans_times(left, right):
    return lax.dot_general(
        left, right, (((0,), (0,)), ((), ())), preferred_element_type=jnp.float32
    )


def layer_norm(values, gain, shift):
    center = jnp.mean(values, axis=-1, keepdims=True)
    offset = values - center
    spread = jnp.mean(offset * offset, axis=-1, keepdims=True)
    return offset * lax.rsqrt(spread + 1e-12) * gain + shift


def gelu_tanh(values):
    return jax.nn.gelu(values, approximate=True)


def ring_body(
    tokens,
    cotangent,
    lengths,
    query_weight,
    key_weight,
    value_weight,
    output_weight,
    up_weight,
    down_weight,
    query_bias,
    value_bias,
    output_bias,
    up_bias,
    down_bias,
    attn_gain,
    attn_shift,
    ffn_gain,
    ffn_shift,
):
    seqs, stretch, width = tokens.shape
    rows = seqs * stretch
    heads = HEADS
    head = width // heads
    gathered = (
        lax.all_gather(query_weight, ("dp", "blk"), axis=0, tiled=True),
        lax.all_gather(key_weight, ("dp", "blk"), axis=0, tiled=True),
        lax.all_gather(value_weight, ("dp", "blk"), axis=0, tiled=True),
        lax.all_gather(output_weight, ("dp", "blk"), axis=0, tiled=True),
        lax.all_gather(up_weight, ("dp", "blk"), axis=0, tiled=True),
        lax.all_gather(down_weight, ("dp", "blk"), axis=0, tiled=True),
        lax.all_gather(query_bias, ("dp", "blk"), axis=0, tiled=True),
        lax.all_gather(value_bias, ("dp", "blk"), axis=0, tiled=True),
        lax.all_gather(output_bias, ("dp", "blk"), axis=0, tiled=True),
        lax.all_gather(up_bias, ("dp", "blk"), axis=0, tiled=True),
        lax.all_gather(down_bias, ("dp", "blk"), axis=0, tiled=True),
        lax.all_gather(attn_gain, ("dp", "blk"), axis=0, tiled=True),
        lax.all_gather(attn_shift, ("dp", "blk"), axis=0, tiled=True),
        lax.all_gather(ffn_gain, ("dp", "blk"), axis=0, tiled=True),
        lax.all_gather(ffn_shift, ("dp", "blk"), axis=0, tiled=True),
    )
    query_full, key_full, value_full, output_full, upper_full, lower_full = gathered[:6]
    (
        bias_query,
        bias_value,
        bias_output,
        bias_upper,
        bias_lower,
        gain_one,
        shift_one,
        gain_two,
        shift_two,
    ) = [item.astype(jnp.float32) for item in gathered[6:]]
    flat = tokens.reshape(rows, width)
    queries = (matmul(flat, query_full) + bias_query).astype(jnp.bfloat16)
    keys_own = matmul(flat, key_full).astype(jnp.bfloat16)
    values_own = (matmul(flat, value_full) + bias_value).astype(jnp.bfloat16)
    query_heads = queries.reshape(seqs, stretch, heads, head)
    own_block = lax.axis_index("blk")
    cycle_size = lax.axis_size("blk")
    start = jnp.int32(0)
    key_piece = lax.all_gather(keys_own.reshape(seqs, stretch, width), "blk", axis=1, tiled=True)
    value_piece = lax.all_gather(
        values_own.reshape(seqs, stretch, width), "blk", axis=1, tiled=True
    )
    count = key_piece.shape[1]
    span = min(count, stretch)
    row_max = jnp.full((seqs, stretch, heads), -1e30, jnp.float32)
    row_total = jnp.zeros((seqs, stretch, heads), jnp.float32)
    accum = jnp.zeros((seqs, stretch, heads, head), jnp.float32)
    for part_no in range(count // span):
        key_heads = key_piece[:, part_no * span : (part_no + 1) * span].reshape(
            seqs, span, heads, head
        )
        value_heads = value_piece[:, part_no * span : (part_no + 1) * span].reshape(
            seqs, span, heads, head
        )
        positions = start + part_no * span + jnp.arange(span, dtype=jnp.int32)
        valid = positions[None, :] < lengths[:, None]
        scores = (
            jnp.einsum(
                "sqhd,skhd->sqhk", query_heads, key_heads, preferred_element_type=jnp.float32
            )
            * 0.125
        )
        scores = jnp.where(valid[:, None, None, :], scores, -jnp.inf)
        new_max = jnp.maximum(row_max, jnp.max(scores, axis=-1))
        expo = jnp.exp(scores - new_max[..., None])
        factor = jnp.exp(row_max - new_max)
        row_total = row_total * factor + jnp.sum(expo, axis=-1)
        accum = accum * factor[..., None] + jnp.einsum(
            "sqhk,skhd->sqhd",
            expo.astype(jnp.bfloat16),
            value_heads,
            preferred_element_type=jnp.float32,
        )
        row_max = new_max
    row_max, row_total, accum = (row_max, row_total, accum)
    log_total = row_max + jnp.log(row_total)
    context_full = accum / row_total[..., None]
    context = context_full.reshape(rows, width).astype(jnp.bfloat16)
    attended = matmul(context, output_full) + bias_output
    hidden, norm_one_back = jax.vjp(
        layer_norm, flat.astype(jnp.float32) + attended, gain_one, shift_one
    )
    hidden_low = hidden.astype(jnp.bfloat16)
    upward = matmul(hidden_low, upper_full) + bias_upper
    active_full, gelu_back = jax.vjp(gelu_tanh, upward)
    active = active_full.astype(jnp.bfloat16)
    downward = matmul(active, lower_full) + bias_lower
    output_full32, norm_two_back = jax.vjp(layer_norm, hidden + downward, gain_two, shift_two)
    layer_out = output_full32.astype(jnp.bfloat16).reshape(seqs, stretch, width)
    query_back, key_back, value_back, output_back, upper_back, lower_back = (
        lax.all_gather(query_weight, ("dp", "blk"), axis=0, tiled=True),
        lax.all_gather(key_weight, ("dp", "blk"), axis=0, tiled=True),
        lax.all_gather(value_weight, ("dp", "blk"), axis=0, tiled=True),
        lax.all_gather(output_weight, ("dp", "blk"), axis=0, tiled=True),
        lax.all_gather(up_weight, ("dp", "blk"), axis=0, tiled=True),
        lax.all_gather(down_weight, ("dp", "blk"), axis=0, tiled=True),
    )
    grad_outer = cotangent.reshape(rows, width).astype(jnp.float32)
    grad_res_two, grad_gain_two, grad_shift_two = norm_two_back(grad_outer)
    grad_down = grad_res_two.astype(jnp.bfloat16)
    grad_lower_bias = jnp.sum(grad_down, axis=0, dtype=jnp.float32)
    grad_lower = trans_times(active, grad_down)
    grad_active = times_trans(grad_down, lower_back)
    (grad_upward,) = gelu_back(grad_active)
    grad_up = grad_upward.astype(jnp.bfloat16)
    grad_upper_bias = jnp.sum(grad_up, axis=0, dtype=jnp.float32)
    grad_upper = trans_times(hidden_low, grad_up)
    grad_hidden = grad_res_two + times_trans(grad_up, upper_back)
    grad_res_one, grad_gain_one, grad_shift_one = norm_one_back(grad_hidden)
    grad_attended = grad_res_one.astype(jnp.bfloat16)
    grad_output_bias = jnp.sum(grad_attended, axis=0, dtype=jnp.float32)
    grad_output = trans_times(context, grad_attended)
    grad_context = times_trans(grad_attended, output_back).astype(jnp.bfloat16)
    context_grad_heads = grad_context.reshape(seqs, stretch, heads, head)
    delta = jnp.sum(context_grad_heads.astype(jnp.float32) * context_full, axis=-1)

    def contribute(key_value, source, pair_grad, query_grad):
        key_heads = key_value[0]
        value_heads = key_value[1]
        positions = source * stretch + jnp.arange(stretch, dtype=jnp.int32)
        valid = positions[None, :] < lengths[:, None]
        scores = (
            jnp.einsum(
                "sqhd,skhd->sqhk", query_heads, key_heads, preferred_element_type=jnp.float32
            )
            * 0.125
        )
        probs = jnp.where(valid[:, None, None, :], jnp.exp(scores - log_total[..., None]), 0.0)
        grad_probs = jnp.einsum(
            "sqhd,skhd->sqhk", context_grad_heads, value_heads, preferred_element_type=jnp.float32
        )
        grad_scores = (probs * (grad_probs - delta[..., None])).astype(jnp.bfloat16)
        query_grad = (
            query_grad
            + jnp.einsum(
                "sqhk,skhd->sqhd", grad_scores, key_heads, preferred_element_type=jnp.float32
            )
            * 0.125
        )
        key_part = (
            jnp.einsum(
                "sqhk,sqhd->skhd", grad_scores, query_heads, preferred_element_type=jnp.float32
            )
            * 0.125
        )
        value_part = jnp.einsum(
            "sqhk,sqhd->skhd",
            probs.astype(jnp.bfloat16),
            context_grad_heads,
            preferred_element_type=jnp.float32,
        )
        pair_grad = pair_grad + jnp.stack([key_part, value_part])
        return (pair_grad, query_grad)

    def rotate_grads(pair_grad):
        return shifted(pair_grad.astype(jnp.bfloat16), "blk", 1).astype(pair_grad.dtype)

    key_value_own = jnp.stack(
        [
            keys_own.reshape(seqs, stretch, heads, head),
            values_own.reshape(seqs, stretch, heads, head),
        ]
    )
    pair_grad, query_grad = contribute(
        key_value_own,
        own_block,
        jnp.zeros((2, seqs, stretch, heads, head), jnp.float32),
        jnp.zeros((seqs, stretch, heads, head), jnp.float32),
    )

    def cycle_turn(turn, state):
        key_value_now, pair_now, query_now = state
        key_value_now = shifted(key_value_now, "blk", 1)
        pair_now = rotate_grads(pair_now)
        source = (own_block - turn) % cycle_size
        pair_now, query_now = contribute(key_value_now, source, pair_now, query_now)
        return (key_value_now, pair_now, query_now)

    final_state = lax.fori_loop(1, cycle_size, cycle_turn, (key_value_own, pair_grad, query_grad))
    pair_home = rotate_grads(final_state[1])
    grad_queries = final_state[2].reshape(rows, width).astype(jnp.bfloat16)
    grad_keys = pair_home[0].reshape(rows, width).astype(jnp.bfloat16)
    grad_values = pair_home[1].reshape(rows, width).astype(jnp.bfloat16)
    grad_query = trans_times(flat, grad_queries)
    grad_key = trans_times(flat, grad_keys)
    grad_value = trans_times(flat, grad_values)
    grad_query_bias = jnp.sum(grad_queries, axis=0, dtype=jnp.float32)
    grad_value_bias = jnp.sum(grad_values, axis=0, dtype=jnp.float32)
    tokens_grad = (
        grad_res_one
        + times_trans(grad_queries, query_back)
        + times_trans(grad_keys, key_back)
        + times_trans(grad_values, value_back)
    ).reshape(seqs, stretch, width)
    shares = (
        lax.psum_scatter(grad_query, ("dp", "blk"), scatter_dimension=0, tiled=True),
        lax.psum_scatter(grad_key, ("dp", "blk"), scatter_dimension=0, tiled=True),
        lax.psum_scatter(grad_value, ("dp", "blk"), scatter_dimension=0, tiled=True),
        lax.psum_scatter(grad_output, ("dp", "blk"), scatter_dimension=0, tiled=True),
        lax.psum_scatter(grad_upper, ("dp", "blk"), scatter_dimension=0, tiled=True),
        lax.psum_scatter(grad_lower, ("dp", "blk"), scatter_dimension=0, tiled=True),
        lax.psum_scatter(grad_query_bias, ("dp", "blk"), scatter_dimension=0, tiled=True),
        lax.psum_scatter(grad_value_bias, ("dp", "blk"), scatter_dimension=0, tiled=True),
        lax.psum_scatter(grad_output_bias, ("dp", "blk"), scatter_dimension=0, tiled=True),
        lax.psum_scatter(grad_upper_bias, ("dp", "blk"), scatter_dimension=0, tiled=True),
        lax.psum_scatter(grad_lower_bias, ("dp", "blk"), scatter_dimension=0, tiled=True),
        lax.psum_scatter(grad_gain_one, ("dp", "blk"), scatter_dimension=0, tiled=True),
        lax.psum_scatter(grad_shift_one, ("dp", "blk"), scatter_dimension=0, tiled=True),
        lax.psum_scatter(grad_gain_two, ("dp", "blk"), scatter_dimension=0, tiled=True),
        lax.psum_scatter(grad_shift_two, ("dp", "blk"), scatter_dimension=0, tiled=True),
    )
    return (layer_out, tokens_grad) + tuple(shares)


def dot_f32(left, right, dims):
    return lax.dot_general(left, right, (dims, ((), ())), preferred_element_type=jnp.float32)


NT = ((1,), (1,))
NN = ((1,), (0,))


def split_three(values):
    high = values.astype(jnp.bfloat16).astype(jnp.float32)
    rest = values - high
    mid = rest.astype(jnp.bfloat16).astype(jnp.float32)
    return high, mid, rest - mid


def spread_three(lane, base, values, into):
    for step, part in enumerate(split_three(values)):
        into = jnp.where(lane == base + step, part, into)
    return into


def fill_keys(info_ref, keys, values, key_aug, value_aug, value_fill, chunk):
    length = keys.shape[0]
    lane = lax.broadcasted_iota(jnp.int32, (chunk, LANES), 1)
    row = lax.broadcasted_iota(jnp.int32, (chunk, LANES), 0)
    for part in range(length // chunk):
        at = slice(part * chunk, (part + 1) * chunk)
        off = (lane == 3) & (row + info_ref[1 + part] >= info_ref[0])
        mask = jnp.where(off, MASKED, 0.0)
        for one in range(PER_TILE):
            mine = lane // (LANES // PER_TILE) == one
            base = 4 * one
            minus = (lane >= base) & (lane < base + 3)
            key_aug[one, at, :LANES] = jnp.where(mine, keys[at], jnp.zeros((), keys.dtype))
            key_aug[one, at, LANES:] = jnp.where(minus, -1.0, mask).astype(jnp.bfloat16)
            value_aug[one, at, :LANES] = jnp.where(mine, values[at], jnp.zeros((), keys.dtype))
            if value_fill:
                value_aug[one, at, LANES:] = jnp.ones((chunk, LANES), jnp.bfloat16)
            else:
                value_aug[one, at, LANES:] = jnp.where(minus, -1.0, 0.0).astype(jnp.bfloat16)


def attend_kernel(
    span, info_ref, query_ref, key_ref, value_ref, near_ref, far_ref, out_ref, aux_ref, key_aug, value_aug
):
    length = key_ref.shape[0]
    tile = query_ref.shape[0]
    lane = lax.broadcasted_iota(jnp.int32, (1, LANES), 1)

    fill_keys(info_ref, key_ref, value_ref, key_aug, value_aug, True, length // 8)

    one_lane = jnp.where(lane == 3, 1.0, 0.0)
    flag = jnp.broadcast_to(one_lane.astype(jnp.bfloat16), (tile, LANES))
    query = jnp.concatenate([query_ref[...], flag], axis=1)
    pieces = [slice(at, at + span) for at in range(0, length, span)]
    scores, peaks = [], []
    for one in range(PER_TILE):
        peak = None
        row = []
        for at in pieces:
            score = dot_f32(query, key_aug[one, at], NT)
            row.append(score)
            for low in range(0, span, LANES):
                part = score[:, low : low + LANES]
                peak = part if peak is None else jnp.maximum(peak, part)
        scores.append(row)
        peaks.append(jnp.max(peak, axis=1, keepdims=True))
    out = None
    aux = one_lane
    for one in range(PER_TILE):
        total = None
        for at, score in zip(pieces, scores[one]):
            expo = jnp.exp2((score - peaks[one]) * SCORE_SCALE).astype(jnp.bfloat16)
            part = dot_f32(expo, value_aug[one, at], NN)
            total = part if total is None else total + part
        weight = total[:, LANES:]
        part = total[:, :LANES] / weight
        out = part if out is None else out + part
        log_total = jnp.log2(weight) * (1.0 / SCORE_SCALE) + peaks[one]
        aux = spread_three(lane, 4 * one, log_total, aux)
    low = out.astype(jnp.bfloat16)
    near_ref[...] = low[: tile // 2]
    far_ref[...] = low[tile // 2 :]
    out_ref[...] = out
    aux_ref[...] = aux.astype(jnp.bfloat16)


def attend(qkv, info, part, parts, span):
    length, width = qkv.shape[0], qkv.shape[1] // 3
    tiles, rows = width // LANES, length // parts
    half = pl.BlockSpec((rows // 2, LANES), lambda pair: (0, pair))
    whole = pl.BlockSpec((rows, LANES), lambda pair: (0, pair))
    block = jax.ShapeDtypeStruct((rows // 2, width), jnp.bfloat16)
    return pl.pallas_call(
        functools.partial(attend_kernel, span),
        grid=(tiles,),
        in_specs=[
            pl.BlockSpec(memory_space=pltpu.SMEM),
            pl.BlockSpec((rows, LANES), lambda pair: (part, pair)),
            pl.BlockSpec((length, LANES), lambda pair: (0, tiles + pair)),
            pl.BlockSpec((length, LANES), lambda pair: (0, 2 * tiles + pair)),
        ],
        out_specs=[half, half, whole, whole],
        out_shape=[
            block,
            block,
            jax.ShapeDtypeStruct((rows, width), jnp.float32),
            jax.ShapeDtypeStruct((rows, width), jnp.bfloat16),
        ],
        scratch_shapes=[pltpu.VMEM((PER_TILE, length, 2 * LANES), jnp.bfloat16)] * 2,
        compiler_params=pltpu.CompilerParams(vmem_limit_bytes=VMEM_LIMIT),
        cost_estimate=pl.CostEstimate(
            flops=16 * rows * length * width,
            bytes_accessed=12 * length * width,
            transcendentals=rows * length * width // 64,
        ),
        name="attend",
    )(info, qkv, qkv, qkv)


def attend_back_kernel(span, counts, info_ref, query_ref, key_ref, value_ref, *refs):
    groups = []
    for count in counts:
        groups.append(refs[:count])
        refs = refs[count:]
    query_grad_ref, key_grad_ref, value_grad_ref, key_aug, value_aug, key_cols, key_sum, value_sum = refs
    length = key_ref.shape[0]
    tile = query_ref.shape[0]
    wide = LANES // PER_TILE
    lane = lax.broadcasted_iota(jnp.int32, (1, LANES), 1)
    step = pl.program_id(1)

    @pl.when(step == 0)
    def _():
        fill_keys(info_ref, key_ref, value_ref, key_aug, value_aug, False, length // 8)
        key_cols[...] = key_ref[...].T
        key_sum[...] = jnp.zeros_like(key_sum)
        value_sum[...] = jnp.zeros_like(value_sum)

    taken = []
    for group in groups:
        per_piece = length // len(group) // tile
        item = group[0][...]
        for at in range(1, len(group)):
            item = jnp.where(step >= at * per_piece, group[at][...], item)
        taken.append(item)
    grad, out, aux = taken
    plain = query_ref[...]
    query = jnp.concatenate([plain, aux], axis=1)
    product = grad.astype(jnp.float32) * out
    delta = jnp.zeros((tile, LANES), jnp.float32)
    for one in range(PER_TILE):
        own = jnp.sum(jnp.where(lane // wide == one, product, 0.0), axis=1, keepdims=True)
        delta = spread_three(lane, 4 * one, own, delta)
    grad_aug = jnp.concatenate([grad, delta.astype(jnp.bfloat16)], axis=1)
    nothing = jnp.zeros((), plain.dtype)
    query_rows = []
    for one in range(PER_TILE):
        mine = lane // wide == one
        query_own = jnp.where(mine, plain, nothing)
        grad_own = jnp.where(mine, grad, nothing)
        total = None
        for low in range(0, length, span):
            at = slice(low, low + span)
            score = dot_f32(key_aug[one, at], query, NT)
            grad_probs = dot_f32(value_aug[one, at], grad_aug, NT)
            probs = jnp.exp2(score * SCORE_SCALE)
            grad_scores = (probs * grad_probs).astype(jnp.bfloat16)
            value_sum[at] += dot_f32(probs.astype(jnp.bfloat16), grad_own, NN)
            key_sum[at] += dot_f32(grad_scores, query_own, NN)
            part = dot_f32(key_cols[wide * one : wide * (one + 1), at], grad_scores, NN)
            total = part if total is None else total + part
        query_rows.append(total)
    query_grad_ref[...] = (jnp.concatenate(query_rows, axis=0).T * 0.125).astype(jnp.bfloat16)

    @pl.when(step == pl.num_programs(1) - 1)
    def _():
        key_grad_ref[...] = (key_sum[...] * 0.125).astype(jnp.bfloat16)
        value_grad_ref[...] = value_sum[...].astype(jnp.bfloat16)


def attend_back(qkv, grads, outs, auxes, info, tile, span):
    length, width = qkv.shape[0], qkv.shape[1] // 3
    tiles = width // LANES

    def piece_specs(pieces):
        per_piece = length // len(pieces) // tile
        return [
            pl.BlockSpec(
                (tile, LANES),
                lambda pair, at, low=low: (jnp.clip(at - low, 0, per_piece - 1), pair),
            )
            for low in range(0, per_piece * len(pieces), per_piece)
        ]

    result = jax.ShapeDtypeStruct((length, width), jnp.bfloat16)
    whole = pl.BlockSpec((length, LANES), lambda pair, at: (0, pair))
    query_spec = pl.BlockSpec((tile, LANES), lambda pair, at: (at, pair))
    return pl.pallas_call(
        functools.partial(attend_back_kernel, span, (len(grads), len(outs), len(auxes))),
        grid=(tiles, length // tile),
        in_specs=[
            pl.BlockSpec(memory_space=pltpu.SMEM),
            query_spec,
            pl.BlockSpec((length, LANES), lambda pair, at: (0, tiles + pair)),
            pl.BlockSpec((length, LANES), lambda pair, at: (0, 2 * tiles + pair)),
        ]
        + piece_specs(grads)
        + piece_specs(outs)
        + piece_specs(auxes),
        out_specs=[query_spec, whole, whole],
        out_shape=[result] * 3,
        scratch_shapes=[pltpu.VMEM((PER_TILE, length, 2 * LANES), jnp.bfloat16)] * 2
        + [pltpu.VMEM((LANES, length), jnp.bfloat16)]
        + [pltpu.VMEM((length, LANES), jnp.float32)] * 2,
        compiler_params=pltpu.CompilerParams(vmem_limit_bytes=VMEM_LIMIT),
        cost_estimate=pl.CostEstimate(
            flops=40 * length * length * width,
            bytes_accessed=22 * length * width,
            transcendentals=length * length * width // 64,
        ),
        name="attend_back",
    )(info, qkv, qkv, qkv, *grads, *outs, *auxes)


def pack_kernel(count, core_ref, *refs):
    query, key, value, output, up, down = refs[:6]
    vectors = refs[6 : 6 + count]
    mine_ref, theirs_ref, second_ref, held_ref, wide_ref = refs[6 + count : 11 + count]
    lines = refs[11 + count : 11 + 2 * count]
    sems, line_sems = refs[11 + 2 * count :]
    share, width = query.shape
    cols = width // 2
    fold = up.shape[1] // width
    copies = [
        pltpu.make_async_copy(item, held_ref.at[at], sems.at[at])
        for at, item in enumerate((query, key, value))
    ]
    copies += [
        pltpu.make_async_copy(item, line, line_sems.at[at])
        for at, (item, line) in enumerate(zip(vectors, lines))
    ]
    later = [pltpu.make_async_copy(output, second_ref.at[0], sems.at[3])]
    for at in range(fold):
        later.append(
            pltpu.make_async_copy(
                down.at[pl.ds(at * share, share)],
                second_ref.at[1 + fold + at],
                sems.at[4 + at],
            )
        )
    later.append(pltpu.make_async_copy(up, wide_ref, sems.at[4 + fold]))
    for copy in copies + later:
        copy.start()
    for copy in copies:
        copy.wait()
    first_core = core_ref[0] == 0
    for at in range(3):
        left, right = held_ref[at, :, :cols], held_ref[at, :, cols:]
        here = slice(at * share, (at + 1) * share)
        mine_ref[here] = jnp.where(first_core, left, right)
        theirs_ref[here] = jnp.where(first_core, right, left)
    for ref in (mine_ref, theirs_ref):
        ref[3 * share :] = jnp.zeros((8, cols), ref.dtype)
        for at, line in enumerate(lines):
            low = at // 8 * LANES
            ref[3 * share + at % 8, low : low + line.shape[0]] = line[...]
    for copy in later:
        copy.wait()
    for at in range(fold):
        second_ref[1 + at] = wide_ref[:, at * width : (at + 1) * width]


def pack(core, matrices, vectors):
    share, width = matrices[0].shape
    cols = width // 2
    fold = matrices[4].shape[1] // width
    count = len(vectors)
    block = jax.ShapeDtypeStruct((3 * share + 8, cols), jnp.bfloat16)
    inside = pl.BlockSpec(memory_space=pltpu.VMEM)
    return pl.pallas_call(
        functools.partial(pack_kernel, count),
        in_specs=[pl.BlockSpec(memory_space=pltpu.SMEM)]
        + [pl.BlockSpec(memory_space=pl.ANY)] * (6 + count),
        out_specs=[inside] * 3,
        out_shape=[
            block,
            block,
            jax.ShapeDtypeStruct((1 + 2 * fold, share, width), jnp.bfloat16),
        ],
        scratch_shapes=[pltpu.VMEM((3, share, width), jnp.bfloat16)]
        + [pltpu.VMEM(matrices[4].shape, jnp.bfloat16)]
        + [pltpu.VMEM(item.shape, item.dtype) for item in vectors]
        + [pltpu.SemaphoreType.DMA((5 + fold,)), pltpu.SemaphoreType.DMA((count,))],
        compiler_params=pltpu.CompilerParams(vmem_limit_bytes=VMEM_LIMIT),
        name="pack",
    )(core, *matrices, *vectors)


def by_device(gathered_ref, rows, columns=slice(None)):
    n_pair, n_blk, n_core = gathered_ref.shape[:3]
    return jnp.concatenate(
        [
            gathered_ref[pair, blk, core, rows, columns]
            for pair in range(n_pair)
            for core in range(n_core)
            for blk in range(n_blk)
        ],
        axis=0,
    )


def unspread(gathered_ref, first_row, entry, width, share):
    low, row = entry // 8 * LANES, first_row + entry % 8
    pieces = by_device(gathered_ref, slice(row, row + 1), slice(low, low + LANES))
    lane = lax.broadcasted_iota(jnp.int32, (LANES, width), 1)
    row = lax.broadcasted_iota(jnp.int32, (LANES, width), 0)
    pick = jnp.where(lax.rem(lane, share) == row, 1.0, 0.0).astype(jnp.bfloat16)
    spread = dot_f32(pieces, pick, NN)
    lane = lax.broadcasted_iota(jnp.int32, (pieces.shape[0], width), 1)
    row = lax.broadcasted_iota(jnp.int32, (pieces.shape[0], width), 0)
    return jnp.sum(jnp.where(lax.div(lane, share) == row, spread, 0.0), axis=0, keepdims=True)


def own_weight(gathered_ref, at, share):
    return by_device(gathered_ref, slice(at * share, (at + 1) * share))


def block_rows(core_ref, own_ref, other_ref):
    own, other = own_ref[...], other_ref[...]
    first = core_ref[0] == 0
    return jnp.concatenate([jnp.where(first, own, other), jnp.where(first, other, own)], axis=0)


def block_specs(half, width):
    return [
        pl.BlockSpec((half, width), lambda at, core: (at, 0)),
        pl.BlockSpec((half, width), lambda at, core: (at + 1 - 2 * lax.rem(at, 2), 0)),
    ]


def project_kernel(share, core_ref, own_ref, other_ref, gathered_ref, out_ref, bias_ref):
    cols = gathered_ref.shape[4]

    @pl.when(pl.program_id(0) == 0)
    def _():
        for at in range(2):
            whole = unspread(gathered_ref, 3 * share, at, 2 * cols, share)
            bias_ref[at : at + 1, :] = jnp.where(
                core_ref[0] == 0, whole[:, :cols], whole[:, cols:]
            )

    tokens = block_rows(core_ref, own_ref, other_ref)
    for at, bias in enumerate((0, None, 1)):
        part = dot_f32(tokens, own_weight(gathered_ref, at, share), NN)
        if bias is not None:
            part = part + bias_ref[bias : bias + 1, :]
        out_ref[:, at * cols : (at + 1) * cols] = part.astype(out_ref.dtype)


def project(core, own, other, gathered, half):
    length, width = 2 * own.shape[0], own.shape[1]
    cols, share = width // 2, (gathered.shape[3] - 8) // 3
    return pl.pallas_call(
        functools.partial(project_kernel, share),
        grid_spec=pltpu.PrefetchScalarGridSpec(
            num_scalar_prefetch=1,
            grid=(length // (2 * half),),
            in_specs=block_specs(half, width)
            + [pl.BlockSpec(gathered.shape, lambda at, core: (0,) * 5)],
            out_specs=pl.BlockSpec((2 * half, 3 * cols), lambda at, core: (at, 0)),
            scratch_shapes=[pltpu.VMEM((8, cols), jnp.float32)],
        ),
        out_shape=jax.ShapeDtypeStruct((length, 3 * cols), jnp.bfloat16),
        compiler_params=pltpu.CompilerParams(vmem_limit_bytes=VMEM_LIMIT),
        cost_estimate=pl.CostEstimate(
            flops=6 * length * width * cols, bytes_accessed=10 * length * width, transcendentals=0
        ),
        name="project",
    )(core, own, other, gathered)


def norm(values, gain, shift):
    center = jnp.mean(values, axis=1, keepdims=True)
    offset = values - center
    scale = lax.rsqrt(jnp.mean(offset * offset, axis=1, keepdims=True) + 1e-12)
    unit = offset * scale
    return unit * gain + shift, unit, scale


def norm_back(grad, gain, unit, scale):
    inner = grad * gain
    mean = jnp.mean(inner, axis=1, keepdims=True)
    return scale * (inner - mean - unit * jnp.mean(inner * unit, axis=1, keepdims=True))


def feed_kernel(
    kept, index_ref, even_ref, odd_ref, tokens_ref, cotangent_ref, small_ref, weights_ref, *refs
):
    feed_rows(
        index_ref[1] == 1, even_ref, odd_ref, tokens_ref, cotangent_ref, small_ref, weights_ref, *refs[kept:]
    )


def feed_rows(
    odd, even_ref, odd_ref, tokens_ref, cotangent_ref, small_ref, weights_ref,
    out_ref, active_ref, grad_down_ref, grad_up_ref, hidden_ref, res_ref, attended_ref, context_ref,
    even_grad_ref, odd_grad_ref, sum_ref,
    weight_ref, vector_ref, slope_ref, sems,
):
    devices, _, share, width = weights_ref.shape
    fold = active_ref.shape[1] // width
    group = devices // fold
    step = pl.program_id(0)
    f32, bf16 = jnp.float32, jnp.bfloat16

    def copy(unit):
        if unit <= fold:
            return pltpu.make_async_copy(weights_ref.at[:, unit], weight_ref.at[unit], sems.at[unit])
        first = group * (unit - 1 - fold)
        return pltpu.make_async_copy(
            weights_ref.at[pl.ds(first, group), pl.ds(1 + fold, fold)],
            weight_ref.at[unit].reshape(group, fold, share, width),
            sems.at[unit],
        )

    order = [0]
    for at in range(fold):
        order += [1 + at, 1 + fold + at]
    ahead = 3

    @pl.when(step == 0)
    def _():
        for unit in order[:ahead]:
            copy(unit).start()
        sum_ref[...] = jnp.zeros_like(sum_ref)
        for entry in range(7):
            times = fold if entry == 1 else 1
            vector_ref[entry : entry + 1, : times * width] = unspread(
                small_ref, 0, 2 + entry, times * width, times * share
            )

    def ready(unit):
        @pl.when(step == 0)
        def _():
            copy(unit).wait()
            after = order.index(unit) + ahead
            if after < len(order):
                copy(order[after]).start()

    def weight(unit):
        return weight_ref[unit].reshape(width, width)

    def vector(entry, low=0):
        return vector_ref[entry : entry + 1, low : low + width]

    def add_sum(entry, value):
        sum_ref[entry : entry + 1, :] += jnp.sum(value, axis=0, keepdims=True)

    even, other = even_ref[...], odd_ref[...]
    context = jnp.concatenate([jnp.where(odd, other, even), jnp.where(odd, even, other)], axis=1)
    context_ref[...] = context
    ready(0)
    attended = dot_f32(context, weight(0), NN) + vector(0)
    hidden, unit_one, scale_one = norm(tokens_ref[...].astype(f32) + attended, vector(3), vector(4))
    hidden_low = hidden.astype(bf16)
    hidden_ref[...] = hidden_low
    down = vector(2)
    for at in range(fold):
        low = at * width
        ready(1 + at)
        up = dot_f32(hidden_low, weight(1 + at), NN) + vector(1, low)
        square = up * up
        tanh = jnp.tanh(0.7978845608 * up * (1.0 + 0.044715 * square))
        half = 0.5 * (1.0 + tanh)
        active = (up * half).astype(bf16)
        rise = (0.5 * 0.7978845608) * up * (1.0 - tanh * tanh)
        slope_ref[at] = half + rise * (1.0 + (3 * 0.044715) * square)
        active_ref[:, low : low + width] = active
        ready(1 + fold + at)
        down = down + dot_f32(active, weight(1 + fold + at), NN)
    out, unit_two, scale_two = norm(hidden + down, vector(5), vector(6))
    out_ref[...] = out.astype(bf16)
    cotangent = cotangent_ref[...].astype(f32)
    add_sum(4, cotangent * unit_two)
    add_sum(5, cotangent)
    grad = norm_back(cotangent, vector(5), unit_two, scale_two)
    grad_down = grad.astype(bf16)
    grad_down_ref[...] = grad_down
    add_sum(1, grad_down.astype(f32))
    for at in range(fold):
        low = at * width
        grad_active = dot_f32(grad_down, weight(1 + fold + at), NT)
        grad_up = (grad_active * slope_ref[at]).astype(bf16)
        grad_up_ref[:, low : low + width] = grad_up
        add_sum(6 + at, grad_up.astype(f32))
        grad = grad + dot_f32(grad_up, weight(1 + at), NT)
    add_sum(2, grad * unit_one)
    add_sum(3, grad)
    res_one = norm_back(grad, vector(3), unit_one, scale_one)
    res_ref[...] = res_one
    grad_attended = res_one.astype(bf16)
    attended_ref[...] = grad_attended
    add_sum(0, grad_attended.astype(f32))
    context_grad = dot_f32(grad_attended, weight(0), NT).astype(bf16)
    left, right = context_grad[:, : width // 2], context_grad[:, width // 2 :]
    even_grad_ref[...] = jnp.where(odd, right, left)
    odd_grad_ref[...] = jnp.where(odd, left, right)


def feed(index, even, other, tokens, cotangent, gathered, second, kept, tile):
    rows, width = even.shape[0], 2 * even.shape[1]
    seqs = tokens.shape[0]
    devices, units, share, _ = second.shape
    fold = (units - 1) // 2
    thin = pl.BlockSpec((tile, width), lambda at, index: (at, 0))
    placed = pl.BlockSpec((None, tile, width), lambda at, index: (index[0], at, 0))
    side = pl.BlockSpec((tile, width // 2), lambda at, index: (at, 0))
    wide = pl.BlockSpec((tile, fold * width), lambda at, index: (at, 0))
    sums = (6 + fold + 7) // 8 * 8

    def like(columns, dtype):
        return jax.ShapeDtypeStruct((rows, columns), dtype)

    bf16, f32 = jnp.bfloat16, jnp.float32
    return pl.pallas_call(
        functools.partial(feed_kernel, len(kept)),
        grid_spec=pltpu.PrefetchScalarGridSpec(
            num_scalar_prefetch=1,
            grid=(rows // tile,),
            in_specs=[
                side,
                side,
                placed,
                placed,
                pl.BlockSpec(
                    gathered.shape[:3] + (8, width // 2),
                    lambda at, index: (0, 0, 0, 3 * share // 8, 0),
                ),
                pl.BlockSpec(memory_space=pl.ANY),
            ]
            + [pl.BlockSpec(memory_space=pl.ANY)] * len(kept),
            out_specs=[placed, wide, thin, wide, thin, thin, thin, thin, side, side]
            + [pl.BlockSpec((sums, width), lambda at, index: (0, 0))],
            scratch_shapes=[
                pltpu.VMEM((units, devices, share, width), bf16),
                pltpu.VMEM((8, fold * width), f32),
                pltpu.VMEM((fold, tile, width), f32),
                pltpu.SemaphoreType.DMA((units,)),
            ],
        ),
        out_shape=[
            jax.ShapeDtypeStruct((seqs, rows, width), bf16),
            like(fold * width, bf16),
            like(width, bf16),
            like(fold * width, bf16),
            like(width, bf16),
            like(width, f32),
            like(width, bf16),
            like(width, bf16),
            like(width // 2, bf16),
            like(width // 2, bf16),
            jax.ShapeDtypeStruct((sums, width), f32),
        ],
        input_output_aliases={7: 0} if kept else {},
        compiler_params=pltpu.CompilerParams(vmem_limit_bytes=VMEM_LIMIT),
        cost_estimate=pl.CostEstimate(
            flops=4 * rows * width * width * (1 + 2 * fold),
            bytes_accessed=rows * width * (20 + 4 * fold) + 2 * units * width * width,
            transcendentals=rows * width * fold,
        ),
        name="feed",
    )(index, even, other, tokens, cotangent, gathered, second, *kept)


TN = ((0,), (0,))


def weight_grad_kernel(parts, *refs):
    groups = [refs[at * parts : (at + 1) * parts] for at in range(6)]
    active, grad_down, hidden, grad_up, context, attended = groups
    out_ref, block_ref, sems = refs[6 * parts :]
    devices, units, share, width = out_ref.shape
    fold = (units - 1) // 2
    group = devices // fold
    step = pl.program_id(0)
    slot = lax.rem(step, 2)

    def column_copy(unit, slot):
        return pltpu.make_async_copy(block_ref.at[slot], out_ref.at[:, unit], sems.at[slot])

    def row_copy(at, slot):
        return pltpu.make_async_copy(
            block_ref.at[slot].reshape(group, fold, share, width),
            out_ref.at[pl.ds(group * at, group), pl.ds(1 + fold, fold)],
            sems.at[slot],
        )

    def store(left, right, slot):
        total = None
        for one, other in zip(left, right):
            part = dot_f32(one[...], other[...], TN)
            total = part if total is None else total + part
        block_ref[slot] = total.astype(block_ref.dtype).reshape(devices, share, width)

    @pl.when(step >= 2)
    def _():
        column_copy(0, slot).wait()

    @pl.when(step == 0)
    def _():
        store(context, attended, 0)
        column_copy(0, 0).start()

    @pl.when((step >= 1) & (step <= fold))
    def _():
        store(hidden, grad_up, slot)
        column_copy(step, slot).start()

    @pl.when(step > fold)
    def _():
        store(active, grad_down, slot)
        row_copy(step - 1 - fold, slot).start()

    @pl.when(step == 2 * fold)
    def _():
        column_copy(0, 0).wait()
        column_copy(0, 1).wait()


def weight_grads(parts, devices):
    rows, width = parts[0][4].shape
    fold = parts[0][0].shape[1] // width
    share, units = width // devices, 1 + 2 * fold
    whole = pl.BlockSpec((rows, width), lambda at: (0, 0))
    active = pl.BlockSpec((rows, width), lambda at: (0, jnp.maximum(at - 1 - fold, 0)))
    up = pl.BlockSpec((rows, width), lambda at: (0, jnp.clip(at - 1, 0, fold - 1)))
    specs = [active, whole, whole, up, whole, whole]
    return pl.pallas_call(
        functools.partial(weight_grad_kernel, len(parts)),
        grid=(1 + 2 * fold,),
        in_specs=[spec for spec in specs for _ in parts],
        out_specs=pl.BlockSpec(memory_space=pl.ANY),
        scratch_shapes=[
            pltpu.VMEM((2, devices, share, width), jnp.bfloat16),
            pltpu.SemaphoreType.DMA((2,)),
        ],
        out_shape=jax.ShapeDtypeStruct((devices, units, share, width), jnp.bfloat16),
        compiler_params=pltpu.CompilerParams(vmem_limit_bytes=VMEM_LIMIT),
        cost_estimate=pl.CostEstimate(
            flops=2 * len(parts) * rows * width * width * (1 + 2 * fold),
            bytes_accessed=2 * (len(parts) * rows + width) * width * units,
            transcendentals=0,
        ),
        name="weight_grads",
    )(*[part[at] for at in range(6) for part in parts])


def own_grads_kernel(
    count, core_ref, query_ref, key_ref, value_ref, own_ref, other_ref, *refs
):
    out_ref, sum_ref, bias_ref = refs[-3:]
    devices, high, wide = out_ref.shape
    cols, share = wide // 3, high - 8
    step = pl.program_id(0)

    @pl.when(step == 0)
    def _():
        sum_ref[...] = jnp.zeros_like(sum_ref)
        bias_ref[...] = jnp.zeros_like(bias_ref)

    tokens = block_rows(core_ref, own_ref, other_ref)
    for at, grad_ref in enumerate((query_ref, key_ref, value_ref)):
        grad = grad_ref[...]
        here = slice(at * cols, (at + 1) * cols)
        sum_ref[:, here] += dot_f32(tokens, grad, TN)
        bias_ref[0:1, here] += jnp.sum(grad.astype(jnp.float32), axis=0, keepdims=True)

    @pl.when(step == pl.num_programs(0) - 1)
    def _():
        out_ref[:, :share, :] = sum_ref[...].astype(out_ref.dtype).reshape(devices, share, wide)
        total = refs[0][...]
        for ref in refs[1:-3]:
            total = total + ref[...]
        zero = jnp.zeros((1, cols), jnp.float32)
        bits = [total[at : at + 1, low : low + cols] for at in range(count) for low in (0, cols)]
        bits += [zero] * (21 - len(bits))
        lines = [jnp.concatenate(bits[at : at + 3], axis=1) for at in range(0, 21, 3)]
        lines = jnp.concatenate([bias_ref[0:1, :]] + lines, axis=0).astype(out_ref.dtype)
        out_ref[:, share:, :] = jnp.broadcast_to(lines[None], (devices, 8, wide))


def own_grads(core, grads, own, other, sums, count, devices, half):
    length, width = 2 * own.shape[0], own.shape[1]
    share, wide = width // devices, 3 * (width // 2)
    grad_spec = pl.BlockSpec((2 * half, wide // 3), lambda at, core: (at, 0))
    return pl.pallas_call(
        functools.partial(own_grads_kernel, count),
        grid_spec=pltpu.PrefetchScalarGridSpec(
            num_scalar_prefetch=1,
            grid=(length // (2 * half),),
            in_specs=[grad_spec] * 3
            + block_specs(half, width)
            + [pl.BlockSpec(item.shape, lambda at, core: (0, 0)) for item in sums],
            out_specs=pl.BlockSpec((devices, share + 8, wide), lambda at, core: (0, 0, 0)),
            scratch_shapes=[
                pltpu.VMEM((width, wide), jnp.float32),
                pltpu.VMEM((8, wide), jnp.float32),
            ],
        ),
        out_shape=jax.ShapeDtypeStruct((devices, share + 8, wide), jnp.bfloat16),
        compiler_params=pltpu.CompilerParams(vmem_limit_bytes=VMEM_LIMIT),
        cost_estimate=pl.CostEstimate(
            flops=2 * length * width * wide, bytes_accessed=6 * length * width, transcendentals=0
        ),
        name="own_grads",
    )(core, *grads, own, other, *sums)


def tokens_grad_kernel(
    share, core_ref, query_ref, key_ref, value_ref, gathered_ref, own_ref, other_ref
):
    total = None
    for at, grad_ref in enumerate((query_ref, key_ref, value_ref)):
        part = dot_f32(grad_ref[...], own_weight(gathered_ref, at, share), NT)
        total = part if total is None else total + part
    half = own_ref.shape[0]
    total = total.astype(own_ref.dtype)
    first = core_ref[0] == 0
    own_ref[...] = jnp.where(first, total[:half], total[half:])
    other_ref[...] = jnp.where(first, total[half:], total[:half])


def tokens_grads(core, grads, gathered, half):
    length, width = grads[0].shape[0], 2 * gathered.shape[4]
    cols, share = width // 2, (gathered.shape[3] - 8) // 3
    rows = jax.ShapeDtypeStruct((length // 2, width), jnp.bfloat16)
    return pl.pallas_call(
        functools.partial(tokens_grad_kernel, share),
        grid_spec=pltpu.PrefetchScalarGridSpec(
            num_scalar_prefetch=1,
            grid=(length // (2 * half),),
            in_specs=[pl.BlockSpec((2 * half, cols), lambda at, core: (at, 0))] * 3
            + [pl.BlockSpec(gathered.shape, lambda at, core: (0,) * 5)],
            out_specs=block_specs(half, width),
        ),
        out_shape=[rows, rows],
        compiler_params=pltpu.CompilerParams(vmem_limit_bytes=VMEM_LIMIT),
        cost_estimate=pl.CostEstimate(
            flops=6 * length * width * cols, bytes_accessed=6 * length * width, transcendentals=0
        ),
        name="tokens_grads",
    )(core, *grads, gathered)


def body(
    tokens,
    cotangent,
    lengths,
    query_weight,
    key_weight,
    value_weight,
    output_weight,
    up_weight,
    down_weight,
    query_bias,
    value_bias,
    output_bias,
    up_bias,
    down_bias,
    attn_gain,
    attn_shift,
    ffn_gain,
    ffn_shift,
):
    seqs, stretch, width = tokens.shape
    rows = seqs * stretch
    n_pair, n_core, n_blk = (lax.axis_size(axis) for axis in ALL)
    devices = n_pair * n_core * n_blk
    pair, core, blk = (lax.axis_index(axis) for axis in ALL)
    half, cols = stretch // 2, width // 2
    own_rows = n_blk * half
    share = query_weight.shape[0]
    fold = up_weight.shape[1] // width
    bf16, f32 = jnp.bfloat16, jnp.float32

    def table(step, back):
        moves = []
        for pair in range(n_pair):
            for src_core in range(n_core):
                for src in range(n_blk):
                    piece = src ^ step
                    sender = (pair * n_core + src_core) * n_blk + src
                    target = (pair * n_core + piece % 2) * n_blk + seqs * src_core + piece // 2
                    moves.append((target, sender) if back else (sender, target))
        return moves

    def move(array, step, back=False):
        return lax.ppermute(array, ALL, table(step, back))

    def after(array, *others):
        return lax.optimization_barrier((array, others))[0]

    def other_core(array):
        return lax.ppermute(array, "core", [(0, 1), (1, 0)])

    def columns(array, which):
        return lax.dynamic_slice_in_dim(array, which * cols, cols, axis=-1)

    def swap(flip, one, two):
        return jnp.where(flip, two, one), jnp.where(flip, one, two)

    def ordered(me, items):
        bit = 1
        while bit < len(items):
            flip = (me & bit) != 0
            items = [jnp.where(flip, items[at ^ bit], items[at]) for at in range(len(items))]
            bit *= 2
        return items

    def others(array, axis, size):
        return [
            lax.ppermute(array, axis, [(at, at ^ step) for at in range(size)])
            for step in range(1, size)
        ]

    which = jnp.reshape(core, (1,)).astype(jnp.int32)
    mine, theirs, second = pack(
        which,
        (query_weight, key_weight, value_weight, output_weight, up_weight, down_weight),
        (query_bias, value_bias, output_bias, up_bias, down_bias)
        + (attn_gain, attn_shift, ffn_gain, ffn_shift),
    )
    gathered = jnp.stack(swap(core == 1, mine, other_core(theirs)))
    gathered = jnp.stack(ordered(blk, [gathered] + others(gathered, "blk", n_blk)))
    tokens_moved = after(tokens, gathered)
    seconds = lax.all_gather(second, "blk", axis=0)
    pieces = tokens_moved.reshape(n_blk, half, width)
    arrived = [
        move(lax.dynamic_index_in_dim(pieces, blk ^ step, 0, keepdims=False), step)
        for step in range(n_blk)
    ]
    terms, arrived[:2] = lax.optimization_barrier(
        ([gathered] + others(gathered, "pair", n_pair), arrived[:2])
    )
    gathered = jnp.stack(ordered(pair, terms))
    second = lax.all_gather(after(seconds, gathered), ("pair", "core"), axis=0)
    second = second.reshape((devices,) + second.shape[2:])
    both = jnp.concatenate(swap(core == 1, lengths, other_core(lengths)))
    own_length = lax.dynamic_index_in_dim(both, blk, 0, keepdims=False)

    parts = n_blk // 2
    piece = 2 * (blk % seqs) + core
    info = jnp.stack(
        [own_length] + [(piece ^ (at // 2)) * stretch + at % 2 * half for at in range(2 * n_blk)]
    ).astype(jnp.int32)
    own_tokens = after(jnp.concatenate(arrived, axis=0), gathered, info)
    other_tokens = other_core(own_tokens)
    odd = blk % 2 == 1

    def after_all(items, *others):
        return lax.optimization_barrier((items, others))[0]

    qkv = project(which, own_tokens, other_tokens, gathered, half)
    attended, returning = [], []
    for part in range(parts):
        query_side = after(qkv, attended[-1]) if part else qkv
        attended.append(attend(query_side, info, part, parts, 512))
        returning.append([move(attended[-1][at], 2 * part + at, True) for at in range(2)])

    fed, context_grads, kept = [], [], ()
    for part in range(parts):
        even, other = after_all(returning[part], fed[-1] if part else attended[-1])
        index = jnp.stack([(blk // 2) ^ part, blk % 2]).astype(jnp.int32)
        fed.append(feed(index, even, other, tokens, cotangent, gathered, second, kept, 256))
        kept = (fed[-1][0],)
        context_grads.append([move(fed[-1][8 + at], 2 * part + at) for at in range(2)])
    layer_out = kept[0]

    early, late = context_grads[0], context_grads[1]
    early, first_active = lax.optimization_barrier((early, fed[0][1]))
    second_grads = weight_grads(
        [
            (item[1] if part else first_active, item[2], item[4], item[3], item[7], item[6])
            for part, item in enumerate(fed)
        ],
        devices,
    )
    late, second_grads = lax.optimization_barrier((late, second_grads))
    total = second_grads
    second_grads = lax.psum_scatter(
        second_grads.reshape((n_pair * n_core, n_blk) + second_grads.shape[1:]),
        ("pair", "core"),
        scatter_dimension=0,
    )
    early[0] = after(early[0], total)
    outs, auxes = [item[2] for item in attended], [item[3] for item in attended]
    grads = attend_back(qkv, list(early) + list(late), outs, auxes, info, 512, 1024)

    own, far = tokens_grads(which, grads, gathered, half)
    summed = (own.astype(f32) + other_core(far).astype(f32)).astype(bf16)
    moved = [move(summed[step * half : (step + 1) * half], step, True) for step in range(n_blk)]
    second_grads, summed = lax.optimization_barrier((second_grads, summed))
    second_grads = lax.psum_scatter(second_grads, "blk", scatter_dimension=0)
    first_grads = own_grads(
        which,
        [after(item, summed) for item in grads],
        own_tokens,
        other_tokens,
        [item[10] for item in fed],
        6 + fold,
        devices,
        half,
    )
    first_grads, moved[0] = lax.optimization_barrier((first_grads, moved[0]))

    def to_sum(array, axis, me, size):
        terms = [lax.dynamic_index_in_dim(array, me, 0, keepdims=False)]
        for step in range(1, size):
            sent = lax.dynamic_index_in_dim(array, me ^ step, 0, keepdims=False)
            terms.append(lax.ppermute(sent, axis, [(at, at ^ step) for at in range(size)]))
        return terms

    def add(terms):
        total = terms[0].astype(f32)
        for term in terms[1:]:
            total += term.astype(f32)
        return total.astype(bf16)

    first_grads = first_grads.reshape(n_pair, n_core, n_blk, share + 8, 3 * cols)
    total = add(to_sum(first_grads, "pair", pair, n_pair))
    moved[1:], total = lax.optimization_barrier((moved[1:], total))
    terms = to_sum(jnp.moveaxis(total, 1, 0), "blk", blk, n_blk)
    returned = []
    for part in range(parts):
        back = jnp.concatenate(swap(odd, *moved[2 * part : 2 * part + 2]), axis=0)
        returned.append(fed[part][5] + back.astype(f32))
    tokens_grad = jnp.stack(swap(blk >= 2, *returned))

    device = (pair * n_core + core) * n_blk + blk

    def own_part(line, size):
        return lax.dynamic_slice_in_dim(line, device * size, size, axis=-1)

    second_grads = second_grads.astype(f32)
    late = (
        second_grads[0],
        jnp.concatenate([second_grads[1 + at] for at in range(fold)], axis=1),
        second_grads[1 + fold :].reshape(fold * share, width),
    )
    terms, tokens_grad, late = lax.optimization_barrier((terms, tokens_grad, late))
    total = add(terms)
    kept = lax.dynamic_index_in_dim(total, core, 0, keepdims=False)
    crossed = other_core(lax.dynamic_index_in_dim(total, 1 - core, 0, keepdims=False))
    left, right = (item.astype(f32) for item in swap(core == 1, kept, crossed))
    projections = [
        jnp.concatenate([left[:, at : at + cols], right[:, at : at + cols]], axis=1)
        for at in range(0, 3 * cols, cols)
    ]
    lines = (kept[share + 1 :].astype(f32) + crossed[share + 1 :].astype(f32)).reshape(-1)
    own_lines = own_part(lines[: 6 * width].reshape(6, width), share)
    up_line = own_part(lines[6 * width : (6 + fold) * width], fold * share)
    return (
        (layer_out, tokens_grad)
        + tuple(item[:share] for item in projections)
        + late
        + (own_part(projections[0][share], share), own_part(projections[2][share], share))
        + (own_lines[0], up_line, own_lines[1], own_lines[2], own_lines[3], own_lines[4], own_lines[5])
    )


def fits(mesh, tokens, up_weight):
    n_dp, n_blk = mesh.shape["dp"], mesh.shape["blk"]
    batch, length, width = tokens.shape
    if n_dp % 2 or n_dp & (n_dp - 1) or batch % n_dp or 2 * (batch // n_dp) != n_blk or n_blk != 4:
        return False
    share = width // (n_dp * n_blk)
    fold = up_weight.shape[1] // width
    return (
        width == HEADS * 64
        and width % (4 * LANES // PER_TILE) == 0
        and up_weight.shape[1] == fold * width
        and share * n_dp * n_blk == width
        and share % 8 == 0
        and 16 <= share
        and (8 + fold) * share <= width // 2
        and fold == 4
        and length % (16 * n_blk) == 0
        and length % 512 == 0
        and length <= 4096
    )


def solution(mesh):
    n_dp, n_blk = mesh.shape["dp"], mesh.shape["blk"]

    def step(*args):
        spread = ("dp", "blk")
        one, use = ring_body, mesh
        where = {"dp": "dp", "blk": "blk", spread: spread}
        if fits(mesh, args[0], args[7]):
            one, use = body, Mesh(mesh.devices.reshape(n_dp // 2, 2, n_blk), ALL)
            where = {"dp": ("pair", "core"), "blk": "blk", spread: ALL}
        block = P(where["dp"], where["blk"], None)
        matrix = P(where[spread], None)
        vector = P(where[spread])
        return jax.shard_map(
            one,
            mesh=use,
            in_specs=(block, block, P(where["dp"])) + (matrix,) * 6 + (vector,) * 9,
            out_specs=(block, block) + (matrix,) * 6 + (vector,) * 9,
            check_vma=False,
        )(*args)

    return step
```

```python
import functools

import jax
import jax.numpy as jnp
from jax import lax
from jax.experimental import pallas as pl
from jax.experimental.pallas import tpu as pltpu
from jax.sharding import Mesh
from jax.sharding import PartitionSpec as P

HEADS = 12
LANES = 128
PER_TILE = 2
SCORE_SCALE = 0.125 * 1.4426950408889634
MASKED = -1e30
ALL = ("pair", "core", "blk")
VMEM_LIMIT = 56 << 20


def shifted(array, axis, by):
    length = lax.axis_size(axis)
    return lax.ppermute(array, axis, [(i, (i + by) % length) for i in range(length)])


def matmul(left, right):
    return jnp.dot(left, right, preferred_element_type=jnp.float32)


def times_trans(left, right):
    return lax.dot_general(
        left, right, (((1,), (1,)), ((), ())), preferred_element_type=jnp.float32
    )


def trans_times(left, right):
    return lax.dot_general(
        left, right, (((0,), (0,)), ((), ())), preferred_element_type=jnp.float32
    )


def layer_norm(values, gain, shift):
    center = jnp.mean(values, axis=-1, keepdims=True)
    offset = values - center
    spread = jnp.mean(offset * offset, axis=-1, keepdims=True)
    return offset * lax.rsqrt(spread + 1e-12) * gain + shift


def gelu_tanh(values):
    return jax.nn.gelu(values, approximate=True)


def ring_body(
    tokens,
    cotangent,
    lengths,
    query_weight,
    key_weight,
    value_weight,
    output_weight,
    up_weight,
    down_weight,
    query_bias,
    value_bias,
    output_bias,
    up_bias,
    down_bias,
    attn_gain,
    attn_shift,
    ffn_gain,
    ffn_shift,
):
    seqs, stretch, width = tokens.shape
    rows = seqs * stretch
    heads = HEADS
    head = width // heads
    gathered = (
        lax.all_gather(query_weight, ("dp", "blk"), axis=0, tiled=True),
        lax.all_gather(key_weight, ("dp", "blk"), axis=0, tiled=True),
        lax.all_gather(value_weight, ("dp", "blk"), axis=0, tiled=True),
        lax.all_gather(output_weight, ("dp", "blk"), axis=0, tiled=True),
        lax.all_gather(up_weight, ("dp", "blk"), axis=0, tiled=True),
        lax.all_gather(down_weight, ("dp", "blk"), axis=0, tiled=True),
        lax.all_gather(query_bias, ("dp", "blk"), axis=0, tiled=True),
        lax.all_gather(value_bias, ("dp", "blk"), axis=0, tiled=True),
        lax.all_gather(output_bias, ("dp", "blk"), axis=0, tiled=True),
        lax.all_gather(up_bias, ("dp", "blk"), axis=0, tiled=True),
        lax.all_gather(down_bias, ("dp", "blk"), axis=0, tiled=True),
        lax.all_gather(attn_gain, ("dp", "blk"), axis=0, tiled=True),
        lax.all_gather(attn_shift, ("dp", "blk"), axis=0, tiled=True),
        lax.all_gather(ffn_gain, ("dp", "blk"), axis=0, tiled=True),
        lax.all_gather(ffn_shift, ("dp", "blk"), axis=0, tiled=True),
    )
    query_full, key_full, value_full, output_full, upper_full, lower_full = gathered[:6]
    (
        bias_query,
        bias_value,
        bias_output,
        bias_upper,
        bias_lower,
        gain_one,
        shift_one,
        gain_two,
        shift_two,
    ) = [item.astype(jnp.float32) for item in gathered[6:]]
    flat = tokens.reshape(rows, width)
    queries = (matmul(flat, query_full) + bias_query).astype(jnp.bfloat16)
    keys_own = matmul(flat, key_full).astype(jnp.bfloat16)
    values_own = (matmul(flat, value_full) + bias_value).astype(jnp.bfloat16)
    query_heads = queries.reshape(seqs, stretch, heads, head)
    own_block = lax.axis_index("blk")
    cycle_size = lax.axis_size("blk")
    start = jnp.int32(0)
    key_piece = lax.all_gather(keys_own.reshape(seqs, stretch, width), "blk", axis=1, tiled=True)
    value_piece = lax.all_gather(
        values_own.reshape(seqs, stretch, width), "blk", axis=1, tiled=True
    )
    count = key_piece.shape[1]
    span = min(count, stretch)
    row_max = jnp.full((seqs, stretch, heads), -1e30, jnp.float32)
    row_total = jnp.zeros((seqs, stretch, heads), jnp.float32)
    accum = jnp.zeros((seqs, stretch, heads, head), jnp.float32)
    for part_no in range(count // span):
        key_heads = key_piece[:, part_no * span : (part_no + 1) * span].reshape(
            seqs, span, heads, head
        )
        value_heads = value_piece[:, part_no * span : (part_no + 1) * span].reshape(
            seqs, span, heads, head
        )
        positions = start + part_no * span + jnp.arange(span, dtype=jnp.int32)
        valid = positions[None, :] < lengths[:, None]
        scores = (
            jnp.einsum(
                "sqhd,skhd->sqhk", query_heads, key_heads, preferred_element_type=jnp.float32
            )
            * 0.125
        )
        scores = jnp.where(valid[:, None, None, :], scores, -jnp.inf)
        new_max = jnp.maximum(row_max, jnp.max(scores, axis=-1))
        expo = jnp.exp(scores - new_max[..., None])
        factor = jnp.exp(row_max - new_max)
        row_total = row_total * factor + jnp.sum(expo, axis=-1)
        accum = accum * factor[..., None] + jnp.einsum(
            "sqhk,skhd->sqhd",
            expo.astype(jnp.bfloat16),
            value_heads,
            preferred_element_type=jnp.float32,
        )
        row_max = new_max
    row_max, row_total, accum = (row_max, row_total, accum)
    log_total = row_max + jnp.log(row_total)
    context_full = accum / row_total[..., None]
    context = context_full.reshape(rows, width).astype(jnp.bfloat16)
    attended = matmul(context, output_full) + bias_output
    hidden, norm_one_back = jax.vjp(
        layer_norm, flat.astype(jnp.float32) + attended, gain_one, shift_one
    )
    hidden_low = hidden.astype(jnp.bfloat16)
    upward = matmul(hidden_low, upper_full) + bias_upper
    active_full, gelu_back = jax.vjp(gelu_tanh, upward)
    active = active_full.astype(jnp.bfloat16)
    downward = matmul(active, lower_full) + bias_lower
    output_full32, norm_two_back = jax.vjp(layer_norm, hidden + downward, gain_two, shift_two)
    layer_out = output_full32.astype(jnp.bfloat16).reshape(seqs, stretch, width)
    query_back, key_back, value_back, output_back, upper_back, lower_back = (
        lax.all_gather(query_weight, ("dp", "blk"), axis=0, tiled=True),
        lax.all_gather(key_weight, ("dp", "blk"), axis=0, tiled=True),
        lax.all_gather(value_weight, ("dp", "blk"), axis=0, tiled=True),
        lax.all_gather(output_weight, ("dp", "blk"), axis=0, tiled=True),
        lax.all_gather(up_weight, ("dp", "blk"), axis=0, tiled=True),
        lax.all_gather(down_weight, ("dp", "blk"), axis=0, tiled=True),
    )
    grad_outer = cotangent.reshape(rows, width).astype(jnp.float32)
    grad_res_two, grad_gain_two, grad_shift_two = norm_two_back(grad_outer)
    grad_down = grad_res_two.astype(jnp.bfloat16)
    grad_lower_bias = jnp.sum(grad_down, axis=0, dtype=jnp.float32)
    grad_lower = trans_times(active, grad_down)
    grad_active = times_trans(grad_down, lower_back)
    (grad_upward,) = gelu_back(grad_active)
    grad_up = grad_upward.astype(jnp.bfloat16)
    grad_upper_bias = jnp.sum(grad_up, axis=0, dtype=jnp.float32)
    grad_upper = trans_times(hidden_low, grad_up)
    grad_hidden = grad_res_two + times_trans(grad_up, upper_back)
    grad_res_one, grad_gain_one, grad_shift_one = norm_one_back(grad_hidden)
    grad_attended = grad_res_one.astype(jnp.bfloat16)
    grad_output_bias = jnp.sum(grad_attended, axis=0, dtype=jnp.float32)
    grad_output = trans_times(context, grad_attended)
    grad_context = times_trans(grad_attended, output_back).astype(jnp.bfloat16)
    context_grad_heads = grad_context.reshape(seqs, stretch, heads, head)
    delta = jnp.sum(context_grad_heads.astype(jnp.float32) * context_full, axis=-1)

    def contribute(key_value, source, pair_grad, query_grad):
        key_heads = key_value[0]
        value_heads = key_value[1]
        positions = source * stretch + jnp.arange(stretch, dtype=jnp.int32)
        valid = positions[None, :] < lengths[:, None]
        scores = (
            jnp.einsum(
                "sqhd,skhd->sqhk", query_heads, key_heads, preferred_element_type=jnp.float32
            )
            * 0.125
        )
        probs = jnp.where(valid[:, None, None, :], jnp.exp(scores - log_total[..., None]), 0.0)
        grad_probs = jnp.einsum(
            "sqhd,skhd->sqhk", context_grad_heads, value_heads, preferred_element_type=jnp.float32
        )
        grad_scores = (probs * (grad_probs - delta[..., None])).astype(jnp.bfloat16)
        query_grad = (
            query_grad
            + jnp.einsum(
                "sqhk,skhd->sqhd", grad_scores, key_heads, preferred_element_type=jnp.float32
            )
            * 0.125
        )
        key_part = (
            jnp.einsum(
                "sqhk,sqhd->skhd", grad_scores, query_heads, preferred_element_type=jnp.float32
            )
            * 0.125
        )
        value_part = jnp.einsum(
            "sqhk,sqhd->skhd",
            probs.astype(jnp.bfloat16),
            context_grad_heads,
            preferred_element_type=jnp.float32,
        )
        pair_grad = pair_grad + jnp.stack([key_part, value_part])
        return (pair_grad, query_grad)

    def rotate_grads(pair_grad):
        return shifted(pair_grad.astype(jnp.bfloat16), "blk", 1).astype(pair_grad.dtype)

    key_value_own = jnp.stack(
        [
            keys_own.reshape(seqs, stretch, heads, head),
            values_own.reshape(seqs, stretch, heads, head),
        ]
    )
    pair_grad, query_grad = contribute(
        key_value_own,
        own_block,
        jnp.zeros((2, seqs, stretch, heads, head), jnp.float32),
        jnp.zeros((seqs, stretch, heads, head), jnp.float32),
    )

    def cycle_turn(turn, state):
        key_value_now, pair_now, query_now = state
        key_value_now = shifted(key_value_now, "blk", 1)
        pair_now = rotate_grads(pair_now)
        source = (own_block - turn) % cycle_size
        pair_now, query_now = contribute(key_value_now, source, pair_now, query_now)
        return (key_value_now, pair_now, query_now)

    final_state = lax.fori_loop(1, cycle_size, cycle_turn, (key_value_own, pair_grad, query_grad))
    pair_home = rotate_grads(final_state[1])
    grad_queries = final_state[2].reshape(rows, width).astype(jnp.bfloat16)
    grad_keys = pair_home[0].reshape(rows, width).astype(jnp.bfloat16)
    grad_values = pair_home[1].reshape(rows, width).astype(jnp.bfloat16)
    grad_query = trans_times(flat, grad_queries)
    grad_key = trans_times(flat, grad_keys)
    grad_value = trans_times(flat, grad_values)
    grad_query_bias = jnp.sum(grad_queries, axis=0, dtype=jnp.float32)
    grad_value_bias = jnp.sum(grad_values, axis=0, dtype=jnp.float32)
    tokens_grad = (
        grad_res_one
        + times_trans(grad_queries, query_back)
        + times_trans(grad_keys, key_back)
        + times_trans(grad_values, value_back)
    ).reshape(seqs, stretch, width)
    shares = (
        lax.psum_scatter(grad_query, ("dp", "blk"), scatter_dimension=0, tiled=True),
        lax.psum_scatter(grad_key, ("dp", "blk"), scatter_dimension=0, tiled=True),
        lax.psum_scatter(grad_value, ("dp", "blk"), scatter_dimension=0, tiled=True),
        lax.psum_scatter(grad_output, ("dp", "blk"), scatter_dimension=0, tiled=True),
        lax.psum_scatter(grad_upper, ("dp", "blk"), scatter_dimension=0, tiled=True),
        lax.psum_scatter(grad_lower, ("dp", "blk"), scatter_dimension=0, tiled=True),
        lax.psum_scatter(grad_query_bias, ("dp", "blk"), scatter_dimension=0, tiled=True),
        lax.psum_scatter(grad_value_bias, ("dp", "blk"), scatter_dimension=0, tiled=True),
        lax.psum_scatter(grad_output_bias, ("dp", "blk"), scatter_dimension=0, tiled=True),
        lax.psum_scatter(grad_upper_bias, ("dp", "blk"), scatter_dimension=0, tiled=True),
        lax.psum_scatter(grad_lower_bias, ("dp", "blk"), scatter_dimension=0, tiled=True),
        lax.psum_scatter(grad_gain_one, ("dp", "blk"), scatter_dimension=0, tiled=True),
        lax.psum_scatter(grad_shift_one, ("dp", "blk"), scatter_dimension=0, tiled=True),
        lax.psum_scatter(grad_gain_two, ("dp", "blk"), scatter_dimension=0, tiled=True),
        lax.psum_scatter(grad_shift_two, ("dp", "blk"), scatter_dimension=0, tiled=True),
    )
    return (layer_out, tokens_grad) + tuple(shares)


def dot_f32(left, right, dims):
    return lax.dot_general(left, right, (dims, ((), ())), preferred_element_type=jnp.float32)


NT = ((1,), (1,))
NN = ((1,), (0,))


def split_three(values):
    high = values.astype(jnp.bfloat16).astype(jnp.float32)
    rest = values - high
    mid = rest.astype(jnp.bfloat16).astype(jnp.float32)
    return high, mid, rest - mid


def spread_three(lane, base, values, into):
    for step, part in enumerate(split_three(values)):
        into = jnp.where(lane == base + step, part, into)
    return into


def fill_keys(info_ref, keys, values, key_aug, value_aug, value_fill, chunk):
    length = keys.shape[0]
    lane = lax.broadcasted_iota(jnp.int32, (chunk, LANES), 1)
    row = lax.broadcasted_iota(jnp.int32, (chunk, LANES), 0)
    for part in range(length // chunk):
        at = slice(part * chunk, (part + 1) * chunk)
        off = (lane == 3) & (row + info_ref[1 + part] >= info_ref[0])
        mask = jnp.where(off, MASKED, 0.0)
        for one in range(PER_TILE):
            mine = lane // (LANES // PER_TILE) == one
            base = 4 * one
            minus = (lane >= base) & (lane < base + 3)
            key_aug[one, at, :LANES] = jnp.where(mine, keys[at], jnp.zeros((), keys.dtype))
            key_aug[one, at, LANES:] = jnp.where(minus, -1.0, mask).astype(jnp.bfloat16)
            value_aug[one, at, :LANES] = jnp.where(mine, values[at], jnp.zeros((), keys.dtype))
            if value_fill:
                value_aug[one, at, LANES:] = jnp.ones((chunk, LANES), jnp.bfloat16)
            else:
                value_aug[one, at, LANES:] = jnp.where(minus, -1.0, 0.0).astype(jnp.bfloat16)


def attend_kernel(
    span, info_ref, query_ref, key_ref, value_ref, near_ref, far_ref, out_ref, aux_ref, key_aug, value_aug
):
    length = key_ref.shape[0]
    tile = query_ref.shape[0]
    lane = lax.broadcasted_iota(jnp.int32, (1, LANES), 1)

    fill_keys(info_ref, key_ref, value_ref, key_aug, value_aug, True, length // 8)

    one_lane = jnp.where(lane == 3, 1.0, 0.0)
    flag = jnp.broadcast_to(one_lane.astype(jnp.bfloat16), (tile, LANES))
    query = jnp.concatenate([query_ref[...], flag], axis=1)
    pieces = [slice(at, at + span) for at in range(0, length, span)]
    scores, peaks = [], []
    for one in range(PER_TILE):
        peak = None
        row = []
        for at in pieces:
            score = dot_f32(query, key_aug[one, at], NT)
            row.append(score)
            for low in range(0, span, LANES):
                part = score[:, low : low + LANES]
                peak = part if peak is None else jnp.maximum(peak, part)
        scores.append(row)
        peaks.append(jnp.max(peak, axis=1, keepdims=True))
    out = None
    aux = one_lane
    for one in range(PER_TILE):
        total = None
        for at, score in zip(pieces, scores[one]):
            expo = jnp.exp2((score - peaks[one]) * SCORE_SCALE).astype(jnp.bfloat16)
            part = dot_f32(expo, value_aug[one, at], NN)
            total = part if total is None else total + part
        weight = total[:, LANES:]
        part = total[:, :LANES] / weight
        out = part if out is None else out + part
        log_total = jnp.log2(weight) * (1.0 / SCORE_SCALE) + peaks[one]
        aux = spread_three(lane, 4 * one, log_total, aux)
    low = out.astype(jnp.bfloat16)
    near_ref[...] = low[: tile // 2]
    far_ref[...] = low[tile // 2 :]
    out_ref[...] = out
    aux_ref[...] = aux.astype(jnp.bfloat16)


def attend(qkv, info, part, parts, span):
    length, width = qkv.shape[0], qkv.shape[1] // 3
    tiles, rows = width // LANES, length // parts
    half = pl.BlockSpec((rows // 2, LANES), lambda pair: (0, pair))
    whole = pl.BlockSpec((rows, LANES), lambda pair: (0, pair))
    block = jax.ShapeDtypeStruct((rows // 2, width), jnp.bfloat16)
    return pl.pallas_call(
        functools.partial(attend_kernel, span),
        grid=(tiles,),
        in_specs=[
            pl.BlockSpec(memory_space=pltpu.SMEM),
            pl.BlockSpec((rows, LANES), lambda pair: (part, pair)),
            pl.BlockSpec((length, LANES), lambda pair: (0, tiles + pair)),
            pl.BlockSpec((length, LANES), lambda pair: (0, 2 * tiles + pair)),
        ],
        out_specs=[half, half, whole, whole],
        out_shape=[
            block,
            block,
            jax.ShapeDtypeStruct((rows, width), jnp.float32),
            jax.ShapeDtypeStruct((rows, width), jnp.bfloat16),
        ],
        scratch_shapes=[pltpu.VMEM((PER_TILE, length, 2 * LANES), jnp.bfloat16)] * 2,
        compiler_params=pltpu.CompilerParams(vmem_limit_bytes=VMEM_LIMIT),
        cost_estimate=pl.CostEstimate(
            flops=16 * rows * length * width,
            bytes_accessed=12 * length * width,
            transcendentals=rows * length * width // 64,
        ),
        name="attend",
    )(info, qkv, qkv, qkv)


def attend_back_kernel(span, counts, info_ref, query_ref, key_ref, value_ref, *refs):
    groups = []
    for count in counts:
        groups.append(refs[:count])
        refs = refs[count:]
    query_grad_ref, key_grad_ref, value_grad_ref, key_aug, value_aug, key_cols, key_sum, value_sum = refs
    length = key_ref.shape[0]
    tile = query_ref.shape[0]
    wide = LANES // PER_TILE
    lane = lax.broadcasted_iota(jnp.int32, (1, LANES), 1)
    step = pl.program_id(1)

    @pl.when(step == 0)
    def _():
        fill_keys(info_ref, key_ref, value_ref, key_aug, value_aug, False, length // 8)
        key_cols[...] = key_ref[...].T
        key_sum[...] = jnp.zeros_like(key_sum)
        value_sum[...] = jnp.zeros_like(value_sum)

    taken = []
    for group in groups:
        per_piece = length // len(group) // tile
        item = group[0][...]
        for at in range(1, len(group)):
            item = jnp.where(step >= at * per_piece, group[at][...], item)
        taken.append(item)
    grad, out, aux = taken
    plain = query_ref[...]
    query = jnp.concatenate([plain, aux], axis=1)
    product = grad.astype(jnp.float32) * out
    delta = jnp.zeros((tile, LANES), jnp.float32)
    for one in range(PER_TILE):
        own = jnp.sum(jnp.where(lane // wide == one, product, 0.0), axis=1, keepdims=True)
        delta = spread_three(lane, 4 * one, own, delta)
    grad_aug = jnp.concatenate([grad, delta.astype(jnp.bfloat16)], axis=1)
    nothing = jnp.zeros((), plain.dtype)
    query_rows = []
    for one in range(PER_TILE):
        mine = lane // wide == one
        query_own = jnp.where(mine, plain, nothing)
        grad_own = jnp.where(mine, grad, nothing)
        total = None
        for low in range(0, length, span):
            at = slice(low, low + span)
            score = dot_f32(key_aug[one, at], query, NT)
            grad_probs = dot_f32(value_aug[one, at], grad_aug, NT)
            probs = jnp.exp2(score * SCORE_SCALE)
            grad_scores = (probs * grad_probs).astype(jnp.bfloat16)
            value_sum[at] += dot_f32(probs.astype(jnp.bfloat16), grad_own, NN)
            key_sum[at] += dot_f32(grad_scores, query_own, NN)
            part = dot_f32(key_cols[wide * one : wide * (one + 1), at], grad_scores, NN)
            total = part if total is None else total + part
        query_rows.append(total)
    query_grad_ref[...] = (jnp.concatenate(query_rows, axis=0).T * 0.125).astype(jnp.bfloat16)

    @pl.when(step == pl.num_programs(1) - 1)
    def _():
        key_grad_ref[...] = (key_sum[...] * 0.125).astype(jnp.bfloat16)
        value_grad_ref[...] = value_sum[...].astype(jnp.bfloat16)


def attend_back(qkv, grads, outs, auxes, info, tile, span):
    length, width = qkv.shape[0], qkv.shape[1] // 3
    tiles = width // LANES

    def piece_specs(pieces):
        per_piece = length // len(pieces) // tile
        return [
            pl.BlockSpec(
                (tile, LANES),
                lambda pair, at, low=low: (jnp.clip(at - low, 0, per_piece - 1), pair),
            )
            for low in range(0, per_piece * len(pieces), per_piece)
        ]

    result = jax.ShapeDtypeStruct((length, width), jnp.bfloat16)
    whole = pl.BlockSpec((length, LANES), lambda pair, at: (0, pair))
    query_spec = pl.BlockSpec((tile, LANES), lambda pair, at: (at, pair))
    return pl.pallas_call(
        functools.partial(attend_back_kernel, span, (len(grads), len(outs), len(auxes))),
        grid=(tiles, length // tile),
        in_specs=[
            pl.BlockSpec(memory_space=pltpu.SMEM),
            query_spec,
            pl.BlockSpec((length, LANES), lambda pair, at: (0, tiles + pair)),
            pl.BlockSpec((length, LANES), lambda pair, at: (0, 2 * tiles + pair)),
        ]
        + piece_specs(grads)
        + piece_specs(outs)
        + piece_specs(auxes),
        out_specs=[query_spec, whole, whole],
        out_shape=[result] * 3,
        scratch_shapes=[pltpu.VMEM((PER_TILE, length, 2 * LANES), jnp.bfloat16)] * 2
        + [pltpu.VMEM((LANES, length), jnp.bfloat16)]
        + [pltpu.VMEM((length, LANES), jnp.float32)] * 2,
        compiler_params=pltpu.CompilerParams(vmem_limit_bytes=VMEM_LIMIT),
        cost_estimate=pl.CostEstimate(
            flops=40 * length * length * width,
            bytes_accessed=22 * length * width,
            transcendentals=length * length * width // 64,
        ),
        name="attend_back",
    )(info, qkv, qkv, qkv, *grads, *outs, *auxes)


def pack_kernel(count, core_ref, *refs):
    query, key, value, output, up, down = refs[:6]
    vectors = refs[6 : 6 + count]
    mine_ref, theirs_ref, second_ref, held_ref, wide_ref = refs[6 + count : 11 + count]
    lines = refs[11 + count : 11 + 2 * count]
    sems, line_sems = refs[11 + 2 * count :]
    share, width = query.shape
    cols = width // 2
    fold = up.shape[1] // width
    copies = [
        pltpu.make_async_copy(item, held_ref.at[at], sems.at[at])
        for at, item in enumerate((query, key, value))
    ]
    copies += [
        pltpu.make_async_copy(item, line, line_sems.at[at])
        for at, (item, line) in enumerate(zip(vectors, lines))
    ]
    later = [pltpu.make_async_copy(output, second_ref.at[0], sems.at[3])]
    for at in range(fold):
        later.append(
            pltpu.make_async_copy(
                down.at[pl.ds(at * share, share)],
                second_ref.at[1 + fold + at],
                sems.at[4 + at],
            )
        )
    later.append(pltpu.make_async_copy(up, wide_ref, sems.at[4 + fold]))
    for copy in copies + later:
        copy.start()
    for copy in copies:
        copy.wait()
    first_core = core_ref[0] == 0
    for at in range(3):
        left, right = held_ref[at, :, :cols], held_ref[at, :, cols:]
        here = slice(at * share, (at + 1) * share)
        mine_ref[here] = jnp.where(first_core, left, right)
        theirs_ref[here] = jnp.where(first_core, right, left)
    for ref in (mine_ref, theirs_ref):
        ref[3 * share :] = jnp.zeros((8, cols), ref.dtype)
        for at, line in enumerate(lines):
            low = at // 8 * LANES
            ref[3 * share + at % 8, low : low + line.shape[0]] = line[...]
    for copy in later:
        copy.wait()
    for at in range(fold):
        second_ref[1 + at] = wide_ref[:, at * width : (at + 1) * width]


def pack(core, matrices, vectors):
    share, width = matrices[0].shape
    cols = width // 2
    fold = matrices[4].shape[1] // width
    count = len(vectors)
    block = jax.ShapeDtypeStruct((3 * share + 8, cols), jnp.bfloat16)
    inside = pl.BlockSpec(memory_space=pltpu.VMEM)
    return pl.pallas_call(
        functools.partial(pack_kernel, count),
        in_specs=[pl.BlockSpec(memory_space=pltpu.SMEM)]
        + [pl.BlockSpec(memory_space=pl.ANY)] * (6 + count),
        out_specs=[inside] * 3,
        out_shape=[
            block,
            block,
            jax.ShapeDtypeStruct((1 + 2 * fold, share, width), jnp.bfloat16),
        ],
        scratch_shapes=[pltpu.VMEM((3, share, width), jnp.bfloat16)]
        + [pltpu.VMEM(matrices[4].shape, jnp.bfloat16)]
        + [pltpu.VMEM(item.shape, item.dtype) for item in vectors]
        + [pltpu.SemaphoreType.DMA((5 + fold,)), pltpu.SemaphoreType.DMA((count,))],
        compiler_params=pltpu.CompilerParams(vmem_limit_bytes=VMEM_LIMIT),
        name="pack",
    )(core, *matrices, *vectors)


def by_device(gathered_ref, rows, columns=slice(None)):
    n_pair, n_blk, n_core = gathered_ref.shape[:3]
    return jnp.concatenate(
        [
            gathered_ref[pair, blk, core, rows, columns]
            for pair in range(n_pair)
            for core in range(n_core)
            for blk in range(n_blk)
        ],
        axis=0,
    )


def unspread(gathered_ref, first_row, entry, width, share):
    low, row = entry // 8 * LANES, first_row + entry % 8
    pieces = by_device(gathered_ref, slice(row, row + 1), slice(low, low + LANES))
    lane = lax.broadcasted_iota(jnp.int32, (LANES, width), 1)
    row = lax.broadcasted_iota(jnp.int32, (LANES, width), 0)
    pick = jnp.where(lax.rem(lane, share) == row, 1.0, 0.0).astype(jnp.bfloat16)
    spread = dot_f32(pieces, pick, NN)
    lane = lax.broadcasted_iota(jnp.int32, (pieces.shape[0], width), 1)
    row = lax.broadcasted_iota(jnp.int32, (pieces.shape[0], width), 0)
    return jnp.sum(jnp.where(lax.div(lane, share) == row, spread, 0.0), axis=0, keepdims=True)


def own_weight(gathered_ref, at, share):
    return by_device(gathered_ref, slice(at * share, (at + 1) * share))


def block_rows(core_ref, own_ref, other_ref):
    own, other = own_ref[...], other_ref[...]
    first = core_ref[0] == 0
    return jnp.concatenate([jnp.where(first, own, other), jnp.where(first, other, own)], axis=0)


def block_specs(half, width):
    return [
        pl.BlockSpec((half, width), lambda at, core: (at, 0)),
        pl.BlockSpec((half, width), lambda at, core: (at + 1 - 2 * lax.rem(at, 2), 0)),
    ]


def project_kernel(share, core_ref, own_ref, other_ref, gathered_ref, out_ref, bias_ref):
    cols = gathered_ref.shape[4]

    @pl.when(pl.program_id(0) == 0)
    def _():
        for at in range(2):
            whole = unspread(gathered_ref, 3 * share, at, 2 * cols, share)
            bias_ref[at : at + 1, :] = jnp.where(
                core_ref[0] == 0, whole[:, :cols], whole[:, cols:]
            )

    tokens = block_rows(core_ref, own_ref, other_ref)
    for at, bias in enumerate((0, None, 1)):
        part = dot_f32(tokens, own_weight(gathered_ref, at, share), NN)
        if bias is not None:
            part = part + bias_ref[bias : bias + 1, :]
        out_ref[:, at * cols : (at + 1) * cols] = part.astype(out_ref.dtype)


def project(core, own, other, gathered, half):
    length, width = 2 * own.shape[0], own.shape[1]
    cols, share = width // 2, (gathered.shape[3] - 8) // 3
    return pl.pallas_call(
        functools.partial(project_kernel, share),
        grid_spec=pltpu.PrefetchScalarGridSpec(
            num_scalar_prefetch=1,
            grid=(length // (2 * half),),
            in_specs=block_specs(half, width)
            + [pl.BlockSpec(gathered.shape, lambda at, core: (0,) * 5)],
            out_specs=pl.BlockSpec((2 * half, 3 * cols), lambda at, core: (at, 0)),
            scratch_shapes=[pltpu.VMEM((8, cols), jnp.float32)],
        ),
        out_shape=jax.ShapeDtypeStruct((length, 3 * cols), jnp.bfloat16),
        compiler_params=pltpu.CompilerParams(vmem_limit_bytes=VMEM_LIMIT),
        cost_estimate=pl.CostEstimate(
            flops=6 * length * width * cols, bytes_accessed=10 * length * width, transcendentals=0
        ),
        name="project",
    )(core, own, other, gathered)


def norm(values, gain, shift):
    center = jnp.mean(values, axis=1, keepdims=True)
    offset = values - center
    scale = lax.rsqrt(jnp.mean(offset * offset, axis=1, keepdims=True) + 1e-12)
    unit = offset * scale
    return unit * gain + shift, unit, scale


def norm_back(grad, gain, unit, scale):
    inner = grad * gain
    mean = jnp.mean(inner, axis=1, keepdims=True)
    return scale * (inner - mean - unit * jnp.mean(inner * unit, axis=1, keepdims=True))


def feed_kernel(
    kept, index_ref, even_ref, odd_ref, tokens_ref, cotangent_ref, small_ref, weights_ref, *refs
):
    feed_rows(
        index_ref[1] == 1, even_ref, odd_ref, tokens_ref, cotangent_ref, small_ref, weights_ref, *refs[kept:]
    )


def feed_rows(
    odd, even_ref, odd_ref, tokens_ref, cotangent_ref, small_ref, weights_ref,
    out_ref, active_ref, grad_down_ref, grad_up_ref, hidden_ref, res_ref, attended_ref, context_ref,
    even_grad_ref, odd_grad_ref, sum_ref,
    weight_ref, vector_ref, slope_ref, sems,
):
    devices, _, share, width = weights_ref.shape
    fold = active_ref.shape[1] // width
    group = devices // fold
    step = pl.program_id(0)
    f32, bf16 = jnp.float32, jnp.bfloat16

    def copy(unit):
        if unit <= fold:
            return pltpu.make_async_copy(weights_ref.at[:, unit], weight_ref.at[unit], sems.at[unit])
        first = group * (unit - 1 - fold)
        return pltpu.make_async_copy(
            weights_ref.at[pl.ds(first, group), pl.ds(1 + fold, fold)],
            weight_ref.at[unit].reshape(group, fold, share, width),
            sems.at[unit],
        )

    order = [0]
    for at in range(fold):
        order += [1 + at, 1 + fold + at]
    ahead = 3

    @pl.when(step == 0)
    def _():
        for unit in order[:ahead]:
            copy(unit).start()
        sum_ref[...] = jnp.zeros_like(sum_ref)
        for entry in range(7):
            times = fold if entry == 1 else 1
            vector_ref[entry : entry + 1, : times * width] = unspread(
                small_ref, 0, 2 + entry, times * width, times * share
            )

    def ready(unit):
        @pl.when(step == 0)
        def _():
            copy(unit).wait()
            after = order.index(unit) + ahead
            if after < len(order):
                copy(order[after]).start()

    def weight(unit):
        return weight_ref[unit].reshape(width, width)

    def vector(entry, low=0):
        return vector_ref[entry : entry + 1, low : low + width]

    def add_sum(entry, value):
        sum_ref[entry : entry + 1, :] += jnp.sum(value, axis=0, keepdims=True)

    even, other = even_ref[...], odd_ref[...]
    context = jnp.concatenate([jnp.where(odd, other, even), jnp.where(odd, even, other)], axis=1)
    context_ref[...] = context
    ready(0)
    attended = dot_f32(context, weight(0), NN) + vector(0)
    hidden, unit_one, scale_one = norm(tokens_ref[...].astype(f32) + attended, vector(3), vector(4))
    hidden_low = hidden.astype(bf16)
    hidden_ref[...] = hidden_low
    down = vector(2)
    for at in range(fold):
        low = at * width
        ready(1 + at)
        up = dot_f32(hidden_low, weight(1 + at), NN) + vector(1, low)
        square = up * up
        tanh = jnp.tanh(0.7978845608 * up * (1.0 + 0.044715 * square))
        half = 0.5 * (1.0 + tanh)
        active = (up * half).astype(bf16)
        rise = (0.5 * 0.7978845608) * up * (1.0 - tanh * tanh)
        slope_ref[at] = half + rise * (1.0 + (3 * 0.044715) * square)
        active_ref[:, low : low + width] = active
        ready(1 + fold + at)
        down = down + dot_f32(active, weight(1 + fold + at), NN)
    out, unit_two, scale_two = norm(hidden + down, vector(5), vector(6))
    out_ref[...] = out.astype(bf16)
    cotangent = cotangent_ref[...].astype(f32)
    add_sum(4, cotangent * unit_two)
    add_sum(5, cotangent)
    grad = norm_back(cotangent, vector(5), unit_two, scale_two)
    grad_down = grad.astype(bf16)
    grad_down_ref[...] = grad_down
    add_sum(1, grad_down.astype(f32))
    for at in range(fold):
        low = at * width
        grad_active = dot_f32(grad_down, weight(1 + fold + at), NT)
        grad_up = (grad_active * slope_ref[at]).astype(bf16)
        grad_up_ref[:, low : low + width] = grad_up
        add_sum(6 + at, grad_up.astype(f32))
        grad = grad + dot_f32(grad_up, weight(1 + at), NT)
    add_sum(2, grad * unit_one)
    add_sum(3, grad)
    res_one = norm_back(grad, vector(3), unit_one, scale_one)
    res_ref[...] = res_one
    grad_attended = res_one.astype(bf16)
    attended_ref[...] = grad_attended
    add_sum(0, grad_attended.astype(f32))
    context_grad = dot_f32(grad_attended, weight(0), NT).astype(bf16)
    left, right = context_grad[:, : width // 2], context_grad[:, width // 2 :]
    even_grad_ref[...] = jnp.where(odd, right, left)
    odd_grad_ref[...] = jnp.where(odd, left, right)


def feed(index, even, other, tokens, cotangent, gathered, second, kept, tile):
    rows, width = even.shape[0], 2 * even.shape[1]
    seqs = tokens.shape[0]
    devices, units, share, _ = second.shape
    fold = (units - 1) // 2
    thin = pl.BlockSpec((tile, width), lambda at, index: (at, 0))
    placed = pl.BlockSpec((None, tile, width), lambda at, index: (index[0], at, 0))
    side = pl.BlockSpec((tile, width // 2), lambda at, index: (at, 0))
    wide = pl.BlockSpec((tile, fold * width), lambda at, index: (at, 0))
    sums = (6 + fold + 7) // 8 * 8

    def like(columns, dtype):
        return jax.ShapeDtypeStruct((rows, columns), dtype)

    bf16, f32 = jnp.bfloat16, jnp.float32
    return pl.pallas_call(
        functools.partial(feed_kernel, len(kept)),
        grid_spec=pltpu.PrefetchScalarGridSpec(
            num_scalar_prefetch=1,
            grid=(rows // tile,),
            in_specs=[
                side,
                side,
                placed,
                placed,
                pl.BlockSpec(
                    gathered.shape[:3] + (8, width // 2),
                    lambda at, index: (0, 0, 0, 3 * share // 8, 0),
                ),
                pl.BlockSpec(memory_space=pl.ANY),
            ]
            + [pl.BlockSpec(memory_space=pl.ANY)] * len(kept),
            out_specs=[placed, wide, thin, wide, thin, thin, thin, thin, side, side]
            + [pl.BlockSpec((sums, width), lambda at, index: (0, 0))],
            scratch_shapes=[
                pltpu.VMEM((units, devices, share, width), bf16),
                pltpu.VMEM((8, fold * width), f32),
                pltpu.VMEM((fold, tile, width), f32),
                pltpu.SemaphoreType.DMA((units,)),
            ],
        ),
        out_shape=[
            jax.ShapeDtypeStruct((seqs, rows, width), bf16),
            like(fold * width, bf16),
            like(width, bf16),
            like(fold * width, bf16),
            like(width, bf16),
            like(width, f32),
            like(width, bf16),
            like(width, bf16),
            like(width // 2, bf16),
            like(width // 2, bf16),
            jax.ShapeDtypeStruct((sums, width), f32),
        ],
        input_output_aliases={7: 0} if kept else {},
        compiler_params=pltpu.CompilerParams(vmem_limit_bytes=VMEM_LIMIT),
        cost_estimate=pl.CostEstimate(
            flops=4 * rows * width * width * (1 + 2 * fold),
            bytes_accessed=rows * width * (20 + 4 * fold) + 2 * units * width * width,
            transcendentals=rows * width * fold,
        ),
        name="feed",
    )(index, even, other, tokens, cotangent, gathered, second, *kept)


TN = ((0,), (0,))


def weight_grad_kernel(parts, *refs):
    groups = [refs[at * parts : (at + 1) * parts] for at in range(6)]
    active, grad_down, hidden, grad_up, context, attended = groups
    out_ref, block_ref, sems = refs[6 * parts :]
    devices, units, share, width = out_ref.shape
    fold = (units - 1) // 2
    group = devices // fold
    step = pl.program_id(0)
    slot = lax.rem(step, 2)

    def column_copy(unit, slot):
        return pltpu.make_async_copy(block_ref.at[slot], out_ref.at[:, unit], sems.at[slot])

    def row_copy(at, slot):
        return pltpu.make_async_copy(
            block_ref.at[slot].reshape(group, fold, share, width),
            out_ref.at[pl.ds(group * at, group), pl.ds(1 + fold, fold)],
            sems.at[slot],
        )

    def store(left, right, slot):
        total = None
        for one, other in zip(left, right):
            part = dot_f32(one[...], other[...], TN)
            total = part if total is None else total + part
        block_ref[slot] = total.astype(block_ref.dtype).reshape(devices, share, width)

    @pl.when(step >= 2)
    def _():
        column_copy(0, slot).wait()

    @pl.when(step == 0)
    def _():
        store(context, attended, 0)
        column_copy(0, 0).start()

    @pl.when((step >= 1) & (step <= fold))
    def _():
        store(hidden, grad_up, slot)
        column_copy(step, slot).start()

    @pl.when(step > fold)
    def _():
        store(active, grad_down, slot)
        row_copy(step - 1 - fold, slot).start()

    @pl.when(step == 2 * fold)
    def _():
        column_copy(0, 0).wait()
        column_copy(0, 1).wait()


def weight_grads(parts, devices):
    rows, width = parts[0][4].shape
    fold = parts[0][0].shape[1] // width
    share, units = width // devices, 1 + 2 * fold
    whole = pl.BlockSpec((rows, width), lambda at: (0, 0))
    active = pl.BlockSpec((rows, width), lambda at: (0, jnp.maximum(at - 1 - fold, 0)))
    up = pl.BlockSpec((rows, width), lambda at: (0, jnp.clip(at - 1, 0, fold - 1)))
    specs = [active, whole, whole, up, whole, whole]
    return pl.pallas_call(
        functools.partial(weight_grad_kernel, len(parts)),
        grid=(1 + 2 * fold,),
        in_specs=[spec for spec in specs for _ in parts],
        out_specs=pl.BlockSpec(memory_space=pl.ANY),
        scratch_shapes=[
            pltpu.VMEM((2, devices, share, width), jnp.bfloat16),
            pltpu.SemaphoreType.DMA((2,)),
        ],
        out_shape=jax.ShapeDtypeStruct((devices, units, share, width), jnp.bfloat16),
        compiler_params=pltpu.CompilerParams(vmem_limit_bytes=VMEM_LIMIT),
        cost_estimate=pl.CostEstimate(
            flops=2 * len(parts) * rows * width * width * (1 + 2 * fold),
            bytes_accessed=2 * (len(parts) * rows + width) * width * units,
            transcendentals=0,
        ),
        name="weight_grads",
    )(*[part[at] for at in range(6) for part in parts])


def own_grads_kernel(
    count, core_ref, query_ref, key_ref, value_ref, own_ref, other_ref, *refs
):
    out_ref, sum_ref, bias_ref = refs[-3:]
    devices, high, wide = out_ref.shape
    cols, share = wide // 3, high - 8
    step = pl.program_id(0)

    @pl.when(step == 0)
    def _():
        sum_ref[...] = jnp.zeros_like(sum_ref)
        bias_ref[...] = jnp.zeros_like(bias_ref)

    tokens = block_rows(core_ref, own_ref, other_ref)
    for at, grad_ref in enumerate((query_ref, key_ref, value_ref)):
        grad = grad_ref[...]
        here = slice(at * cols, (at + 1) * cols)
        sum_ref[:, here] += dot_f32(tokens, grad, TN)
        bias_ref[0:1, here] += jnp.sum(grad.astype(jnp.float32), axis=0, keepdims=True)

    @pl.when(step == pl.num_programs(0) - 1)
    def _():
        out_ref[:, :share, :] = sum_ref[...].astype(out_ref.dtype).reshape(devices, share, wide)
        total = refs[0][...]
        for ref in refs[1:-3]:
            total = total + ref[...]
        zero = jnp.zeros((1, cols), jnp.float32)
        bits = [total[at : at + 1, low : low + cols] for at in range(count) for low in (0, cols)]
        bits += [zero] * (21 - len(bits))
        lines = [jnp.concatenate(bits[at : at + 3], axis=1) for at in range(0, 21, 3)]
        lines = jnp.concatenate([bias_ref[0:1, :]] + lines, axis=0).astype(out_ref.dtype)
        out_ref[:, share:, :] = jnp.broadcast_to(lines[None], (devices, 8, wide))


def own_grads(core, grads, own, other, sums, count, devices, half):
    length, width = 2 * own.shape[0], own.shape[1]
    share, wide = width // devices, 3 * (width // 2)
    grad_spec = pl.BlockSpec((2 * half, wide // 3), lambda at, core: (at, 0))
    return pl.pallas_call(
        functools.partial(own_grads_kernel, count),
        grid_spec=pltpu.PrefetchScalarGridSpec(
            num_scalar_prefetch=1,
            grid=(length // (2 * half),),
            in_specs=[grad_spec] * 3
            + block_specs(half, width)
            + [pl.BlockSpec(item.shape, lambda at, core: (0, 0)) for item in sums],
            out_specs=pl.BlockSpec((devices, share + 8, wide), lambda at, core: (0, 0, 0)),
            scratch_shapes=[
                pltpu.VMEM((width, wide), jnp.float32),
                pltpu.VMEM((8, wide), jnp.float32),
            ],
        ),
        out_shape=jax.ShapeDtypeStruct((devices, share + 8, wide), jnp.bfloat16),
        compiler_params=pltpu.CompilerParams(vmem_limit_bytes=VMEM_LIMIT),
        cost_estimate=pl.CostEstimate(
            flops=2 * length * width * wide, bytes_accessed=6 * length * width, transcendentals=0
        ),
        name="own_grads",
    )(core, *grads, own, other, *sums)


def tokens_grad_kernel(
    share, core_ref, query_ref, key_ref, value_ref, gathered_ref, own_ref, other_ref
):
    total = None
    for at, grad_ref in enumerate((query_ref, key_ref, value_ref)):
        part = dot_f32(grad_ref[...], own_weight(gathered_ref, at, share), NT)
        total = part if total is None else total + part
    half = own_ref.shape[0]
    total = total.astype(own_ref.dtype)
    first = core_ref[0] == 0
    own_ref[...] = jnp.where(first, total[:half], total[half:])
    other_ref[...] = jnp.where(first, total[half:], total[:half])


def tokens_grads(core, grads, gathered, half):
    length, width = grads[0].shape[0], 2 * gathered.shape[4]
    cols, share = width // 2, (gathered.shape[3] - 8) // 3
    rows = jax.ShapeDtypeStruct((length // 2, width), jnp.bfloat16)
    return pl.pallas_call(
        functools.partial(tokens_grad_kernel, share),
        grid_spec=pltpu.PrefetchScalarGridSpec(
            num_scalar_prefetch=1,
            grid=(length // (2 * half),),
            in_specs=[pl.BlockSpec((2 * half, cols), lambda at, core: (at, 0))] * 3
            + [pl.BlockSpec(gathered.shape, lambda at, core: (0,) * 5)],
            out_specs=block_specs(half, width),
        ),
        out_shape=[rows, rows],
        compiler_params=pltpu.CompilerParams(vmem_limit_bytes=VMEM_LIMIT),
        cost_estimate=pl.CostEstimate(
            flops=6 * length * width * cols, bytes_accessed=6 * length * width, transcendentals=0
        ),
        name="tokens_grads",
    )(core, *grads, gathered)


def body(
    tokens,
    cotangent,
    lengths,
    query_weight,
    key_weight,
    value_weight,
    output_weight,
    up_weight,
    down_weight,
    query_bias,
    value_bias,
    output_bias,
    up_bias,
    down_bias,
    attn_gain,
    attn_shift,
    ffn_gain,
    ffn_shift,
):
    seqs, stretch, width = tokens.shape
    rows = seqs * stretch
    n_pair, n_core, n_blk = (lax.axis_size(axis) for axis in ALL)
    devices = n_pair * n_core * n_blk
    pair, core, blk = (lax.axis_index(axis) for axis in ALL)
    half, cols = stretch // 2, width // 2
    own_rows = n_blk * half
    share = query_weight.shape[0]
    fold = up_weight.shape[1] // width
    bf16, f32 = jnp.bfloat16, jnp.float32

    def table(step, back):
        moves = []
        for pair in range(n_pair):
            for src_core in range(n_core):
                for src in range(n_blk):
                    piece = src ^ step
                    sender = (pair * n_core + src_core) * n_blk + src
                    target = (pair * n_core + piece % 2) * n_blk + seqs * src_core + piece // 2
                    moves.append((target, sender) if back else (sender, target))
        return moves

    def move(array, step, back=False):
        return lax.ppermute(array, ALL, table(step, back))

    def after(array, *others):
        return lax.optimization_barrier((array, others))[0]

    def other_core(array):
        return lax.ppermute(array, "core", [(0, 1), (1, 0)])

    def columns(array, which):
        return lax.dynamic_slice_in_dim(array, which * cols, cols, axis=-1)

    def swap(flip, one, two):
        return jnp.where(flip, two, one), jnp.where(flip, one, two)

    def ordered(me, items):
        bit = 1
        while bit < len(items):
            flip = (me & bit) != 0
            items = [jnp.where(flip, items[at ^ bit], items[at]) for at in range(len(items))]
            bit *= 2
        return items

    def others(array, axis, size):
        return [
            lax.ppermute(array, axis, [(at, at ^ step) for at in range(size)])
            for step in range(1, size)
        ]

    which = jnp.reshape(core, (1,)).astype(jnp.int32)
    mine, theirs, second = pack(
        which,
        (query_weight, key_weight, value_weight, output_weight, up_weight, down_weight),
        (query_bias, value_bias, output_bias, up_bias, down_bias)
        + (attn_gain, attn_shift, ffn_gain, ffn_shift),
    )
    gathered = jnp.stack(swap(core == 1, mine, other_core(theirs)))
    gathered = jnp.stack(ordered(blk, [gathered] + others(gathered, "blk", n_blk)))
    tokens_moved = after(tokens, gathered)
    seconds = lax.all_gather(second, "blk", axis=0)
    pieces = tokens_moved.reshape(n_blk, half, width)
    arrived = [
        move(lax.dynamic_index_in_dim(pieces, blk ^ step, 0, keepdims=False), step)
        for step in range(n_blk)
    ]
    terms, arrived[:2] = lax.optimization_barrier(
        ([gathered] + others(gathered, "pair", n_pair), arrived[:2])
    )
    gathered = jnp.stack(ordered(pair, terms))
    second = lax.all_gather(after(seconds, gathered), ("pair", "core"), axis=0)
    second = second.reshape((devices,) + second.shape[2:])
    both = jnp.concatenate(swap(core == 1, lengths, other_core(lengths)))
    own_length = lax.dynamic_index_in_dim(both, blk, 0, keepdims=False)

    parts = n_blk // 2
    piece = 2 * (blk % seqs) + core
    info = jnp.stack(
        [own_length] + [(piece ^ (at // 2)) * stretch + at % 2 * half for at in range(2 * n_blk)]
    ).astype(jnp.int32)
    own_tokens = after(jnp.concatenate(arrived, axis=0), gathered, info)
    other_tokens = other_core(own_tokens)
    odd = blk % 2 == 1

    def after_all(items, *others):
        return lax.optimization_barrier((items, others))[0]

    qkv = project(which, own_tokens, other_tokens, gathered, half)
    attended, returning = [], []
    for part in range(parts):
        query_side = after(qkv, attended[-1]) if part else qkv
        attended.append(attend(query_side, info, part, parts, 512))
        returning.append([move(attended[-1][at], 2 * part + at, True) for at in range(2)])

    fed, context_grads, kept = [], [], ()
    for part in range(parts):
        even, other = after_all(returning[part], fed[-1] if part else attended[-1])
        index = jnp.stack([(blk // 2) ^ part, blk % 2]).astype(jnp.int32)
        fed.append(feed(index, even, other, tokens, cotangent, gathered, second, kept, 256))
        kept = (fed[-1][0],)
        context_grads.append([move(fed[-1][8 + at], 2 * part + at) for at in range(2)])
    layer_out = kept[0]

    early, late = context_grads[0], context_grads[1]
    early, first_active = lax.optimization_barrier((early, fed[0][1]))
    second_grads = weight_grads(
        [
            (item[1] if part else first_active, item[2], item[4], item[3], item[7], item[6])
            for part, item in enumerate(fed)
        ],
        devices,
    )
    late, second_grads = lax.optimization_barrier((late, second_grads))
    total = second_grads
    second_grads = lax.psum_scatter(
        second_grads.reshape((n_pair * n_core, n_blk) + second_grads.shape[1:]),
        ("pair", "core"),
        scatter_dimension=0,
    )
    early[0] = after(early[0], total)
    outs, auxes = [item[2] for item in attended], [item[3] for item in attended]
    grads = attend_back(qkv, list(early) + list(late), outs, auxes, info, 512, 1024)

    own, far = tokens_grads(which, grads, gathered, half)
    second_grads, own, far = lax.optimization_barrier((second_grads, own, far))
    second_grads = lax.psum_scatter(second_grads, "blk", scatter_dimension=0)
    summed = (own.astype(f32) + other_core(far).astype(f32)).astype(bf16)
    moved = [move(summed[step * half : (step + 1) * half], step, True) for step in range(n_blk)]
    first_grads = own_grads(
        which,
        [after(item, summed) for item in grads],
        own_tokens,
        other_tokens,
        [item[10] for item in fed],
        6 + fold,
        devices,
        half,
    )

    def to_sum(array, axis, me, size):
        terms = [lax.dynamic_index_in_dim(array, me, 0, keepdims=False)]
        for step in range(1, size):
            sent = lax.dynamic_index_in_dim(array, me ^ step, 0, keepdims=False)
            terms.append(lax.ppermute(sent, axis, [(at, at ^ step) for at in range(size)]))
        return terms

    def add(terms):
        total = terms[0].astype(f32)
        for term in terms[1:]:
            total += term.astype(f32)
        return total.astype(bf16)

    first_grads = first_grads.reshape(n_pair, n_core, n_blk, share + 8, 3 * cols)
    total = add(to_sum(first_grads, "pair", pair, n_pair))
    moved, total, second_grads = lax.optimization_barrier((moved, total, second_grads))
    terms = to_sum(jnp.moveaxis(total, 1, 0), "blk", blk, n_blk)
    returned = []
    for part in range(parts):
        back = jnp.concatenate(swap(odd, *moved[2 * part : 2 * part + 2]), axis=0)
        returned.append(fed[part][5] + back.astype(f32))
    tokens_grad = jnp.stack(swap(blk >= 2, *returned))

    device = (pair * n_core + core) * n_blk + blk

    def own_part(line, size):
        return lax.dynamic_slice_in_dim(line, device * size, size, axis=-1)

    second_grads = second_grads.astype(f32)
    late = (
        second_grads[0],
        jnp.concatenate([second_grads[1 + at] for at in range(fold)], axis=1),
        second_grads[1 + fold :].reshape(fold * share, width),
    )
    terms, tokens_grad, late = lax.optimization_barrier((terms, tokens_grad, late))
    total = add(terms)
    kept = lax.dynamic_index_in_dim(total, core, 0, keepdims=False)
    crossed = other_core(lax.dynamic_index_in_dim(total, 1 - core, 0, keepdims=False))
    left, right = (item.astype(f32) for item in swap(core == 1, kept, crossed))
    projections = [
        jnp.concatenate([left[:, at : at + cols], right[:, at : at + cols]], axis=1)
        for at in range(0, 3 * cols, cols)
    ]
    lines = (kept[share + 1 :].astype(f32) + crossed[share + 1 :].astype(f32)).reshape(-1)
    own_lines = own_part(lines[: 6 * width].reshape(6, width), share)
    up_line = own_part(lines[6 * width : (6 + fold) * width], fold * share)
    return (
        (layer_out, tokens_grad)
        + tuple(item[:share] for item in projections)
        + late
        + (own_part(projections[0][share], share), own_part(projections[2][share], share))
        + (own_lines[0], up_line, own_lines[1], own_lines[2], own_lines[3], own_lines[4], own_lines[5])
    )


def fits(mesh, tokens, up_weight):
    n_dp, n_blk = mesh.shape["dp"], mesh.shape["blk"]
    batch, length, width = tokens.shape
    if n_dp % 2 or n_dp & (n_dp - 1) or batch % n_dp or 2 * (batch // n_dp) != n_blk or n_blk != 4:
        return False
    share = width // (n_dp * n_blk)
    fold = up_weight.shape[1] // width
    return (
        width == HEADS * 64
        and width % (4 * LANES // PER_TILE) == 0
        and up_weight.shape[1] == fold * width
        and share * n_dp * n_blk == width
        and share % 8 == 0
        and 16 <= share
        and (8 + fold) * share <= width // 2
        and fold == 4
        and length % (16 * n_blk) == 0
        and length % 512 == 0
        and length <= 4096
    )


def solution(mesh):
    n_dp, n_blk = mesh.shape["dp"], mesh.shape["blk"]

    def step(*args):
        spread = ("dp", "blk")
        one, use = ring_body, mesh
        where = {"dp": "dp", "blk": "blk", spread: spread}
        if fits(mesh, args[0], args[7]):
            one, use = body, Mesh(mesh.devices.reshape(n_dp // 2, 2, n_blk), ALL)
            where = {"dp": ("pair", "core"), "blk": "blk", spread: ALL}
        block = P(where["dp"], where["blk"], None)
        matrix = P(where[spread], None)
        vector = P(where[spread])
        return jax.shard_map(
            one,
            mesh=use,
            in_specs=(block, block, P(where["dp"])) + (matrix,) * 6 + (vector,) * 9,
            out_specs=(block, block) + (matrix,) * 6 + (vector,) * 9,
            check_vma=False,
        )(*args)

    return step
```

```python
import functools

import jax
import jax.numpy as jnp
from jax import lax
from jax.experimental import pallas as pl
from jax.experimental.pallas import tpu as pltpu
from jax.sharding import Mesh
from jax.sharding import PartitionSpec as P

HEADS = 12
LANES = 128
PER_TILE = 2
SCORE_SCALE = 0.125 * 1.4426950408889634
MASKED = -1e30
ALL = ("pair", "core", "blk")
VMEM_LIMIT = 56 << 20


def shifted(array, axis, by):
    length = lax.axis_size(axis)
    return lax.ppermute(array, axis, [(i, (i + by) % length) for i in range(length)])


def matmul(left, right):
    return jnp.dot(left, right, preferred_element_type=jnp.float32)


def times_trans(left, right):
    return lax.dot_general(
        left, right, (((1,), (1,)), ((), ())), preferred_element_type=jnp.float32
    )


def trans_times(left, right):
    return lax.dot_general(
        left, right, (((0,), (0,)), ((), ())), preferred_element_type=jnp.float32
    )


def layer_norm(values, gain, shift):
    center = jnp.mean(values, axis=-1, keepdims=True)
    offset = values - center
    spread = jnp.mean(offset * offset, axis=-1, keepdims=True)
    return offset * lax.rsqrt(spread + 1e-12) * gain + shift


def gelu_tanh(values):
    return jax.nn.gelu(values, approximate=True)


def ring_body(
    tokens,
    cotangent,
    lengths,
    query_weight,
    key_weight,
    value_weight,
    output_weight,
    up_weight,
    down_weight,
    query_bias,
    value_bias,
    output_bias,
    up_bias,
    down_bias,
    attn_gain,
    attn_shift,
    ffn_gain,
    ffn_shift,
):
    seqs, stretch, width = tokens.shape
    rows = seqs * stretch
    heads = HEADS
    head = width // heads
    gathered = (
        lax.all_gather(query_weight, ("dp", "blk"), axis=0, tiled=True),
        lax.all_gather(key_weight, ("dp", "blk"), axis=0, tiled=True),
        lax.all_gather(value_weight, ("dp", "blk"), axis=0, tiled=True),
        lax.all_gather(output_weight, ("dp", "blk"), axis=0, tiled=True),
        lax.all_gather(up_weight, ("dp", "blk"), axis=0, tiled=True),
        lax.all_gather(down_weight, ("dp", "blk"), axis=0, tiled=True),
        lax.all_gather(query_bias, ("dp", "blk"), axis=0, tiled=True),
        lax.all_gather(value_bias, ("dp", "blk"), axis=0, tiled=True),
        lax.all_gather(output_bias, ("dp", "blk"), axis=0, tiled=True),
        lax.all_gather(up_bias, ("dp", "blk"), axis=0, tiled=True),
        lax.all_gather(down_bias, ("dp", "blk"), axis=0, tiled=True),
        lax.all_gather(attn_gain, ("dp", "blk"), axis=0, tiled=True),
        lax.all_gather(attn_shift, ("dp", "blk"), axis=0, tiled=True),
        lax.all_gather(ffn_gain, ("dp", "blk"), axis=0, tiled=True),
        lax.all_gather(ffn_shift, ("dp", "blk"), axis=0, tiled=True),
    )
    query_full, key_full, value_full, output_full, upper_full, lower_full = gathered[:6]
    (
        bias_query,
        bias_value,
        bias_output,
        bias_upper,
        bias_lower,
        gain_one,
        shift_one,
        gain_two,
        shift_two,
    ) = [item.astype(jnp.float32) for item in gathered[6:]]
    flat = tokens.reshape(rows, width)
    queries = (matmul(flat, query_full) + bias_query).astype(jnp.bfloat16)
    keys_own = matmul(flat, key_full).astype(jnp.bfloat16)
    values_own = (matmul(flat, value_full) + bias_value).astype(jnp.bfloat16)
    query_heads = queries.reshape(seqs, stretch, heads, head)
    own_block = lax.axis_index("blk")
    cycle_size = lax.axis_size("blk")
    start = jnp.int32(0)
    key_piece = lax.all_gather(keys_own.reshape(seqs, stretch, width), "blk", axis=1, tiled=True)
    value_piece = lax.all_gather(
        values_own.reshape(seqs, stretch, width), "blk", axis=1, tiled=True
    )
    count = key_piece.shape[1]
    span = min(count, stretch)
    row_max = jnp.full((seqs, stretch, heads), -1e30, jnp.float32)
    row_total = jnp.zeros((seqs, stretch, heads), jnp.float32)
    accum = jnp.zeros((seqs, stretch, heads, head), jnp.float32)
    for part_no in range(count // span):
        key_heads = key_piece[:, part_no * span : (part_no + 1) * span].reshape(
            seqs, span, heads, head
        )
        value_heads = value_piece[:, part_no * span : (part_no + 1) * span].reshape(
            seqs, span, heads, head
        )
        positions = start + part_no * span + jnp.arange(span, dtype=jnp.int32)
        valid = positions[None, :] < lengths[:, None]
        scores = (
            jnp.einsum(
                "sqhd,skhd->sqhk", query_heads, key_heads, preferred_element_type=jnp.float32
            )
            * 0.125
        )
        scores = jnp.where(valid[:, None, None, :], scores, -jnp.inf)
        new_max = jnp.maximum(row_max, jnp.max(scores, axis=-1))
        expo = jnp.exp(scores - new_max[..., None])
        factor = jnp.exp(row_max - new_max)
        row_total = row_total * factor + jnp.sum(expo, axis=-1)
        accum = accum * factor[..., None] + jnp.einsum(
            "sqhk,skhd->sqhd",
            expo.astype(jnp.bfloat16),
            value_heads,
            preferred_element_type=jnp.float32,
        )
        row_max = new_max
    row_max, row_total, accum = (row_max, row_total, accum)
    log_total = row_max + jnp.log(row_total)
    context_full = accum / row_total[..., None]
    context = context_full.reshape(rows, width).astype(jnp.bfloat16)
    attended = matmul(context, output_full) + bias_output
    hidden, norm_one_back = jax.vjp(
        layer_norm, flat.astype(jnp.float32) + attended, gain_one, shift_one
    )
    hidden_low = hidden.astype(jnp.bfloat16)
    upward = matmul(hidden_low, upper_full) + bias_upper
    active_full, gelu_back = jax.vjp(gelu_tanh, upward)
    active = active_full.astype(jnp.bfloat16)
    downward = matmul(active, lower_full) + bias_lower
    output_full32, norm_two_back = jax.vjp(layer_norm, hidden + downward, gain_two, shift_two)
    layer_out = output_full32.astype(jnp.bfloat16).reshape(seqs, stretch, width)
    query_back, key_back, value_back, output_back, upper_back, lower_back = (
        lax.all_gather(query_weight, ("dp", "blk"), axis=0, tiled=True),
        lax.all_gather(key_weight, ("dp", "blk"), axis=0, tiled=True),
        lax.all_gather(value_weight, ("dp", "blk"), axis=0, tiled=True),
        lax.all_gather(output_weight, ("dp", "blk"), axis=0, tiled=True),
        lax.all_gather(up_weight, ("dp", "blk"), axis=0, tiled=True),
        lax.all_gather(down_weight, ("dp", "blk"), axis=0, tiled=True),
    )
    grad_outer = cotangent.reshape(rows, width).astype(jnp.float32)
    grad_res_two, grad_gain_two, grad_shift_two = norm_two_back(grad_outer)
    grad_down = grad_res_two.astype(jnp.bfloat16)
    grad_lower_bias = jnp.sum(grad_down, axis=0, dtype=jnp.float32)
    grad_lower = trans_times(active, grad_down)
    grad_active = times_trans(grad_down, lower_back)
    (grad_upward,) = gelu_back(grad_active)
    grad_up = grad_upward.astype(jnp.bfloat16)
    grad_upper_bias = jnp.sum(grad_up, axis=0, dtype=jnp.float32)
    grad_upper = trans_times(hidden_low, grad_up)
    grad_hidden = grad_res_two + times_trans(grad_up, upper_back)
    grad_res_one, grad_gain_one, grad_shift_one = norm_one_back(grad_hidden)
    grad_attended = grad_res_one.astype(jnp.bfloat16)
    grad_output_bias = jnp.sum(grad_attended, axis=0, dtype=jnp.float32)
    grad_output = trans_times(context, grad_attended)
    grad_context = times_trans(grad_attended, output_back).astype(jnp.bfloat16)
    context_grad_heads = grad_context.reshape(seqs, stretch, heads, head)
    delta = jnp.sum(context_grad_heads.astype(jnp.float32) * context_full, axis=-1)

    def contribute(key_value, source, pair_grad, query_grad):
        key_heads = key_value[0]
        value_heads = key_value[1]
        positions = source * stretch + jnp.arange(stretch, dtype=jnp.int32)
        valid = positions[None, :] < lengths[:, None]
        scores = (
            jnp.einsum(
                "sqhd,skhd->sqhk", query_heads, key_heads, preferred_element_type=jnp.float32
            )
            * 0.125
        )
        probs = jnp.where(valid[:, None, None, :], jnp.exp(scores - log_total[..., None]), 0.0)
        grad_probs = jnp.einsum(
            "sqhd,skhd->sqhk", context_grad_heads, value_heads, preferred_element_type=jnp.float32
        )
        grad_scores = (probs * (grad_probs - delta[..., None])).astype(jnp.bfloat16)
        query_grad = (
            query_grad
            + jnp.einsum(
                "sqhk,skhd->sqhd", grad_scores, key_heads, preferred_element_type=jnp.float32
            )
            * 0.125
        )
        key_part = (
            jnp.einsum(
                "sqhk,sqhd->skhd", grad_scores, query_heads, preferred_element_type=jnp.float32
            )
            * 0.125
        )
        value_part = jnp.einsum(
            "sqhk,sqhd->skhd",
            probs.astype(jnp.bfloat16),
            context_grad_heads,
            preferred_element_type=jnp.float32,
        )
        pair_grad = pair_grad + jnp.stack([key_part, value_part])
        return (pair_grad, query_grad)

    def rotate_grads(pair_grad):
        return shifted(pair_grad.astype(jnp.bfloat16), "blk", 1).astype(pair_grad.dtype)

    key_value_own = jnp.stack(
        [
            keys_own.reshape(seqs, stretch, heads, head),
            values_own.reshape(seqs, stretch, heads, head),
        ]
    )
    pair_grad, query_grad = contribute(
        key_value_own,
        own_block,
        jnp.zeros((2, seqs, stretch, heads, head), jnp.float32),
        jnp.zeros((seqs, stretch, heads, head), jnp.float32),
    )

    def cycle_turn(turn, state):
        key_value_now, pair_now, query_now = state
        key_value_now = shifted(key_value_now, "blk", 1)
        pair_now = rotate_grads(pair_now)
        source = (own_block - turn) % cycle_size
        pair_now, query_now = contribute(key_value_now, source, pair_now, query_now)
        return (key_value_now, pair_now, query_now)

    final_state = lax.fori_loop(1, cycle_size, cycle_turn, (key_value_own, pair_grad, query_grad))
    pair_home = rotate_grads(final_state[1])
    grad_queries = final_state[2].reshape(rows, width).astype(jnp.bfloat16)
    grad_keys = pair_home[0].reshape(rows, width).astype(jnp.bfloat16)
    grad_values = pair_home[1].reshape(rows, width).astype(jnp.bfloat16)
    grad_query = trans_times(flat, grad_queries)
    grad_key = trans_times(flat, grad_keys)
    grad_value = trans_times(flat, grad_values)
    grad_query_bias = jnp.sum(grad_queries, axis=0, dtype=jnp.float32)
    grad_value_bias = jnp.sum(grad_values, axis=0, dtype=jnp.float32)
    tokens_grad = (
        grad_res_one
        + times_trans(grad_queries, query_back)
        + times_trans(grad_keys, key_back)
        + times_trans(grad_values, value_back)
    ).reshape(seqs, stretch, width)
    shares = (
        lax.psum_scatter(grad_query, ("dp", "blk"), scatter_dimension=0, tiled=True),
        lax.psum_scatter(grad_key, ("dp", "blk"), scatter_dimension=0, tiled=True),
        lax.psum_scatter(grad_value, ("dp", "blk"), scatter_dimension=0, tiled=True),
        lax.psum_scatter(grad_output, ("dp", "blk"), scatter_dimension=0, tiled=True),
        lax.psum_scatter(grad_upper, ("dp", "blk"), scatter_dimension=0, tiled=True),
        lax.psum_scatter(grad_lower, ("dp", "blk"), scatter_dimension=0, tiled=True),
        lax.psum_scatter(grad_query_bias, ("dp", "blk"), scatter_dimension=0, tiled=True),
        lax.psum_scatter(grad_value_bias, ("dp", "blk"), scatter_dimension=0, tiled=True),
        lax.psum_scatter(grad_output_bias, ("dp", "blk"), scatter_dimension=0, tiled=True),
        lax.psum_scatter(grad_upper_bias, ("dp", "blk"), scatter_dimension=0, tiled=True),
        lax.psum_scatter(grad_lower_bias, ("dp", "blk"), scatter_dimension=0, tiled=True),
        lax.psum_scatter(grad_gain_one, ("dp", "blk"), scatter_dimension=0, tiled=True),
        lax.psum_scatter(grad_shift_one, ("dp", "blk"), scatter_dimension=0, tiled=True),
        lax.psum_scatter(grad_gain_two, ("dp", "blk"), scatter_dimension=0, tiled=True),
        lax.psum_scatter(grad_shift_two, ("dp", "blk"), scatter_dimension=0, tiled=True),
    )
    return (layer_out, tokens_grad) + tuple(shares)


def dot_f32(left, right, dims):
    return lax.dot_general(left, right, (dims, ((), ())), preferred_element_type=jnp.float32)


NT = ((1,), (1,))
NN = ((1,), (0,))


def split_three(values):
    high = values.astype(jnp.bfloat16).astype(jnp.float32)
    rest = values - high
    mid = rest.astype(jnp.bfloat16).astype(jnp.float32)
    return high, mid, rest - mid


def spread_three(lane, base, values, into):
    for step, part in enumerate(split_three(values)):
        into = jnp.where(lane == base + step, part, into)
    return into


def fill_keys(info_ref, keys, values, key_aug, value_aug, value_fill, chunk):
    length = keys.shape[0]
    lane = lax.broadcasted_iota(jnp.int32, (chunk, LANES), 1)
    row = lax.broadcasted_iota(jnp.int32, (chunk, LANES), 0)
    for part in range(length // chunk):
        at = slice(part * chunk, (part + 1) * chunk)
        off = (lane == 3) & (row + info_ref[1 + part] >= info_ref[0])
        mask = jnp.where(off, MASKED, 0.0)
        for one in range(PER_TILE):
            mine = lane // (LANES // PER_TILE) == one
            base = 4 * one
            minus = (lane >= base) & (lane < base + 3)
            key_aug[one, at, :LANES] = jnp.where(mine, keys[at], jnp.zeros((), keys.dtype))
            key_aug[one, at, LANES:] = jnp.where(minus, -1.0, mask).astype(jnp.bfloat16)
            value_aug[one, at, :LANES] = jnp.where(mine, values[at], jnp.zeros((), keys.dtype))
            if value_fill:
                value_aug[one, at, LANES:] = jnp.ones((chunk, LANES), jnp.bfloat16)
            else:
                value_aug[one, at, LANES:] = jnp.where(minus, -1.0, 0.0).astype(jnp.bfloat16)


def attend_kernel(
    span, info_ref, query_ref, key_ref, value_ref, near_ref, far_ref, out_ref, aux_ref, key_aug, value_aug
):
    length = key_ref.shape[0]
    tile = query_ref.shape[0]
    lane = lax.broadcasted_iota(jnp.int32, (1, LANES), 1)

    fill_keys(info_ref, key_ref, value_ref, key_aug, value_aug, True, length // 8)

    one_lane = jnp.where(lane == 3, 1.0, 0.0)
    flag = jnp.broadcast_to(one_lane.astype(jnp.bfloat16), (tile, LANES))
    query = jnp.concatenate([query_ref[...], flag], axis=1)
    pieces = [slice(at, at + span) for at in range(0, length, span)]
    scores, peaks = [], []
    for one in range(PER_TILE):
        peak = None
        row = []
        for at in pieces:
            score = dot_f32(query, key_aug[one, at], NT)
            row.append(score)
            for low in range(0, span, LANES):
                part = score[:, low : low + LANES]
                peak = part if peak is None else jnp.maximum(peak, part)
        scores.append(row)
        peaks.append(jnp.max(peak, axis=1, keepdims=True))
    out = None
    aux = one_lane
    for one in range(PER_TILE):
        total = None
        for at, score in zip(pieces, scores[one]):
            expo = jnp.exp2((score - peaks[one]) * SCORE_SCALE).astype(jnp.bfloat16)
            part = dot_f32(expo, value_aug[one, at], NN)
            total = part if total is None else total + part
        weight = total[:, LANES:]
        part = total[:, :LANES] / weight
        out = part if out is None else out + part
        log_total = jnp.log2(weight) * (1.0 / SCORE_SCALE) + peaks[one]
        aux = spread_three(lane, 4 * one, log_total, aux)
    low = out.astype(jnp.bfloat16)
    near_ref[...] = low[: tile // 2]
    far_ref[...] = low[tile // 2 :]
    out_ref[...] = out
    aux_ref[...] = aux.astype(jnp.bfloat16)


def attend(qkv, info, part, parts, span):
    length, width = qkv.shape[0], qkv.shape[1] // 3
    tiles, rows = width // LANES, length // parts
    half = pl.BlockSpec((rows // 2, LANES), lambda pair: (0, pair))
    whole = pl.BlockSpec((rows, LANES), lambda pair: (0, pair))
    block = jax.ShapeDtypeStruct((rows // 2, width), jnp.bfloat16)
    return pl.pallas_call(
        functools.partial(attend_kernel, span),
        grid=(tiles,),
        in_specs=[
            pl.BlockSpec(memory_space=pltpu.SMEM),
            pl.BlockSpec((rows, LANES), lambda pair: (part, pair)),
            pl.BlockSpec((length, LANES), lambda pair: (0, tiles + pair)),
            pl.BlockSpec((length, LANES), lambda pair: (0, 2 * tiles + pair)),
        ],
        out_specs=[half, half, whole, whole],
        out_shape=[
            block,
            block,
            jax.ShapeDtypeStruct((rows, width), jnp.float32),
            jax.ShapeDtypeStruct((rows, width), jnp.bfloat16),
        ],
        scratch_shapes=[pltpu.VMEM((PER_TILE, length, 2 * LANES), jnp.bfloat16)] * 2,
        compiler_params=pltpu.CompilerParams(vmem_limit_bytes=VMEM_LIMIT),
        cost_estimate=pl.CostEstimate(
            flops=16 * rows * length * width,
            bytes_accessed=12 * length * width,
            transcendentals=rows * length * width // 64,
        ),
        name="attend",
    )(info, qkv, qkv, qkv)


def attend_back_kernel(span, counts, info_ref, query_ref, key_ref, value_ref, *refs):
    groups = []
    for count in counts:
        groups.append(refs[:count])
        refs = refs[count:]
    query_grad_ref, key_grad_ref, value_grad_ref, key_aug, value_aug, key_cols, key_sum, value_sum = refs
    length = key_ref.shape[0]
    tile = query_ref.shape[0]
    wide = LANES // PER_TILE
    lane = lax.broadcasted_iota(jnp.int32, (1, LANES), 1)
    step = pl.program_id(1)

    @pl.when(step == 0)
    def _():
        fill_keys(info_ref, key_ref, value_ref, key_aug, value_aug, False, length // 8)
        key_cols[...] = key_ref[...].T
        key_sum[...] = jnp.zeros_like(key_sum)
        value_sum[...] = jnp.zeros_like(value_sum)

    taken = []
    for group in groups:
        per_piece = length // len(group) // tile
        item = group[0][...]
        for at in range(1, len(group)):
            item = jnp.where(step >= at * per_piece, group[at][...], item)
        taken.append(item)
    grad, out, aux = taken
    plain = query_ref[...]
    query = jnp.concatenate([plain, aux], axis=1)
    product = grad.astype(jnp.float32) * out
    delta = jnp.zeros((tile, LANES), jnp.float32)
    for one in range(PER_TILE):
        own = jnp.sum(jnp.where(lane // wide == one, product, 0.0), axis=1, keepdims=True)
        delta = spread_three(lane, 4 * one, own, delta)
    grad_aug = jnp.concatenate([grad, delta.astype(jnp.bfloat16)], axis=1)
    nothing = jnp.zeros((), plain.dtype)
    query_rows = []
    for one in range(PER_TILE):
        mine = lane // wide == one
        query_own = jnp.where(mine, plain, nothing)
        grad_own = jnp.where(mine, grad, nothing)
        total = None
        for low in range(0, length, span):
            at = slice(low, low + span)
            score = dot_f32(key_aug[one, at], query, NT)
            grad_probs = dot_f32(value_aug[one, at], grad_aug, NT)
            probs = jnp.exp2(score * SCORE_SCALE)
            grad_scores = (probs * grad_probs).astype(jnp.bfloat16)
            value_sum[at] += dot_f32(probs.astype(jnp.bfloat16), grad_own, NN)
            key_sum[at] += dot_f32(grad_scores, query_own, NN)
            part = dot_f32(key_cols[wide * one : wide * (one + 1), at], grad_scores, NN)
            total = part if total is None else total + part
        query_rows.append(total)
    query_grad_ref[...] = (jnp.concatenate(query_rows, axis=0).T * 0.125).astype(jnp.bfloat16)

    @pl.when(step == pl.num_programs(1) - 1)
    def _():
        key_grad_ref[...] = (key_sum[...] * 0.125).astype(jnp.bfloat16)
        value_grad_ref[...] = value_sum[...].astype(jnp.bfloat16)


def attend_back(qkv, grads, outs, auxes, info, tile, span):
    length, width = qkv.shape[0], qkv.shape[1] // 3
    tiles = width // LANES

    def piece_specs(pieces):
        per_piece = length // len(pieces) // tile
        return [
            pl.BlockSpec(
                (tile, LANES),
                lambda pair, at, low=low: (jnp.clip(at - low, 0, per_piece - 1), pair),
            )
            for low in range(0, per_piece * len(pieces), per_piece)
        ]

    result = jax.ShapeDtypeStruct((length, width), jnp.bfloat16)
    whole = pl.BlockSpec((length, LANES), lambda pair, at: (0, pair))
    query_spec = pl.BlockSpec((tile, LANES), lambda pair, at: (at, pair))
    return pl.pallas_call(
        functools.partial(attend_back_kernel, span, (len(grads), len(outs), len(auxes))),
        grid=(tiles, length // tile),
        in_specs=[
            pl.BlockSpec(memory_space=pltpu.SMEM),
            query_spec,
            pl.BlockSpec((length, LANES), lambda pair, at: (0, tiles + pair)),
            pl.BlockSpec((length, LANES), lambda pair, at: (0, 2 * tiles + pair)),
        ]
        + piece_specs(grads)
        + piece_specs(outs)
        + piece_specs(auxes),
        out_specs=[query_spec, whole, whole],
        out_shape=[result] * 3,
        scratch_shapes=[pltpu.VMEM((PER_TILE, length, 2 * LANES), jnp.bfloat16)] * 2
        + [pltpu.VMEM((LANES, length), jnp.bfloat16)]
        + [pltpu.VMEM((length, LANES), jnp.float32)] * 2,
        compiler_params=pltpu.CompilerParams(vmem_limit_bytes=VMEM_LIMIT),
        cost_estimate=pl.CostEstimate(
            flops=40 * length * length * width,
            bytes_accessed=22 * length * width,
            transcendentals=length * length * width // 64,
        ),
        name="attend_back",
    )(info, qkv, qkv, qkv, *grads, *outs, *auxes)


def pack_kernel(count, core_ref, *refs):
    query, key, value, output, up, down = refs[:6]
    vectors = refs[6 : 6 + count]
    mine_ref, theirs_ref, second_ref, held_ref, wide_ref = refs[6 + count : 11 + count]
    lines = refs[11 + count : 11 + 2 * count]
    sems, line_sems = refs[11 + 2 * count :]
    share, width = query.shape
    cols = width // 2
    fold = up.shape[1] // width
    copies = [
        pltpu.make_async_copy(item, held_ref.at[at], sems.at[at])
        for at, item in enumerate((query, key, value))
    ]
    copies += [
        pltpu.make_async_copy(item, line, line_sems.at[at])
        for at, (item, line) in enumerate(zip(vectors, lines))
    ]
    later = [pltpu.make_async_copy(output, second_ref.at[0], sems.at[3])]
    for at in range(fold):
        later.append(
            pltpu.make_async_copy(
                down.at[pl.ds(at * share, share)],
                second_ref.at[1 + fold + at],
                sems.at[4 + at],
            )
        )
    later.append(pltpu.make_async_copy(up, wide_ref, sems.at[4 + fold]))
    for copy in copies + later:
        copy.start()
    for copy in copies:
        copy.wait()
    first_core = core_ref[0] == 0
    for at in range(3):
        left, right = held_ref[at, :, :cols], held_ref[at, :, cols:]
        here = slice(at * share, (at + 1) * share)
        mine_ref[here] = jnp.where(first_core, left, right)
        theirs_ref[here] = jnp.where(first_core, right, left)
    for ref in (mine_ref, theirs_ref):
        ref[3 * share :] = jnp.zeros((8, cols), ref.dtype)
        for at, line in enumerate(lines):
            low = at // 8 * LANES
            ref[3 * share + at % 8, low : low + line.shape[0]] = line[...]
    for copy in later:
        copy.wait()
    for at in range(fold):
        second_ref[1 + at] = wide_ref[:, at * width : (at + 1) * width]


def pack(core, matrices, vectors):
    share, width = matrices[0].shape
    cols = width // 2
    fold = matrices[4].shape[1] // width
    count = len(vectors)
    block = jax.ShapeDtypeStruct((3 * share + 8, cols), jnp.bfloat16)
    inside = pl.BlockSpec(memory_space=pltpu.VMEM)
    return pl.pallas_call(
        functools.partial(pack_kernel, count),
        in_specs=[pl.BlockSpec(memory_space=pltpu.SMEM)]
        + [pl.BlockSpec(memory_space=pl.ANY)] * (6 + count),
        out_specs=[inside] * 3,
        out_shape=[
            block,
            block,
            jax.ShapeDtypeStruct((1 + 2 * fold, share, width), jnp.bfloat16),
        ],
        scratch_shapes=[pltpu.VMEM((3, share, width), jnp.bfloat16)]
        + [pltpu.VMEM(matrices[4].shape, jnp.bfloat16)]
        + [pltpu.VMEM(item.shape, item.dtype) for item in vectors]
        + [pltpu.SemaphoreType.DMA((5 + fold,)), pltpu.SemaphoreType.DMA((count,))],
        compiler_params=pltpu.CompilerParams(vmem_limit_bytes=VMEM_LIMIT),
        name="pack",
    )(core, *matrices, *vectors)


def by_device(gathered_ref, rows, columns=slice(None)):
    n_pair, n_blk, n_core = gathered_ref.shape[:3]
    return jnp.concatenate(
        [
            gathered_ref[pair, blk, core, rows, columns]
            for pair in range(n_pair)
            for core in range(n_core)
            for blk in range(n_blk)
        ],
        axis=0,
    )


def unspread(gathered_ref, first_row, entry, width, share):
    low, row = entry // 8 * LANES, first_row + entry % 8
    pieces = by_device(gathered_ref, slice(row, row + 1), slice(low, low + LANES))
    lane = lax.broadcasted_iota(jnp.int32, (LANES, width), 1)
    row = lax.broadcasted_iota(jnp.int32, (LANES, width), 0)
    pick = jnp.where(lax.rem(lane, share) == row, 1.0, 0.0).astype(jnp.bfloat16)
    spread = dot_f32(pieces, pick, NN)
    lane = lax.broadcasted_iota(jnp.int32, (pieces.shape[0], width), 1)
    row = lax.broadcasted_iota(jnp.int32, (pieces.shape[0], width), 0)
    return jnp.sum(jnp.where(lax.div(lane, share) == row, spread, 0.0), axis=0, keepdims=True)


def own_weight(gathered_ref, at, share):
    return by_device(gathered_ref, slice(at * share, (at + 1) * share))


def block_rows(core_ref, own_ref, other_ref):
    own, other = own_ref[...], other_ref[...]
    first = core_ref[0] == 0
    return jnp.concatenate([jnp.where(first, own, other), jnp.where(first, other, own)], axis=0)


def block_specs(half, width):
    return [
        pl.BlockSpec((half, width), lambda at, core: (at, 0)),
        pl.BlockSpec((half, width), lambda at, core: (at + 1 - 2 * lax.rem(at, 2), 0)),
    ]


def project_kernel(share, core_ref, own_ref, other_ref, gathered_ref, out_ref, bias_ref):
    cols = gathered_ref.shape[4]

    @pl.when(pl.program_id(0) == 0)
    def _():
        for at in range(2):
            whole = unspread(gathered_ref, 3 * share, at, 2 * cols, share)
            bias_ref[at : at + 1, :] = jnp.where(
                core_ref[0] == 0, whole[:, :cols], whole[:, cols:]
            )

    tokens = block_rows(core_ref, own_ref, other_ref)
    for at, bias in enumerate((0, None, 1)):
        part = dot_f32(tokens, own_weight(gathered_ref, at, share), NN)
        if bias is not None:
            part = part + bias_ref[bias : bias + 1, :]
        out_ref[:, at * cols : (at + 1) * cols] = part.astype(out_ref.dtype)


def project(core, own, other, gathered, half):
    length, width = 2 * own.shape[0], own.shape[1]
    cols, share = width // 2, (gathered.shape[3] - 8) // 3
    return pl.pallas_call(
        functools.partial(project_kernel, share),
        grid_spec=pltpu.PrefetchScalarGridSpec(
            num_scalar_prefetch=1,
            grid=(length // (2 * half),),
            in_specs=block_specs(half, width)
            + [pl.BlockSpec(gathered.shape, lambda at, core: (0,) * 5)],
            out_specs=pl.BlockSpec((2 * half, 3 * cols), lambda at, core: (at, 0)),
            scratch_shapes=[pltpu.VMEM((8, cols), jnp.float32)],
        ),
        out_shape=jax.ShapeDtypeStruct((length, 3 * cols), jnp.bfloat16),
        compiler_params=pltpu.CompilerParams(vmem_limit_bytes=VMEM_LIMIT),
        cost_estimate=pl.CostEstimate(
            flops=6 * length * width * cols, bytes_accessed=10 * length * width, transcendentals=0
        ),
        name="project",
    )(core, own, other, gathered)


def norm(values, gain, shift):
    center = jnp.mean(values, axis=1, keepdims=True)
    offset = values - center
    scale = lax.rsqrt(jnp.mean(offset * offset, axis=1, keepdims=True) + 1e-12)
    unit = offset * scale
    return unit * gain + shift, unit, scale


def norm_back(grad, gain, unit, scale):
    inner = grad * gain
    mean = jnp.mean(inner, axis=1, keepdims=True)
    return scale * (inner - mean - unit * jnp.mean(inner * unit, axis=1, keepdims=True))


def feed_kernel(
    kept, index_ref, even_ref, odd_ref, tokens_ref, cotangent_ref, small_ref, weights_ref, *refs
):
    feed_rows(
        index_ref[1] == 1, even_ref, odd_ref, tokens_ref, cotangent_ref, small_ref, weights_ref, *refs[kept:]
    )


def feed_rows(
    odd, even_ref, odd_ref, tokens_ref, cotangent_ref, small_ref, weights_ref,
    out_ref, active_ref, grad_down_ref, grad_up_ref, hidden_ref, res_ref, attended_ref, context_ref,
    even_grad_ref, odd_grad_ref, sum_ref,
    weight_ref, vector_ref, slope_ref, sems,
):
    devices, _, share, width = weights_ref.shape
    fold = active_ref.shape[1] // width
    group = devices // fold
    step = pl.program_id(0)
    f32, bf16 = jnp.float32, jnp.bfloat16

    def copy(unit):
        if unit <= fold:
            return pltpu.make_async_copy(weights_ref.at[:, unit], weight_ref.at[unit], sems.at[unit])
        first = group * (unit - 1 - fold)
        return pltpu.make_async_copy(
            weights_ref.at[pl.ds(first, group), pl.ds(1 + fold, fold)],
            weight_ref.at[unit].reshape(group, fold, share, width),
            sems.at[unit],
        )

    order = [0]
    for at in range(fold):
        order += [1 + at, 1 + fold + at]
    ahead = 3

    @pl.when(step == 0)
    def _():
        for unit in order[:ahead]:
            copy(unit).start()
        sum_ref[...] = jnp.zeros_like(sum_ref)
        for entry in range(7):
            times = fold if entry == 1 else 1
            vector_ref[entry : entry + 1, : times * width] = unspread(
                small_ref, 0, 2 + entry, times * width, times * share
            )

    def ready(unit):
        @pl.when(step == 0)
        def _():
            copy(unit).wait()
            after = order.index(unit) + ahead
            if after < len(order):
                copy(order[after]).start()

    def weight(unit):
        return weight_ref[unit].reshape(width, width)

    def vector(entry, low=0):
        return vector_ref[entry : entry + 1, low : low + width]

    def add_sum(entry, value):
        sum_ref[entry : entry + 1, :] += jnp.sum(value, axis=0, keepdims=True)

    even, other = even_ref[...], odd_ref[...]
    context = jnp.concatenate([jnp.where(odd, other, even), jnp.where(odd, even, other)], axis=1)
    context_ref[...] = context
    ready(0)
    attended = dot_f32(context, weight(0), NN) + vector(0)
    hidden, unit_one, scale_one = norm(tokens_ref[...].astype(f32) + attended, vector(3), vector(4))
    hidden_low = hidden.astype(bf16)
    hidden_ref[...] = hidden_low
    down = vector(2)
    for at in range(fold):
        low = at * width
        ready(1 + at)
        up = dot_f32(hidden_low, weight(1 + at), NN) + vector(1, low)
        square = up * up
        tanh = jnp.tanh(0.7978845608 * up * (1.0 + 0.044715 * square))
        half = 0.5 * (1.0 + tanh)
        active = (up * half).astype(bf16)
        rise = (0.5 * 0.7978845608) * up * (1.0 - tanh * tanh)
        slope_ref[at] = half + rise * (1.0 + (3 * 0.044715) * square)
        active_ref[:, low : low + width] = active
        ready(1 + fold + at)
        down = down + dot_f32(active, weight(1 + fold + at), NN)
    out, unit_two, scale_two = norm(hidden + down, vector(5), vector(6))
    out_ref[...] = out.astype(bf16)
    cotangent = cotangent_ref[...].astype(f32)
    add_sum(4, cotangent * unit_two)
    add_sum(5, cotangent)
    grad = norm_back(cotangent, vector(5), unit_two, scale_two)
    grad_down = grad.astype(bf16)
    grad_down_ref[...] = grad_down
    add_sum(1, grad_down.astype(f32))
    for at in range(fold):
        low = at * width
        grad_active = dot_f32(grad_down, weight(1 + fold + at), NT)
        grad_up = (grad_active * slope_ref[at]).astype(bf16)
        grad_up_ref[:, low : low + width] = grad_up
        add_sum(6 + at, grad_up.astype(f32))
        grad = grad + dot_f32(grad_up, weight(1 + at), NT)
    add_sum(2, grad * unit_one)
    add_sum(3, grad)
    res_one = norm_back(grad, vector(3), unit_one, scale_one)
    res_ref[...] = res_one
    grad_attended = res_one.astype(bf16)
    attended_ref[...] = grad_attended
    add_sum(0, grad_attended.astype(f32))
    context_grad = dot_f32(grad_attended, weight(0), NT).astype(bf16)
    left, right = context_grad[:, : width // 2], context_grad[:, width // 2 :]
    even_grad_ref[...] = jnp.where(odd, right, left)
    odd_grad_ref[...] = jnp.where(odd, left, right)


def feed(index, even, other, tokens, cotangent, gathered, second, kept, tile):
    rows, width = even.shape[0], 2 * even.shape[1]
    seqs = tokens.shape[0]
    devices, units, share, _ = second.shape
    fold = (units - 1) // 2
    thin = pl.BlockSpec((tile, width), lambda at, index: (at, 0))
    placed = pl.BlockSpec((None, tile, width), lambda at, index: (index[0], at, 0))
    side = pl.BlockSpec((tile, width // 2), lambda at, index: (at, 0))
    wide = pl.BlockSpec((tile, fold * width), lambda at, index: (at, 0))
    sums = (6 + fold + 7) // 8 * 8

    def like(columns, dtype):
        return jax.ShapeDtypeStruct((rows, columns), dtype)

    bf16, f32 = jnp.bfloat16, jnp.float32
    return pl.pallas_call(
        functools.partial(feed_kernel, len(kept)),
        grid_spec=pltpu.PrefetchScalarGridSpec(
            num_scalar_prefetch=1,
            grid=(rows // tile,),
            in_specs=[
                side,
                side,
                placed,
                placed,
                pl.BlockSpec(
                    gathered.shape[:3] + (8, width // 2),
                    lambda at, index: (0, 0, 0, 3 * share // 8, 0),
                ),
                pl.BlockSpec(memory_space=pl.ANY),
            ]
            + [pl.BlockSpec(memory_space=pl.ANY)] * len(kept),
            out_specs=[placed, wide, thin, wide, thin, thin, thin, thin, side, side]
            + [pl.BlockSpec((sums, width), lambda at, index: (0, 0))],
            scratch_shapes=[
                pltpu.VMEM((units, devices, share, width), bf16),
                pltpu.VMEM((8, fold * width), f32),
                pltpu.VMEM((fold, tile, width), f32),
                pltpu.SemaphoreType.DMA((units,)),
            ],
        ),
        out_shape=[
            jax.ShapeDtypeStruct((seqs, rows, width), bf16),
            like(fold * width, bf16),
            like(width, bf16),
            like(fold * width, bf16),
            like(width, bf16),
            like(width, f32),
            like(width, bf16),
            like(width, bf16),
            like(width // 2, bf16),
            like(width // 2, bf16),
            jax.ShapeDtypeStruct((sums, width), f32),
        ],
        input_output_aliases={7: 0} if kept else {},
        compiler_params=pltpu.CompilerParams(vmem_limit_bytes=VMEM_LIMIT),
        cost_estimate=pl.CostEstimate(
            flops=4 * rows * width * width * (1 + 2 * fold),
            bytes_accessed=rows * width * (20 + 4 * fold) + 2 * units * width * width,
            transcendentals=rows * width * fold,
        ),
        name="feed",
    )(index, even, other, tokens, cotangent, gathered, second, *kept)


TN = ((0,), (0,))


def weight_grad_kernel(parts, *refs):
    groups = [refs[at * parts : (at + 1) * parts] for at in range(6)]
    active, grad_down, hidden, grad_up, context, attended = groups
    out_ref, block_ref, sems = refs[6 * parts :]
    devices, units, share, width = out_ref.shape
    fold = (units - 1) // 2
    group = devices // fold
    step = pl.program_id(0)
    slot = lax.rem(step, 2)

    def column_copy(unit, slot):
        return pltpu.make_async_copy(block_ref.at[slot], out_ref.at[:, unit], sems.at[slot])

    def row_copy(at, slot):
        return pltpu.make_async_copy(
            block_ref.at[slot].reshape(group, fold, share, width),
            out_ref.at[pl.ds(group * at, group), pl.ds(1 + fold, fold)],
            sems.at[slot],
        )

    def store(left, right, slot):
        total = None
        for one, other in zip(left, right):
            part = dot_f32(one[...], other[...], TN)
            total = part if total is None else total + part
        block_ref[slot] = total.astype(block_ref.dtype).reshape(devices, share, width)

    @pl.when(step >= 2)
    def _():
        column_copy(0, slot).wait()

    @pl.when(step == 0)
    def _():
        store(context, attended, 0)
        column_copy(0, 0).start()

    @pl.when((step >= 1) & (step <= fold))
    def _():
        store(hidden, grad_up, slot)
        column_copy(step, slot).start()

    @pl.when(step > fold)
    def _():
        store(active, grad_down, slot)
        row_copy(step - 1 - fold, slot).start()

    @pl.when(step == 2 * fold)
    def _():
        column_copy(0, 0).wait()
        column_copy(0, 1).wait()


def weight_grads(parts, devices):
    rows, width = parts[0][4].shape
    fold = parts[0][0].shape[1] // width
    share, units = width // devices, 1 + 2 * fold
    whole = pl.BlockSpec((rows, width), lambda at: (0, 0))
    active = pl.BlockSpec((rows, width), lambda at: (0, jnp.maximum(at - 1 - fold, 0)))
    up = pl.BlockSpec((rows, width), lambda at: (0, jnp.clip(at - 1, 0, fold - 1)))
    specs = [active, whole, whole, up, whole, whole]
    return pl.pallas_call(
        functools.partial(weight_grad_kernel, len(parts)),
        grid=(1 + 2 * fold,),
        in_specs=[spec for spec in specs for _ in parts],
        out_specs=pl.BlockSpec(memory_space=pl.ANY),
        scratch_shapes=[
            pltpu.VMEM((2, devices, share, width), jnp.bfloat16),
            pltpu.SemaphoreType.DMA((2,)),
        ],
        out_shape=jax.ShapeDtypeStruct((devices, units, share, width), jnp.bfloat16),
        compiler_params=pltpu.CompilerParams(vmem_limit_bytes=VMEM_LIMIT),
        cost_estimate=pl.CostEstimate(
            flops=2 * len(parts) * rows * width * width * (1 + 2 * fold),
            bytes_accessed=2 * (len(parts) * rows + width) * width * units,
            transcendentals=0,
        ),
        name="weight_grads",
    )(*[part[at] for at in range(6) for part in parts])


def own_grads_kernel(
    count, core_ref, query_ref, key_ref, value_ref, own_ref, other_ref, *refs
):
    out_ref, sum_ref, bias_ref = refs[-3:]
    devices, high, wide = out_ref.shape
    cols, share = wide // 3, high - 8
    step = pl.program_id(0)

    @pl.when(step == 0)
    def _():
        sum_ref[...] = jnp.zeros_like(sum_ref)
        bias_ref[...] = jnp.zeros_like(bias_ref)

    tokens = block_rows(core_ref, own_ref, other_ref)
    for at, grad_ref in enumerate((query_ref, key_ref, value_ref)):
        grad = grad_ref[...]
        here = slice(at * cols, (at + 1) * cols)
        sum_ref[:, here] += dot_f32(tokens, grad, TN)
        bias_ref[0:1, here] += jnp.sum(grad.astype(jnp.float32), axis=0, keepdims=True)

    @pl.when(step == pl.num_programs(0) - 1)
    def _():
        out_ref[:, :share, :] = sum_ref[...].astype(out_ref.dtype).reshape(devices, share, wide)
        total = refs[0][...]
        for ref in refs[1:-3]:
            total = total + ref[...]
        zero = jnp.zeros((1, cols), jnp.float32)
        bits = [total[at : at + 1, low : low + cols] for at in range(count) for low in (0, cols)]
        bits += [zero] * (21 - len(bits))
        lines = [jnp.concatenate(bits[at : at + 3], axis=1) for at in range(0, 21, 3)]
        lines = jnp.concatenate([bias_ref[0:1, :]] + lines, axis=0).astype(out_ref.dtype)
        out_ref[:, share:, :] = jnp.broadcast_to(lines[None], (devices, 8, wide))


def own_grads(core, grads, own, other, sums, count, devices, half):
    length, width = 2 * own.shape[0], own.shape[1]
    share, wide = width // devices, 3 * (width // 2)
    grad_spec = pl.BlockSpec((2 * half, wide // 3), lambda at, core: (at, 0))
    return pl.pallas_call(
        functools.partial(own_grads_kernel, count),
        grid_spec=pltpu.PrefetchScalarGridSpec(
            num_scalar_prefetch=1,
            grid=(length // (2 * half),),
            in_specs=[grad_spec] * 3
            + block_specs(half, width)
            + [pl.BlockSpec(item.shape, lambda at, core: (0, 0)) for item in sums],
            out_specs=pl.BlockSpec((devices, share + 8, wide), lambda at, core: (0, 0, 0)),
            scratch_shapes=[
                pltpu.VMEM((width, wide), jnp.float32),
                pltpu.VMEM((8, wide), jnp.float32),
            ],
        ),
        out_shape=jax.ShapeDtypeStruct((devices, share + 8, wide), jnp.bfloat16),
        compiler_params=pltpu.CompilerParams(vmem_limit_bytes=VMEM_LIMIT),
        cost_estimate=pl.CostEstimate(
            flops=2 * length * width * wide, bytes_accessed=6 * length * width, transcendentals=0
        ),
        name="own_grads",
    )(core, *grads, own, other, *sums)


def tokens_grad_kernel(
    share, core_ref, query_ref, key_ref, value_ref, gathered_ref, own_ref, other_ref
):
    total = None
    for at, grad_ref in enumerate((query_ref, key_ref, value_ref)):
        part = dot_f32(grad_ref[...], own_weight(gathered_ref, at, share), NT)
        total = part if total is None else total + part
    half = own_ref.shape[0]
    total = total.astype(own_ref.dtype)
    first = core_ref[0] == 0
    own_ref[...] = jnp.where(first, total[:half], total[half:])
    other_ref[...] = jnp.where(first, total[half:], total[:half])


def tokens_grads(core, grads, gathered, half):
    length, width = grads[0].shape[0], 2 * gathered.shape[4]
    cols, share = width // 2, (gathered.shape[3] - 8) // 3
    rows = jax.ShapeDtypeStruct((length // 2, width), jnp.bfloat16)
    return pl.pallas_call(
        functools.partial(tokens_grad_kernel, share),
        grid_spec=pltpu.PrefetchScalarGridSpec(
            num_scalar_prefetch=1,
            grid=(length // (2 * half),),
            in_specs=[pl.BlockSpec((2 * half, cols), lambda at, core: (at, 0))] * 3
            + [pl.BlockSpec(gathered.shape, lambda at, core: (0,) * 5)],
            out_specs=block_specs(half, width),
        ),
        out_shape=[rows, rows],
        compiler_params=pltpu.CompilerParams(vmem_limit_bytes=VMEM_LIMIT),
        cost_estimate=pl.CostEstimate(
            flops=6 * length * width * cols, bytes_accessed=6 * length * width, transcendentals=0
        ),
        name="tokens_grads",
    )(core, *grads, gathered)


def body(
    tokens,
    cotangent,
    lengths,
    query_weight,
    key_weight,
    value_weight,
    output_weight,
    up_weight,
    down_weight,
    query_bias,
    value_bias,
    output_bias,
    up_bias,
    down_bias,
    attn_gain,
    attn_shift,
    ffn_gain,
    ffn_shift,
):
    seqs, stretch, width = tokens.shape
    rows = seqs * stretch
    n_pair, n_core, n_blk = (lax.axis_size(axis) for axis in ALL)
    devices = n_pair * n_core * n_blk
    pair, core, blk = (lax.axis_index(axis) for axis in ALL)
    half, cols = stretch // 2, width // 2
    own_rows = n_blk * half
    share = query_weight.shape[0]
    fold = up_weight.shape[1] // width
    bf16, f32 = jnp.bfloat16, jnp.float32

    def table(step, back):
        moves = []
        for pair in range(n_pair):
            for src_core in range(n_core):
                for src in range(n_blk):
                    piece = src ^ step
                    sender = (pair * n_core + src_core) * n_blk + src
                    target = (pair * n_core + piece % 2) * n_blk + seqs * src_core + piece // 2
                    moves.append((target, sender) if back else (sender, target))
        return moves

    def move(array, step, back=False):
        return lax.ppermute(array, ALL, table(step, back))

    def after(array, *others):
        return lax.optimization_barrier((array, others))[0]

    def other_core(array):
        return lax.ppermute(array, "core", [(0, 1), (1, 0)])

    def columns(array, which):
        return lax.dynamic_slice_in_dim(array, which * cols, cols, axis=-1)

    def swap(flip, one, two):
        return jnp.where(flip, two, one), jnp.where(flip, one, two)

    def ordered(me, items):
        bit = 1
        while bit < len(items):
            flip = (me & bit) != 0
            items = [jnp.where(flip, items[at ^ bit], items[at]) for at in range(len(items))]
            bit *= 2
        return items

    def others(array, axis, size):
        return [
            lax.ppermute(array, axis, [(at, at ^ step) for at in range(size)])
            for step in range(1, size)
        ]

    which = jnp.reshape(core, (1,)).astype(jnp.int32)
    mine, theirs, second = pack(
        which,
        (query_weight, key_weight, value_weight, output_weight, up_weight, down_weight),
        (query_bias, value_bias, output_bias, up_bias, down_bias)
        + (attn_gain, attn_shift, ffn_gain, ffn_shift),
    )
    gathered = jnp.stack(swap(core == 1, mine, other_core(theirs)))
    gathered = jnp.stack(ordered(blk, [gathered] + others(gathered, "blk", n_blk)))
    tokens_moved = after(tokens, gathered)
    seconds = lax.all_gather(second, "blk", axis=0)
    pieces = tokens_moved.reshape(n_blk, half, width)
    arrived = [
        move(lax.dynamic_index_in_dim(pieces, blk ^ step, 0, keepdims=False), step)
        for step in range(n_blk)
    ]
    terms, arrived[:2] = lax.optimization_barrier(
        ([gathered] + others(gathered, "pair", n_pair), arrived[:2])
    )
    gathered = jnp.stack(ordered(pair, terms))
    second = lax.all_gather(after(seconds, gathered), ("pair", "core"), axis=0)
    second = second.reshape((devices,) + second.shape[2:])
    both = jnp.concatenate(swap(core == 1, lengths, other_core(lengths)))
    own_length = lax.dynamic_index_in_dim(both, blk, 0, keepdims=False)

    parts = n_blk // 2
    piece = 2 * (blk % seqs) + core
    info = jnp.stack(
        [own_length] + [(piece ^ (at // 2)) * stretch + at % 2 * half for at in range(2 * n_blk)]
    ).astype(jnp.int32)
    own_tokens = after(jnp.concatenate(arrived, axis=0), gathered, info)
    other_tokens = other_core(own_tokens)
    odd = blk % 2 == 1

    def after_all(items, *others):
        return lax.optimization_barrier((items, others))[0]

    qkv = project(which, own_tokens, other_tokens, gathered, half)
    attended, returning = [], []
    for part in range(parts):
        query_side = after(qkv, attended[-1]) if part else qkv
        attended.append(attend(query_side, info, part, parts, 512))
        returning.append([move(attended[-1][at], 2 * part + at, True) for at in range(2)])

    fed, context_grads, kept = [], [], ()
    for part in range(parts):
        even, other = after_all(returning[part], fed[-1] if part else attended[-1])
        index = jnp.stack([(blk // 2) ^ part, blk % 2]).astype(jnp.int32)
        fed.append(feed(index, even, other, tokens, cotangent, gathered, second, kept, 256))
        kept = (fed[-1][0],)
        context_grads.append([move(fed[-1][8 + at], 2 * part + at) for at in range(2)])
    layer_out = kept[0]

    early, late = context_grads[0], context_grads[1]
    early, first_active = lax.optimization_barrier((early, fed[0][1]))
    second_grads = weight_grads(
        [
            (item[1] if part else first_active, item[2], item[4], item[3], item[7], item[6])
            for part, item in enumerate(fed)
        ],
        devices,
    )
    late, second_grads = lax.optimization_barrier((late, second_grads))
    total = second_grads
    second_grads = lax.psum_scatter(
        second_grads.reshape((n_pair * n_core, n_blk) + second_grads.shape[1:]),
        ("pair", "core"),
        scatter_dimension=0,
    )
    early[0] = after(early[0], total)
    outs, auxes = [item[2] for item in attended], [item[3] for item in attended]
    grads = attend_back(qkv, list(early) + list(late), outs, auxes, info, 512, 1024)

    own, far = tokens_grads(which, grads, gathered, half)
    second_grads, own, far = lax.optimization_barrier((second_grads, own, far))
    second_grads = lax.psum_scatter(second_grads, "blk", scatter_dimension=0)
    summed = (own.astype(f32) + other_core(far).astype(f32)).astype(bf16)
    moved = [move(summed[step * half : (step + 1) * half], step, True) for step in range(n_blk)]
    first_grads = own_grads(
        which,
        [after(item, summed) for item in grads],
        own_tokens,
        other_tokens,
        [item[10] for item in fed],
        6 + fold,
        devices,
        half,
    )

    def to_sum(array, axis, me, size):
        terms = [lax.dynamic_index_in_dim(array, me, 0, keepdims=False)]
        for step in range(1, size):
            sent = lax.dynamic_index_in_dim(array, me ^ step, 0, keepdims=False)
            terms.append(lax.ppermute(sent, axis, [(at, at ^ step) for at in range(size)]))
        return terms

    def add(terms):
        total = terms[0].astype(f32)
        for term in terms[1:]:
            total += term.astype(f32)
        return total.astype(bf16)

    first_grads = first_grads.reshape(n_pair, n_core, n_blk, share + 8, 3 * cols)
    total = add(to_sum(first_grads, "pair", pair, n_pair))
    moved, total, second_grads = lax.optimization_barrier((moved, total, second_grads))
    terms = to_sum(jnp.moveaxis(total, 1, 0), "blk", blk, n_blk)
    returned = []
    for part in range(parts):
        back = jnp.concatenate(swap(odd, *moved[2 * part : 2 * part + 2]), axis=0)
        returned.append(fed[part][5] + back.astype(f32))
    tokens_grad = jnp.stack(swap(blk >= 2, *returned))

    device = (pair * n_core + core) * n_blk + blk

    def own_part(line, size):
        return lax.dynamic_slice_in_dim(line, device * size, size, axis=-1)

    second_grads = second_grads.astype(f32)
    late = (
        second_grads[0],
        jnp.concatenate([second_grads[1 + at] for at in range(fold)], axis=1),
        second_grads[1 + fold :].reshape(fold * share, width),
    )
    terms, tokens_grad, late = lax.optimization_barrier((terms, tokens_grad, late))
    total = add(terms)
    kept = lax.dynamic_index_in_dim(total, core, 0, keepdims=False)
    crossed = other_core(lax.dynamic_index_in_dim(total, 1 - core, 0, keepdims=False))
    left, right = (item.astype(f32) for item in swap(core == 1, kept, crossed))
    projections = [
        jnp.concatenate([left[:, at : at + cols], right[:, at : at + cols]], axis=1)
        for at in range(0, 3 * cols, cols)
    ]
    lines = (kept[share + 1 :].astype(f32) + crossed[share + 1 :].astype(f32)).reshape(-1)
    biases = [projections[at][share : share + 1] for at in (0, 2)]
    own_lines = own_part(
        jnp.concatenate(biases + [lines[: 6 * width].reshape(6, width)], axis=0), share
    )
    up_line = own_part(lines[6 * width : (6 + fold) * width], fold * share)
    return (
        (layer_out, tokens_grad)
        + tuple(item[:share] for item in projections)
        + late
        + (own_lines[0], own_lines[1], own_lines[2], up_line)
        + tuple(own_lines[at] for at in range(3, 8))
    )


def fits(mesh, tokens, up_weight):
    n_dp, n_blk = mesh.shape["dp"], mesh.shape["blk"]
    batch, length, width = tokens.shape
    if n_dp % 2 or n_dp & (n_dp - 1) or batch % n_dp or 2 * (batch // n_dp) != n_blk or n_blk != 4:
        return False
    share = width // (n_dp * n_blk)
    fold = up_weight.shape[1] // width
    return (
        width == HEADS * 64
        and width % (4 * LANES // PER_TILE) == 0
        and up_weight.shape[1] == fold * width
        and share * n_dp * n_blk == width
        and share % 8 == 0
        and 16 <= share
        and (8 + fold) * share <= width // 2
        and fold == 4
        and length % (16 * n_blk) == 0
        and length % 512 == 0
        and length <= 4096
    )


def solution(mesh):
    n_dp, n_blk = mesh.shape["dp"], mesh.shape["blk"]

    def step(*args):
        spread = ("dp", "blk")
        one, use = ring_body, mesh
        where = {"dp": "dp", "blk": "blk", spread: spread}
        if fits(mesh, args[0], args[7]):
            one, use = body, Mesh(mesh.devices.reshape(n_dp // 2, 2, n_blk), ALL)
            where = {"dp": ("pair", "core"), "blk": "blk", spread: ALL}
        block = P(where["dp"], where["blk"], None)
        matrix = P(where[spread], None)
        vector = P(where[spread])
        return jax.shard_map(
            one,
            mesh=use,
            in_specs=(block, block, P(where["dp"])) + (matrix,) * 6 + (vector,) * 9,
            out_specs=(block, block) + (matrix,) * 6 + (vector,) * 9,
            check_vma=False,
        )(*args)

    return step
```
